32 devices in a mesh: shot: 2 (over y), gx: 4 (over z), section: 2 (over x), gy: 2 (over core).
Axes of the slice: x: 2, y: 2, z: 4, core: 2. Of those that a mesh axis runs over, the one named last changes fastest.
Arguments:
- wave_now: float32 [256, 32, 512], P(('shot', 'gx'), 'section', 'gy'), parts along dimension 0, may hold values from -6 to 6
- wave_before: float32 [256, 32, 512], P(('shot', 'gx'), 'section', 'gy'), parts along dimension 0, may hold values from -6 to 6
- courant: float32 [256, 32, 512], P(('shot', 'gx'), 'section', 'gy'), parts along dimension 0, may hold values from 0.03 to 0.12
- anisotropy: float32 [256, 32, 512], P(('shot', 'gx'), 'section', 'gy'), parts along dimension 0, may hold values from 0 to 0.3
- tilt: float32 [256, 32, 512], P(('shot', 'gx'), 'section', 'gy'), parts along dimension 0, may hold values from -3.140625 to 3.140625
- reflectivity: bfloat16 [17, 256, 32, 512], P(None, ('shot', 'gx'), 'section', 'gy'), parts along dimension 1, may hold values from -2.5 to 2.5
- offsets: int32 [17], replicated, may hold values from -16 to 16, as said below
Outputs:
- background: float32 [256, 32, 512], P(('shot', 'gx'), 'section', 'gy'), parts along dimension 0
- scattered: float32 [256, 32, 512], P(('shot', 'gx'), 'section', 'gy'), parts along dimension 0
The draws below stay inside these ranges and needn't reach their ends.
There are 2 independent parts, one for each index of `shot`. The reference program is written for one: setup_inputs(seed, part) draws one part's arguments, and reference() takes and returns one part's arrays. A program takes and returns all parts, laid end to end along the dimension named above; an argument that names none is the same for every part. Nothing has to cross between parts.
Inputs may be any that keep to these rules, and one draw needn't show every extreme that they name: 17 distinct offsets, among them 0, -16 and 16.
All inputs are finite; a program needn't handle non-finite values.
Results may differ from the reference program's by a relative error of at most 0.0003.
Values sent between devices are 32-bit elements; how exact they have to be, the bound alone decides.
No kernel may reach another device: no remote copies, remote signals or barrier semaphores. Data moves between devices by JAX's collectives and lax.ppermute only.
A program may use at most 64 MiB of HBM per device.

```python
import math
import jax
import jax.numpy as jnp
from jax import lax

NOFF = 17
MARGIN = 16
ROUNDS = 3
STEPS = 2
NX = 128
NZ = 32
NY = 512


def draw_offsets(key, part):
    inside_values = jnp.concatenate([jnp.arange(1 - MARGIN, 0), jnp.arange(1, MARGIN)]).astype(jnp.int32)
    key_pick, key_order = jax.random.split(jax.random.fold_in(key, 11))
    chosen = jax.random.permutation(key_pick, inside_values)[:NOFF - 3]
    end_values = jnp.array([-MARGIN, 0, MARGIN], jnp.int32)
    return jax.random.permutation(key_order, jnp.concatenate([end_values, chosen])).astype(jnp.int32)


def block_levels(own_key, extent, cuts, least, top_value):
    factor_of, own = 1.0, jax.random.fold_in(own_key, 6)
    for position, parts in cuts:
        draws = jnp.exp(jax.random.uniform(jax.random.fold_in(own, position), (parts,), jnp.float32, least / len(cuts), top_value / len(cuts)))
        factor_of = factor_of * jnp.repeat(draws, extent[position] // parts).reshape([-1 if axis == position else 1 for axis in range(len(extent))])
    return factor_of


def noise(own_key, shape, deviation, limit, shards=(), dtype=jnp.bfloat16):
    level = block_levels(own_key, shape, shards, -0.22, 0.18) if shards else 1.0
    values = jax.random.normal(own_key, shape, jnp.float32) * deviation * level
    return jnp.minimum(jnp.maximum(values, -limit), limit).astype(dtype)


def setup_inputs(seed: int = 0, part: int = 0) -> dict:
    streams_of = jax.random.split(jax.random.key(seed), 8)
    part_keys = jax.random.split(jax.random.fold_in(streams_of[7], part), 8)
    wave_now = noise(part_keys[0], (NX, NZ, NY), 1.0, 6.0, ((0, 4), (1, 2), (2, 2)), jnp.float32)
    wave_before = noise(part_keys[1], (NX, NZ, NY), 1.0, 6.0, ((0, 4), (1, 2), (2, 2)), jnp.float32)
    courant = jnp.clip(jnp.exp(math.log(0.12) - 1.3862944 * jax.random.uniform(part_keys[2], (NX, NZ, NY), jnp.float32) ** block_levels(part_keys[2], (NX, NZ, NY), ((0, 4), (1, 2), (2, 2)), -0.2, 0.2)), 0.03, 0.12)
    anisotropy = jnp.clip(0.3 * jax.random.uniform(part_keys[3], (NX, NZ, NY), jnp.float32) ** block_levels(part_keys[3], (NX, NZ, NY), ((0, 4), (1, 2), (2, 2)), -0.2, 0.2), 0.0, 0.3)
    tilt = jnp.clip(jax.random.uniform(part_keys[4], (NX, NZ, NY), jnp.float32, -3.140625, 3.140625), -3.140625, 3.140625)
    reflectivity = noise(part_keys[5], (NOFF, NX, NZ, NY), 0.25, 2.5, ((1, 4), (2, 2), (3, 2)))
    offsets = draw_offsets(jax.random.fold_in(streams_of[7], 71), part)
    return {"wave_now": wave_now, "wave_before": wave_before, "courant": courant, "anisotropy": anisotropy, "tilt": tilt, "reflectivity": reflectivity, "offsets": offsets}


def coefficients(courant, anisotropy, tilt):
    sine_tilt = jnp.sin(tilt)
    cosine_tilt = jnp.cos(tilt)
    stretch = 1.0 + 2.0 * anisotropy
    coef_xx = courant * (stretch * cosine_tilt * cosine_tilt + sine_tilt * sine_tilt)
    coef_zz = courant * (stretch * sine_tilt * sine_tilt + cosine_tilt * cosine_tilt)
    coef_yy = courant * stretch
    coef_xz = courant * 4.0 * anisotropy * sine_tilt * cosine_tilt
    return coef_xx, coef_zz, coef_yy, coef_xz


def apply_operator(padded, coef_set):
    centre = padded[1:-1, 1:-1, 1:-1]
    diff_xx = padded[2:, 1:-1, 1:-1] + padded[:-2, 1:-1, 1:-1] - 2.0 * centre
    diff_zz = padded[1:-1, 2:, 1:-1] + padded[1:-1, :-2, 1:-1] - 2.0 * centre
    diff_yy = padded[1:-1, 1:-1, 2:] + padded[1:-1, 1:-1, :-2] - 2.0 * centre
    diff_xz = 0.25 * (padded[2:, 2:, 1:-1] - padded[2:, :-2, 1:-1] - padded[:-2, 2:, 1:-1] + padded[:-2, :-2, 1:-1])
    return coef_set[0] * diff_xx + coef_set[1] * diff_zz + coef_set[2] * diff_yy + coef_set[3] * diff_xz


def reference(wave_now, wave_before, courant, anisotropy, tilt, reflectivity, offsets):
    coef_set = coefficients(courant, anisotropy, tilt)
    current = wave_now
    prior = wave_before
    wave_scat = jnp.zeros_like(wave_now)
    scat_prior = jnp.zeros_like(wave_now)
    for round_index in range(ROUNDS):
        for step_index in range(STEPS):
            advanced = 2.0 * current - prior + apply_operator(jnp.pad(current, 1), coef_set)
            prior = current
            current = advanced
        extended = jnp.pad(current, ((MARGIN, MARGIN), (0, 0), (0, 0)))

        def accumulate(offset_index, running):
            start = (MARGIN + offsets[offset_index]).astype(jnp.int32)
            moved = lax.dynamic_slice_in_dim(extended, start, current.shape[0], 0)
            return running + reflectivity[offset_index].astype(jnp.float32) * moved

        source = lax.fori_loop(0, NOFF, accumulate, jnp.zeros_like(current))
        forcing = courant * source
        for step_index in range(STEPS):
            advanced = 2.0 * wave_scat - scat_prior + apply_operator(jnp.pad(wave_scat, 1), coef_set) + forcing
            scat_prior = wave_scat
            wave_scat = advanced
    return current, wave_scat
```

```python
import functools

import jax
import jax.numpy as jnp
from jax import lax
from jax.experimental import pallas as pl
from jax.experimental.pallas import tpu as pltpu
from jax.sharding import PartitionSpec as P

NOFF = 17
MARGIN = 16
TILE = 8
F32 = jnp.float32


class Geometry:
    def __init__(self, rows, depth, half, sections):
        self.B, self.Z, self.H, self.Y = rows // 2, depth, half, 2 * half
        self.two = sections == 2
        self.sides = 1 if self.two else 2
        self.ZE = depth + TILE * self.sides
        assert self.B >= MARGIN and depth % TILE == 0 and half % 128 == 0


def near_side(side, geo):
    first = (geo.B - 2) + side * (geo.B + 2)
    return first, first + 1 - side


def tile_mask(sender, depth, turn, width):
    place = lax.broadcasted_iota(jnp.int32, (TILE, width), 0)
    place = lax.rem(place + (TILE - turn), TILE)
    start = (1 - sender) * (TILE - depth)
    return (place >= start) & (place < start + depth)


def turned(value, turn):
    turn = turn % TILE
    return value if turn == 0 else pltpu.roll(value, turn, 0)


def senders(s, geo):
    return [s] if geo.two else [0, 1]


def receivers(s, geo):
    return [(geo.Z, 1 - s)] if geo.two else [(geo.ZE - TILE, 0), (geo.Z, 1)]


def edge_tile(ref, row, sender, geo):
    start = pl.multiple_of((1 - sender) * (geo.Z - TILE), TILE)
    return ref[row, pl.ds(start, TILE), :]


def packed(items, row, sender, geo):
    out = jnp.zeros((TILE, geo.Y), F32)
    for ref, depth, turn in items:
        out = jnp.where(
            tile_mask(sender, depth, turn, geo.Y), turned(edge_tile(ref, row, sender, geo), turn), out
        )
    return out


def unpacked(tile, depth, turn, sender, geo):
    return jnp.where(tile_mask(sender, depth, 0, geo.Y), turned(tile, TILE - turn), 0.0)


def pack_tiles(items, g, s, tiles, corners, geo):
    for sender, tile_ref, corner_ref in zip(senders(s, geo), tiles, corners):

        def one(row, carry):
            tile_ref[row] = packed(items, row, sender, geo)
            return carry

        lax.fori_loop(0, geo.B, one, 0)
        for k in range(2):
            corner_ref[k] = tile_ref[g * (geo.B - 2) + k]


def put_tiles(dst, place, tiles, index, depth, turn, s, geo):
    for (offset, sender), ref in zip(receivers(s, geo), tiles):
        dst[place, offset : offset + TILE, :] = unpacked(ref[index], depth, turn, sender, geo)


def fill(dst, own, xrow, crow, tiles, xtiles, ctiles, depth, turn, g, s, geo):
    def one(row, carry):
        dst[geo.B + row, 0 : geo.Z, :] = own[row]
        put_tiles(dst, geo.B + row, tiles, row, depth, turn, s, geo)
        return carry

    lax.fori_loop(0, geo.B, one, 0)
    for side, get, edge in ((g, xrow, xtiles), (1 - g, crow, ctiles)):
        first, nearest = near_side(side, geo)
        for k in range(depth):
            place = first + k if depth == 2 else nearest
            index = k if depth == 2 else 1 - side
            if get is not None:
                dst[place, 0 : geo.Z, :] = get(k)
            put_tiles(dst, place, edge, index, depth, turn, s, geo)


def fill_blocks(dst, xblock, cblock, g, geo):
    def one(row, carry):
        dst[g * 2 * geo.B + row, 0 : geo.Z, :] = xblock[row]
        dst[(1 - g) * 2 * geo.B + row, 0 : geo.Z, :] = cblock[row]
        return carry

    lax.fori_loop(0, geo.B, one, 0)


def advance(src, first, count, prior, extra, store, coefs, dif, tot, geo):
    xx, zz, yy, xz = coefs

    def rolls(row, carry):
        value = src[row]
        above = pltpu.roll(value, geo.ZE - 1, 0)
        below = pltpu.roll(value, 1, 0)
        dif[row] = above - below
        tot[row] = above + below
        return carry

    lax.fori_loop(first - 1, first + count + 1, rolls, 0)
    lane = lax.broadcasted_iota(jnp.int32, (geo.ZE, geo.Y), 1)

    def one(row, carry):
        at = row - (geo.B - 1)
        value = src[row]
        right = jnp.where(lane == geo.Y - 1, 0.0, pltpu.roll(value, geo.Y - 1, 1))
        left = jnp.where(lane == 0, 0.0, pltpu.roll(value, 1, 1))
        cx, cz, cy = xx[at], zz[at], yy[at]
        out = (2.0 - 2.0 * (cx + cz + cy)) * value - prior(row)
        out = out + cx * (src[row + 1] + src[row - 1]) + cz * tot[row] + cy * (right + left)
        out = out + xz[at] * (dif[row + 1] - dif[row - 1])
        if extra is not None:
            out = out + extra(row)
        store(row, out)
        return carry

    lax.fori_loop(first, first + count, one, 0)


def make_source(ext, refl, refl_far, offsets, courant, out, g, geo):
    near = pl.multiple_of(g * geo.H, 128)
    far = pl.multiple_of((1 - g) * geo.H, 128)

    def one(row, carry):
        acc = jnp.zeros((geo.Z, geo.H), F32)
        acc_far = jnp.zeros((geo.Z, geo.H), F32)
        for h in range(NOFF):
            place = geo.B + row + offsets[h]
            acc = acc + refl[h, g * geo.B + row].astype(F32) * ext[place, 0 : geo.Z, pl.ds(near, geo.H)]
            acc_far = acc_far + refl_far[h, row] * ext[place, 0 : geo.Z, pl.ds(far, geo.H)]
        out[row, :, pl.ds(near, geo.H)] = courant[row, :, pl.ds(near, geo.H)] * acc
        out[row, :, pl.ds(far, geo.H)] = courant[row, :, pl.ds(far, geo.H)] * acc_far
        return carry

    lax.fori_loop(0, geo.B, one, 0)


def edge_rows(ref, depth, side, geo):
    return side * (geo.B - depth)


def trig_products(angle):
    turns = jnp.floor(angle * 0.6366197723675814 + 0.5)
    rest = angle - turns * 1.5703125
    rest = rest - turns * 4.837512969970703125e-4
    rest = rest - turns * 7.549789954891882e-8
    odd = (turns - 2.0 * jnp.floor(turns * 0.5)) > 0.5
    square = rest * rest
    sine = rest + rest * square * (
        -1.6666654611e-1 + square * (8.3321608736e-3 + square * -1.9515295891e-4)
    )
    cosine = 1.0 - 0.5 * square + square * square * (
        4.166664568298827e-2 + square * (-1.388731625493765e-3 + square * 2.443315711809948e-5)
    )
    sine_square = jnp.where(odd, cosine * cosine, sine * sine)
    cosine_square = jnp.where(odd, sine * sine, cosine * cosine)
    product = sine * cosine
    return sine_square, cosine_square, jnp.where(odd, -product, product)


def join_kernel(geo, scal, *refs):
    raw, far = refs[:5], refs[5]
    own = refs[6:11]
    px, pc = refs[11], refs[12]
    tiles, corners = refs[13 : 13 + geo.sides], refs[13 + geo.sides :]
    g, s = scal[0], scal[1]
    near_y = pl.multiple_of(g * geo.H, 128)
    far_y = pl.multiple_of((1 - g) * geo.H, 128)

    def one(row, carry):
        for k in range(5):
            own[k][row, :, pl.ds(near_y, geo.H)] = raw[k][g * geo.B + row]
            own[k][row, :, pl.ds(far_y, geo.H)] = far[k, row]
        return carry

    lax.fori_loop(0, geo.B, one, 0)
    for side, out in ((g, px), (1 - g, pc)):
        for k in range(2):
            out[k] = own[0][edge_rows(own[0], 2, side, geo) + k]
        for k in range(1, 5):
            out[1 + k] = own[k][edge_rows(own[k], 1, side, geo)]
    items = [(own[0], 2, 0)] + [(own[k], 1, 1 + k) for k in range(1, 5)]
    pack_tiles(items, g, s, tiles, corners, geo)


def first_kernel(geo, scal, *refs):
    n = geo.sides
    now, before, courant, aniso, tilt, xr, cr = refs[:7]
    tiles, xtiles, ctiles = refs[7 : 7 + n], refs[7 + n : 7 + 2 * n], refs[7 + 2 * n : 7 + 3 * n]
    out_block, prior_ext, xx, zz, yy, xz = refs[7 + 3 * n : 13 + 3 * n]
    out_tiles, out_corners = refs[13 + 3 * n : 13 + 4 * n], refs[13 + 4 * n : 13 + 5 * n]
    ext, old, dif, tot, mid, ca, cb, cc = refs[13 + 5 * n :]
    g, s = scal[0], scal[1]
    for k, (dst, own) in enumerate(((old, before), (ca, courant), (cb, aniso), (cc, tilt)), 1):
        fill(dst, own, lambda _, k=k: xr[1 + k], lambda _, k=k: cr[1 + k], tiles, xtiles, ctiles, 1, 1 + k, g, s, geo)
    fill(ext, now, lambda k: xr[k], lambda k: cr[k], tiles, xtiles, ctiles, 2, 0, g, s, geo)

    def coefficients(row, carry):
        at = row - (geo.B - 1)
        speed, stretch = ca[row], 2.0 * cb[row]
        sine_square, cosine_square, product = trig_products(cc[row])
        xx[at] = speed * (1.0 + stretch * cosine_square)
        zz[at] = speed * (1.0 + stretch * sine_square)
        yy[at] = speed * (1.0 + stretch)
        xz[at] = (0.5 * speed) * (stretch * product)
        return carry

    lax.fori_loop(geo.B - 1, 2 * geo.B + 1, coefficients, 0)
    two_steps(ext, mid, lambda row: old[row], prior_ext, out_block, (xx, zz, yy, xz), dif, tot, geo)
    pack_tiles([(out_block, 2, 0)], g, s, out_tiles, out_corners, geo)


def two_steps(ext, mid, prior, prior_ext, out_block, coefs, dif, tot, geo):
    def keep(row, value):
        mid[row] = value
        prior_ext[row - (geo.B - 1)] = value

    def keep_block(row, value):
        out_block[row - geo.B] = value[0 : geo.Z]

    advance(ext, geo.B - 1, geo.B + 2, prior, None, keep, coefs, dif, tot, geo)
    advance(mid, geo.B, geo.B, lambda row: ext[row], None, keep_block, coefs, dif, tot, geo)


def second_kernel(geo, scal, offsets, *refs):
    n = geo.sides
    now, before, xr, cr, courant, refl, refl_far, *coefs = refs[:11]
    tiles, xtiles, ctiles = refs[11 : 11 + n], refs[11 + n : 11 + 2 * n], refs[11 + 2 * n : 11 + 3 * n]
    px, pc, prior_ext, force = refs[11 + 3 * n : 15 + 3 * n]
    out_tiles, out_corners = refs[15 + 3 * n : 15 + 4 * n], refs[15 + 4 * n : 15 + 5 * n]
    ext, dif, tot, mid = refs[15 + 5 * n :]
    g, s = scal[0], scal[1]
    fill(ext, now, None, None, tiles, xtiles, ctiles, 2, 0, g, s, geo)
    fill_blocks(ext, xr, cr, g, geo)
    two_steps(ext, mid, lambda row: before[row - (geo.B - 1)], prior_ext, px, coefs, dif, tot, geo)
    make_source(ext, refl, refl_far, offsets, courant, force, g, geo)

    def one(row, carry):
        pc[row] = px[row]
        return carry

    lax.fori_loop(0, geo.B, one, 0)
    for side, out in ((g, px), (1 - g, pc)):
        for k in range(2):
            out[geo.B + k] = force[edge_rows(force, 2, side, geo) + k]
    pack_tiles([(px, 2, 0), (force, 2, 4)], g, s, out_tiles, out_corners, geo)


def third_kernel(geo, scal, offsets, *refs):
    n = geo.sides
    now, before, xr, cr, courant, refl, refl_far, *coefs = refs[:11]
    force = refs[11]
    tiles, xtiles, ctiles = refs[12 : 12 + n], refs[12 + n : 12 + 2 * n], refs[12 + 2 * n : 12 + 3 * n]
    px, pc, force_out, scat, scat_prior = refs[12 + 3 * n : 17 + 3 * n]
    out_tiles, out_corners = refs[17 + 3 * n : 17 + 4 * n], refs[17 + 4 * n : 17 + 5 * n]
    ext, dif, tot, mid, wave = refs[17 + 5 * n :]
    g, s = scal[0], scal[1]
    B = geo.B
    fill(ext, now, None, None, tiles, xtiles, ctiles, 2, 0, g, s, geo)
    fill_blocks(ext, xr, cr, g, geo)
    def keep_mid(row, value):
        mid[row] = value

    def keep_block(row, value):
        px[row - B] = value[0 : geo.Z]
        pc[row - B] = value[0 : geo.Z]

    advance(ext, B - 1, B + 2, lambda row: before[row - (B - 1)], None, keep_mid, coefs, dif, tot, geo)
    advance(mid, B, B, lambda row: ext[row], None, keep_block, coefs, dif, tot, geo)
    make_source(ext, refl, refl_far, offsets, courant, force_out, g, geo)
    fill(wave, force, lambda k: xr[B + k], lambda k: cr[B + k], tiles, xtiles, ctiles, 2, 4, g, s, geo)

    def keep_wave(row, value):
        mid[row] = value
        scat_prior[row - (B - 1)] = value

    def keep_scat(row, value):
        scat[row - B] = value[0 : geo.Z] + force_out[row - B]

    advance(wave, B - 1, B + 2, lambda row: -wave[row], None, keep_wave, coefs, dif, tot, geo)
    advance(mid, B, B, lambda row: wave[row], None, keep_scat, coefs, dif, tot, geo)
    for side, out in ((g, px), (1 - g, pc)):
        for k in range(2):
            out[B + k] = scat[edge_rows(scat, 2, side, geo) + k]
        out[B + 2] = force_out[edge_rows(force_out, 1, side, geo)]
    pack_tiles([(scat, 2, 0), (force_out, 1, 2)], g, s, out_tiles, out_corners, geo)


def fourth_kernel(geo, scal, offsets, *refs):
    n = geo.sides
    now, scat, before, xr, cr, courant, refl, refl_far, *coefs = refs[:12]
    force2 = refs[12]
    tiles, xtiles, ctiles = refs[13 : 13 + n], refs[13 + n : 13 + 2 * n], refs[13 + 2 * n : 13 + 3 * n]
    scat_out, scat_prior, force_out, px, pc, back = refs[13 + 3 * n : 19 + 3 * n]
    out_rows, out_corners = refs[19 + 3 * n : 19 + 4 * n], refs[19 + 4 * n : 19 + 5 * n]
    ext, dif, tot, mid, wave = refs[19 + 5 * n :]
    g, s = scal[0], scal[1]
    B = geo.B

    def own(row, carry):
        ext[B + row, 0 : geo.Z, :] = now[row]
        back[row] = now[row, :, pl.ds(pl.multiple_of((1 - g) * geo.H, 128), geo.H)]
        return carry

    lax.fori_loop(0, B, own, 0)
    fill_blocks(ext, xr, cr, g, geo)
    make_source(ext, refl, refl_far, offsets, courant, force_out, g, geo)
    fill(wave, scat, lambda k: xr[B + k], lambda k: cr[B + k], tiles, xtiles, ctiles, 2, 0, g, s, geo)
    fill(ext, force2, lambda k: xr[B + 2], lambda k: cr[B + 2], tiles, xtiles, ctiles, 1, 2, g, s, geo)

    def keep_wave(row, value):
        mid[row] = value

    def keep_scat(row, value):
        scat_out[row - B] = value[0 : geo.Z] + force_out[row - B]
        scat_prior[row - B] = mid[row, 0 : geo.Z, :]

    advance(wave, B - 1, B + 2, lambda row: before[row - (B - 1)], lambda row: ext[row], keep_wave, coefs, dif, tot, geo)
    advance(mid, B, B, lambda row: wave[row], None, keep_scat, coefs, dif, tot, geo)
    px[0] = scat_out[edge_rows(scat_out, 1, g, geo)]
    pc[0] = scat_out[edge_rows(scat_out, 1, 1 - g, geo)]
    for sender, rows, corner in zip(senders(s, geo), out_rows, out_corners):
        for row in range(B):
            tile = edge_tile(scat_out, row, sender, geo)
            rows[row : row + 1, :] = jnp.where(sender == 0, tile[TILE - 1 : TILE], tile[0:1])
        tile = edge_tile(scat_out, g * (B - 1), sender, geo)
        corner[...] = jnp.where(sender == 0, tile[TILE - 1 : TILE], tile[0:1])


def fifth_kernel(geo, scal, *refs):
    n = geo.sides
    scat, before, force, xr, cr, *coefs = refs[:9]
    rows, xrows, crows = refs[9 : 9 + n], refs[9 + n : 9 + 2 * n], refs[9 + 2 * n : 9 + 3 * n]
    out_near, out_far = refs[9 + 3 * n : 11 + 3 * n]
    ext, dif, tot = refs[11 + 3 * n :]
    g, s = scal[0], scal[1]
    B = geo.B
    places = [(row, rows, row) for row in range(B)]

    def halo(place, offset, sender, value):
        whole = jnp.broadcast_to(value, (TILE, geo.Y))
        ext[place, offset : offset + TILE, :] = jnp.where(tile_mask(sender, 1, 0, geo.Y), whole, 0.0)

    def own(row, carry):
        ext[B + row, 0 : geo.Z, :] = scat[row]
        return carry

    lax.fori_loop(0, B, own, 0)
    for (offset, sender), ref in zip(receivers(s, geo), rows):
        for row in range(B):
            halo(B + row, offset, sender, ref[row : row + 1, :])
    for side, line, edge in ((g, xr, xrows), (1 - g, cr, crows)):
        _, place = near_side(side, geo)
        ext[place, 0 : geo.Z, :] = line[0]
        for (offset, sender), ref in zip(receivers(s, geo), edge):
            halo(place, offset, sender, ref[...])
    near = pl.multiple_of(g * geo.H, 128)
    far = pl.multiple_of((1 - g) * geo.H, 128)

    def keep(row, value):
        ext[row, 0 : geo.Z, :] = ext[row, 0 : geo.Z, :]
        dif[0, 0 : geo.Z, :] = value[0 : geo.Z] - before[row - B] + force[row - B]
        out_near[row - B] = dif[0, 0 : geo.Z, pl.ds(near, geo.H)]
        out_far[row - B] = dif[0, 0 : geo.Z, pl.ds(far, geo.H)]

    advance(ext, B, B, lambda row: 0.0, None, keep, coefs, dif, tot, geo)


def shards(sections, gx, wave_now, wave_before, courant, anisotropy, tilt, reflectivity, offsets):
    rows, depth, half = wave_now.shape
    geo = Geometry(rows, depth, half, sections)
    B, Z, H, Y, ZE, n = geo.B, geo.Z, geo.H, geo.Y, geo.ZE, geo.sides
    g = lax.axis_index("gy")
    s = lax.axis_index("section")
    scal = jnp.stack([g, s]).astype(jnp.int32)
    swap = [(0, 1), (1, 0)]
    pairs_x = [p for i in range(gx - 1) for p in ((2 * i + 1, 2 * i + 2), (2 * i + 2, 2 * i + 1))]

    def z_moves():
        if geo.two:
            return [[(0, 1), (1, 0)]]
        return [[(i, i + 1) for i in range(sections - 1)], [(i + 1, i) for i in range(sections - 1)]]

    def corner_pairs(move):
        out = []
        for a, b in pairs_x:
            for i, j in move:
                out.append((((a // 2) * sections + i) * 2 + a % 2, ((b // 2) * sections + j) * 2 + b % 2))
        return out

    def chip(value):
        return lax.ppermute(value, "gy", swap)

    def exchange(px, pc, tiles, corners, depth):
        xr = lax.ppermute(px, ("gx", "gy"), pairs_x)
        zr = [lax.ppermute(t, "section", m) for t, m in zip(tiles, z_moves())]
        xz = [lax.ppermute(t, ("gx", "section", "gy"), corner_pairs(m)) for t, m in zip(corners, z_moves())]
        cr = chip(pc)
        start = (1 - g) * (B - depth)
        cz = [chip(lax.dynamic_slice_in_dim(t, start, depth, 0)) for t in zr]
        return xr, cr, [*zr, *xz, *cz]

    def shape(*dims):
        return jax.ShapeDtypeStruct(dims, F32)

    def call(kernel, inputs, outs, scratch, smem=1):
        specs = [pl.BlockSpec(memory_space=pltpu.SMEM)] * smem
        specs += [pl.BlockSpec(memory_space=pltpu.VMEM)] * (len(inputs) - smem)
        return pl.pallas_call(
            functools.partial(kernel, geo),
            out_shape=outs,
            in_specs=specs,
            out_specs=[pl.BlockSpec(memory_space=pltpu.VMEM)] * len(outs),
            scratch_shapes=[pltpu.VMEM(d, F32) for d in scratch],
        )(*inputs)

    block, wide, ext = (B, Z, Y), (B + 2, ZE, Y), (3 * B, ZE, Y)
    tile_outs = [shape(B, TILE, Y)] * n + [shape(2, TILE, Y)] * n
    fields = (wave_now, wave_before, courant, anisotropy, tilt)
    other = (1 - g) * B
    far = chip(jnp.stack([lax.dynamic_slice_in_dim(f, other, B, 0) for f in fields]))
    *own, px, pc, r0, r1 = _split(
        call(join_kernel, [scal, *fields, far], [shape(*block)] * 5 + [shape(6, Z, Y)] * 2 + tile_outs, []), 7, n
    )
    xr, cr, halo = exchange(px, pc, r0, r1, 2)
    refl_far = chip(lax.dynamic_slice_in_dim(reflectivity, other, B, 1).astype(F32))
    now, prior, *coefs, r0, r1 = _split(
        call(first_kernel, [scal, *own, xr, cr, *halo], [shape(*block)] + [shape(*wide)] * 5 + tile_outs, [ext] * 8), 6, n
    )
    xr, cr, halo = exchange(now, now, r0, r1, 2)
    px, pc, prior, force, r0, r1 = _split(
        call(
            second_kernel,
            [scal, offsets, now, prior, xr, cr, own[2], reflectivity, refl_far, *coefs, *halo],
            [shape(B + 2, Z, Y)] * 2 + [shape(*wide), shape(*block)] + tile_outs,
            [ext] * 4,
            2,
        ),
        4,
        n,
    )
    xr, cr, halo = exchange(px, pc, r0, r1, 2)
    px, pc, force2, scat, scat_prior, r0, r1 = _split(
        call(
            third_kernel,
            [scal, offsets, px, prior, xr, cr, own[2], reflectivity, refl_far, *coefs, force, *halo],
            [shape(B + 3, Z, Y)] * 2 + [shape(*block)] * 2 + [shape(*wide)] + tile_outs,
            [ext] * 5,
            2,
        ),
        5,
        n,
    )
    xr, cr, halo = exchange(px, pc, r0, r1, 2)
    scat, scat_prior, force3, qx, qc, back, r0, r1 = _split(
        call(
            fourth_kernel,
            [scal, offsets, px, scat, scat_prior, xr, cr, own[2], reflectivity, refl_far, *coefs, force2, *halo],
            [shape(*block)] * 3
            + [shape(1, Z, Y)] * 2
            + [shape(B, Z, H)]
            + [shape(B, Y)] * n
            + [shape(1, Y)] * n,
            [ext] * 5,
            2,
        ),
        6,
        n,
    )
    xr, cr, halo = exchange(qx, qc, r0, r1, 1)
    near_w, far_w = call(fifth_kernel, [scal, scat, scat_prior, force3, xr, cr, *coefs, *halo], [shape(B, Z, H)] * 2, [ext] * 3)
    near_u = lax.dynamic_slice_in_dim(px[:B], g * H, H, 2)

    def joined(near, other):
        return jnp.where(g == 0, jnp.concatenate([near, other], 0), jnp.concatenate([other, near], 0))

    return joined(near_u, chip(back)), joined(near_w, chip(far_w))


def _split(values, count, n):
    return [*values[:count], values[count : count + n], values[count + n :]]


def solution(mesh):
    spec = P(("shot", "gx"), "section", "gy")
    assert mesh.shape["gy"] == 2
    return jax.shard_map(
        functools.partial(shards, mesh.shape["section"], mesh.shape["gx"]),
        mesh=mesh,
        in_specs=(spec,) * 5 + (P(None, ("shot", "gx"), "section", "gy"), P()),
        out_specs=(spec, spec),
        check_vma=False,
    )
```

```python
import functools

import jax
import jax.numpy as jnp
from jax import lax
from jax.experimental import pallas as pl
from jax.experimental.pallas import tpu as pltpu
from jax.sharding import PartitionSpec as P


NOFF = 17
MARGIN = 16
TILE = 8
F32 = jnp.float32
UNROLL = 4
SLACK = 8 << 20


class Geometry:
    def __init__(self, rows, depth, half, sections):
        self.B, self.Z, self.H, self.Y = rows // 2, depth, half, 2 * half
        self.two = sections == 2
        self.sides = 1 if self.two else 2
        self.ZE = depth + TILE * self.sides
        assert self.B >= MARGIN and depth % TILE == 0 and half % 128 == 0


def near_side(side, geo):
    first = (geo.B - 2) + side * (geo.B + 2)
    return first, first + 1 - side


def tile_mask(sender, depth, turn, width):
    place = lax.broadcasted_iota(jnp.int32, (TILE, width), 0)
    place = lax.rem(place + (TILE - turn), TILE)
    start = (1 - sender) * (TILE - depth)
    return (place >= start) & (place < start + depth)


def turned(value, turn):
    turn = turn % TILE
    return value if turn == 0 else pltpu.roll(value, turn, 0)


def senders(s, geo):
    return [s] if geo.two else [0, 1]


def receivers(s, geo):
    return [(geo.Z, 1 - s)] if geo.two else [(geo.ZE - TILE, 0), (geo.Z, 1)]


def edge_tile(ref, row, sender, geo):
    start = pl.multiple_of((1 - sender) * (geo.Z - TILE), TILE)
    return ref[row, pl.ds(start, TILE), :]


def pack_corner(items, row, sender, geo):
    out = jnp.zeros((TILE, geo.Y), F32)
    for ref, depth, turn in items:
        value = turned(edge_tile(ref, row, sender, geo), turn)
        out = jnp.where(tile_mask(sender, depth, turn, geo.Y), value, out)
    return out


def tiles_of(depths, geo):
    starts, total = [], 0
    for depth in depths:
        starts.append(total)
        total += geo.B * depth // TILE
    return starts, total


def pack_tiles(items, g, s, tiles, corners, geo):
    starts, _ = tiles_of([depth for _, depth, _ in items], geo)
    for sender, tile_ref, corner_ref in zip(senders(s, geo), tiles, corners):
        for (ref, depth, _), start in zip(items, starts):
            per = TILE // depth
            masks = [tile_mask(sender, depth, k * depth, geo.Y) for k in range(1, per)]
            for q in range(geo.B // per):
                out = edge_tile(ref, q * per, sender, geo)
                for k in range(1, per):
                    value = turned(edge_tile(ref, q * per + k, sender, geo), k * depth)
                    out = jnp.where(masks[k - 1], value, out)
                tile_ref[start + q] = out
        for k in range(corner_ref.shape[0]):
            row = g * (geo.B - corner_ref.shape[0]) + k
            corner_ref[k] = pack_corner(items, row, sender, geo)


def unpack_row(ref, start, x, depth, sender, geo):
    per = TILE // depth
    value = turned(ref[start + x // per], TILE - (x % per) * depth)
    return jnp.where(tile_mask(sender, depth, 0, geo.Y), value, 0.0)


def fill(dst, own, xrow, crow, tiles, xtiles, ctiles, start, depth, turn, g, s, geo):
    ends = list(zip(receivers(s, geo), tiles, xtiles, ctiles))

    def one(row, carry):
        dst[geo.B + row, 0 : geo.Z, :] = own[row]
        return carry

    lax.fori_loop(0, geo.B, one, 0, unroll=4)
    for (offset, sender), tile, _, _ in ends:
        for row in range(geo.B):
            dst[geo.B + row, offset : offset + TILE, :] = unpack_row(tile, start, row, depth, sender, geo)
    for side, get, is_x in ((g, xrow, True), (1 - g, crow, False)):
        first, nearest = near_side(side, geo)
        for k in range(depth):
            place = first + k if depth == 2 else nearest
            if get is not None:
                dst[place, 0 : geo.Z, :] = get(k)
            for (offset, sender), _, xtile, ctile in ends:
                if is_x:
                    index = k if depth == xtile.shape[0] else 1 - side
                    value = turned(xtile[index], TILE - turn)
                    value = jnp.where(tile_mask(sender, depth, 0, geo.Y), value, 0.0)
                else:
                    low = unpack_row(ctile, start, k, depth, sender, geo)
                    high = unpack_row(ctile, start, geo.B - depth + k, depth, sender, geo)
                    value = jnp.where(side == 1, low, high)
                dst[place, offset : offset + TILE, :] = value


def fill_blocks(dst, xblock, cblock, g, geo):
    def one(row, carry):
        dst[g * 2 * geo.B + row, 0 : geo.Z, :] = xblock[row]
        dst[(1 - g) * 2 * geo.B + row, 0 : geo.Z, :] = cblock[row]
        return carry

    lax.fori_loop(0, geo.B, one, 0)


def each(first, count, body, group):
    group = max(k for k in range(1, group + 1) if count % k == 0)

    def trip(index, carry):
        for k in range(group):
            body(first + index * group + k)
        return carry

    lax.fori_loop(0, count // group, trip, 0)


def advance(src, first, count, prior, extra, store, coefs, dif, tot, geo):
    xx, zz, yy, xz = coefs

    def rolls(row):
        value = src[row]
        above = pltpu.roll(value, geo.ZE - 1, 0)
        below = pltpu.roll(value, 1, 0)
        dif[row] = above - below
        tot[row] = above + below

    each(first - 1, count + 2, rolls, 6)
    lane = lax.broadcasted_iota(jnp.int32, (geo.ZE, geo.Y), 1)

    def one(row):
        at = row - (geo.B - 1)
        value = src[row]
        right = jnp.where(lane == geo.Y - 1, 0.0, pltpu.roll(value, geo.Y - 1, 1))
        left = jnp.where(lane == 0, 0.0, pltpu.roll(value, 1, 1))
        cx, cz, cy = xx[at], zz[at], yy[at]
        out = (2.0 - 2.0 * (cx + cz + cy)) * value - prior(row)
        out = out + cx * (src[row + 1] + src[row - 1]) + cz * tot[row] + cy * (right + left)
        out = out + xz[at] * (dif[row + 1] - dif[row - 1])
        if extra is not None:
            out = out + extra(row)
        store(row, out)

    each(first, count, one, UNROLL)


def make_source(ext, refl, refl_far, offsets, courant, out, g, geo):
    near = pl.multiple_of(g * geo.H, 128)
    far = pl.multiple_of((1 - g) * geo.H, 128)

    def one(row):
        acc = jnp.zeros((geo.Z, geo.H), F32)
        acc_far = jnp.zeros((geo.Z, geo.H), F32)
        for h in range(NOFF):
            place = geo.B + row + offsets[h]
            acc = acc + refl[h, g * geo.B + row].astype(F32) * ext[place, 0 : geo.Z, pl.ds(near, geo.H)]
            acc_far = acc_far + refl_far[h, row] * ext[place, 0 : geo.Z, pl.ds(far, geo.H)]
        out[row, :, pl.ds(near, geo.H)] = courant[row, :, pl.ds(near, geo.H)] * acc
        out[row, :, pl.ds(far, geo.H)] = courant[row, :, pl.ds(far, geo.H)] * acc_far

    each(0, geo.B, one, 2)


def edge_rows(depth, side, geo):
    return side * (geo.B - depth)


def trig_products(angle):
    turns = jnp.floor(angle * 0.6366197723675814 + 0.5)
    rest = angle - turns * 1.5703125
    rest = rest - turns * 4.837512969970703125e-4
    rest = rest - turns * 7.549789954891882e-8
    odd = (turns - 2.0 * jnp.floor(turns * 0.5)) > 0.5
    square = rest * rest
    sine = rest + rest * square * (
        -1.6666654611e-1 + square * (8.3321608736e-3 + square * -1.9515295891e-4)
    )
    cosine = 1.0 - 0.5 * square + square * square * (
        4.166664568298827e-2 + square * (-1.388731625493765e-3 + square * 2.443315711809948e-5)
    )
    sine_square = jnp.where(odd, cosine * cosine, sine * sine)
    cosine_square = jnp.where(odd, sine * sine, cosine * cosine)
    product = sine * cosine
    return sine_square, cosine_square, jnp.where(odd, -product, product)


def half_kernel(geo, scal, *refs):
    *fields, out = refs

    def one(row, carry):
        for k, field in enumerate(fields):
            out[k, row] = field[row]
        return carry

    lax.fori_loop(0, geo.B, one, 0, unroll=4)


def widen_kernel(geo, scal, refl, out):
    def one(h, carry):
        for row in range(geo.B):
            out[h, row] = refl[h, row].astype(F32)
        return carry

    lax.fori_loop(0, NOFF, one, 0)


def join_kernel(geo, scal, *refs):
    raw, far = refs[:5], refs[5]
    own = refs[6:11]
    px, pc = refs[11], refs[12]
    tiles, corners = refs[13 : 13 + geo.sides], refs[13 + geo.sides :]
    g, s = scal[0], scal[1]
    near_y = pl.multiple_of(g * geo.H, 128)
    far_y = pl.multiple_of((1 - g) * geo.H, 128)

    def one(row, carry):
        for k in range(5):
            own[k][row, :, pl.ds(near_y, geo.H)] = raw[k][row]
            own[k][row, :, pl.ds(far_y, geo.H)] = far[k, row]
        return carry

    lax.fori_loop(0, geo.B, one, 0, unroll=2)
    for side, out in ((g, px), (1 - g, pc)):
        for k in range(2):
            out[k] = own[0][edge_rows(2, side, geo) + k]
        for k in range(1, 5):
            out[1 + k] = own[k][edge_rows(1, side, geo)]
    items = [(own[0], 2, 0)] + [(own[k], 1, 1 + k) for k in range(1, 5)]
    pack_tiles(items, g, s, tiles, corners, geo)


def first_kernel(geo, scal, *refs):
    n = geo.sides
    now, before, courant, aniso, tilt, xr, cr = refs[:7]
    tiles, xtiles, ctiles = refs[7 : 7 + n], refs[7 + n : 7 + 2 * n], refs[7 + 2 * n : 7 + 3 * n]
    out_block, prior_ext, xx, zz, yy, xz = refs[7 + 3 * n : 13 + 3 * n]
    out_tiles, out_corners = refs[13 + 3 * n : 13 + 4 * n], refs[13 + 4 * n : 13 + 5 * n]
    ext, old, dif, tot, mid, ca, cb, cc = refs[13 + 5 * n :]
    g, s = scal[0], scal[1]
    starts, _ = tiles_of([2, 1, 1, 1, 1], geo)
    for k, (dst, own) in enumerate(((old, before), (ca, courant), (cb, aniso), (cc, tilt)), 1):
        xrow, crow = (lambda _, k=k: xr[1 + k]), (lambda _, k=k: cr[1 + k])
        fill(dst, own, xrow, crow, tiles, xtiles, ctiles, starts[k], 1, 1 + k, g, s, geo)
    fill(ext, now, lambda k: xr[k], lambda k: cr[k], tiles, xtiles, ctiles, 0, 2, 0, g, s, geo)

    def coefficients(row, carry):
        at = row - (geo.B - 1)
        speed, stretch = ca[row], 2.0 * cb[row]
        sine_square, cosine_square, product = trig_products(cc[row])
        xx[at] = speed * (1.0 + stretch * cosine_square)
        zz[at] = speed * (1.0 + stretch * sine_square)
        yy[at] = speed * (1.0 + stretch)
        xz[at] = (0.5 * speed) * (stretch * product)
        return carry

    lax.fori_loop(geo.B - 1, 2 * geo.B + 1, coefficients, 0)
    two_steps(ext, mid, lambda row: old[row], prior_ext, out_block, (xx, zz, yy, xz), dif, tot, geo)
    pack_tiles([(out_block, 2, 0)], g, s, out_tiles, out_corners, geo)


def two_steps(ext, mid, prior, prior_ext, out_block, coefs, dif, tot, geo):
    def keep(row, value):
        mid[row] = value
        prior_ext[row - (geo.B - 1)] = value

    def keep_block(row, value):
        out_block[row - geo.B] = value[0 : geo.Z]

    advance(ext, geo.B - 1, geo.B + 2, prior, None, keep, coefs, dif, tot, geo)
    advance(mid, geo.B, geo.B, lambda row: ext[row], None, keep_block, coefs, dif, tot, geo)


def second_kernel(geo, scal, offsets, *refs):
    n = geo.sides
    now, before, xr, cr, courant, refl, refl_far, *coefs = refs[:11]
    tiles, xtiles, ctiles = refs[11 : 11 + n], refs[11 + n : 11 + 2 * n], refs[11 + 2 * n : 11 + 3 * n]
    px, pc, prior_ext, force = refs[11 + 3 * n : 15 + 3 * n]
    out_tiles, out_corners = refs[15 + 3 * n : 15 + 4 * n], refs[15 + 4 * n : 15 + 5 * n]
    ext, dif, tot, mid = refs[15 + 5 * n :]
    g, s = scal[0], scal[1]
    fill(ext, now, None, None, tiles, xtiles, ctiles, 0, 2, 0, g, s, geo)
    fill_blocks(ext, xr, cr, g, geo)
    two_steps(ext, mid, lambda row: before[row - (geo.B - 1)], prior_ext, px, coefs, dif, tot, geo)
    make_source(ext, refl, refl_far, offsets, courant, force, g, geo)

    def one(row, carry):
        pc[row] = px[row]
        return carry

    lax.fori_loop(0, geo.B, one, 0)
    for side, out in ((g, px), (1 - g, pc)):
        for k in range(2):
            out[geo.B + k] = force[edge_rows(2, side, geo) + k]
    pack_tiles([(px, 2, 0), (force, 2, 4)], g, s, out_tiles, out_corners, geo)


def third_kernel(geo, scal, offsets, *refs):
    n = geo.sides
    now, before, xr, cr, courant, refl, refl_far, *coefs = refs[:11]
    force = refs[11]
    tiles, xtiles, ctiles = refs[12 : 12 + n], refs[12 + n : 12 + 2 * n], refs[12 + 2 * n : 12 + 3 * n]
    px, pc, force_out, scat, scat_prior = refs[12 + 3 * n : 17 + 3 * n]
    out_tiles, out_corners = refs[17 + 3 * n : 17 + 4 * n], refs[17 + 4 * n : 17 + 5 * n]
    ext, dif, tot, mid, wave = refs[17 + 5 * n :]
    g, s = scal[0], scal[1]
    B = geo.B
    fill(ext, now, None, None, tiles, xtiles, ctiles, 0, 2, 0, g, s, geo)
    fill_blocks(ext, xr, cr, g, geo)

    def keep_mid(row, value):
        mid[row] = value

    def keep_block(row, value):
        px[row - B] = value[0 : geo.Z]
        pc[row - B] = value[0 : geo.Z]

    advance(ext, B - 1, B + 2, lambda row: before[row - (B - 1)], None, keep_mid, coefs, dif, tot, geo)
    advance(mid, B, B, lambda row: ext[row], None, keep_block, coefs, dif, tot, geo)
    make_source(ext, refl, refl_far, offsets, courant, force_out, g, geo)
    start = tiles_of([2, 2], geo)[0][1]
    fill(wave, force, lambda k: xr[B + k], lambda k: cr[B + k], tiles, xtiles, ctiles, start, 2, 4, g, s, geo)

    def keep_wave(row, value):
        mid[row] = value
        scat_prior[row - (B - 1)] = value

    def keep_scat(row, value):
        scat[row - B] = value[0 : geo.Z] + force_out[row - B]

    advance(wave, B - 1, B + 2, lambda row: -wave[row], None, keep_wave, coefs, dif, tot, geo)
    advance(mid, B, B, lambda row: wave[row], None, keep_scat, coefs, dif, tot, geo)
    for side, out in ((g, px), (1 - g, pc)):
        for k in range(2):
            out[B + k] = scat[edge_rows(2, side, geo) + k]
        out[B + 2] = force_out[edge_rows(1, side, geo)]
    pack_tiles([(scat, 2, 0), (force_out, 1, 2)], g, s, out_tiles, out_corners, geo)


def fourth_kernel(geo, scal, offsets, *refs):
    n = geo.sides
    now, scat, before, xr, cr, courant, refl, refl_far, *coefs = refs[:12]
    force2 = refs[12]
    tiles, xtiles, ctiles = refs[13 : 13 + n], refs[13 + n : 13 + 2 * n], refs[13 + 2 * n : 13 + 3 * n]
    scat_out, scat_prior, force_out, px, pc, near, back = refs[13 + 3 * n : 20 + 3 * n]
    out_tiles, out_corners = refs[20 + 3 * n : 20 + 4 * n], refs[20 + 4 * n : 20 + 5 * n]
    ext, dif, tot, mid, wave = refs[20 + 5 * n :]
    g, s = scal[0], scal[1]
    B = geo.B

    def own(row, carry):
        ext[B + row, 0 : geo.Z, :] = now[row]
        back[row] = now[row, :, pl.ds(pl.multiple_of((1 - g) * geo.H, 128), geo.H)]
        near[row] = now[row, :, pl.ds(pl.multiple_of(g * geo.H, 128), geo.H)]
        return carry

    lax.fori_loop(0, B, own, 0)
    fill_blocks(ext, xr, cr, g, geo)
    make_source(ext, refl, refl_far, offsets, courant, force_out, g, geo)
    fill(wave, scat, lambda k: xr[B + k], lambda k: cr[B + k], tiles, xtiles, ctiles, 0, 2, 0, g, s, geo)
    start = tiles_of([2, 1], geo)[0][1]
    fill(ext, force2, lambda _: xr[B + 2], lambda _: cr[B + 2], tiles, xtiles, ctiles, start, 1, 2, g, s, geo)

    def keep_wave(row, value):
        mid[row] = value

    def keep_scat(row, value):
        scat_out[row - B] = value[0 : geo.Z] + force_out[row - B]
        scat_prior[row - B] = mid[row, 0 : geo.Z, :]

    advance(wave, B - 1, B + 2, lambda row: before[row - (B - 1)], lambda row: ext[row], keep_wave, coefs, dif, tot, geo)
    advance(mid, B, B, lambda row: wave[row], None, keep_scat, coefs, dif, tot, geo)
    px[0] = scat_out[edge_rows(1, g, geo)]
    pc[0] = scat_out[edge_rows(1, 1 - g, geo)]
    pack_tiles([(scat_out, 1, 0)], g, s, out_tiles, out_corners, geo)


def fifth_kernel(geo, scal, *refs):
    n = geo.sides
    scat, before, force, xr, cr, *coefs = refs[:9]
    tiles, xtiles, ctiles = refs[9 : 9 + n], refs[9 + n : 9 + 2 * n], refs[9 + 2 * n : 9 + 3 * n]
    out_near, out_far = refs[9 + 3 * n : 11 + 3 * n]
    ext, dif, tot = refs[11 + 3 * n :]
    g, s = scal[0], scal[1]
    B = geo.B
    fill(ext, scat, lambda _: xr[0], lambda _: cr[0], tiles, xtiles, ctiles, 0, 1, 0, g, s, geo)
    low, high = slice(0, geo.H), slice(geo.H, geo.Y)

    def keep(row, value):
        at = row - B
        value = value[0 : geo.Z] - before[at] + force[at]
        out_near[at] = jnp.where(g == 0, value[:, low], value[:, high])
        out_far[at] = jnp.where(g == 0, value[:, high], value[:, low])

    advance(ext, B, B, lambda row: 0.0, None, keep, coefs, dif, tot, geo)


def finish_kernel(geo, scal, near, far, out):
    g = scal[0]

    def one(row, carry):
        out[g * geo.B + row] = near[row]
        out[(1 - g) * geo.B + row] = far[row]
        return carry

    lax.fori_loop(0, geo.B, one, 0, unroll=4)


def shards(sections, gx, wave_now, wave_before, courant, anisotropy, tilt, reflectivity, offsets):
    rows, depth, half = wave_now.shape
    geo = Geometry(rows, depth, half, sections)
    B, Z, H, Y, ZE, n = geo.B, geo.Z, geo.H, geo.Y, geo.ZE, geo.sides
    g = lax.axis_index("gy")
    s = lax.axis_index("section")
    scal = jnp.stack([g, s]).astype(jnp.int32)
    swap = [(0, 1), (1, 0)]
    pairs_x = [p for i in range(gx - 1) for p in ((2 * i + 1, 2 * i + 2), (2 * i + 2, 2 * i + 1))]

    def z_moves():
        if geo.two:
            return [[(0, 1), (1, 0)]]
        return [[(i, i + 1) for i in range(sections - 1)], [(i + 1, i) for i in range(sections - 1)]]

    def corner_pairs(move):
        out = []
        for a, b in pairs_x:
            for i, j in move:
                out.append((((a // 2) * sections + i) * 2 + a % 2, ((b // 2) * sections + j) * 2 + b % 2))
        return out

    def chip(value):
        return lax.ppermute(value, "gy", swap)

    def exchange(px, pc, tiles, corners):
        xr = lax.ppermute(px, ("gx", "gy"), pairs_x)
        xz = [
            lax.ppermute(t, ("gx", "section", "gy"), corner_pairs(m)) for t, m in zip(corners, z_moves())
        ]
        zr = [lax.ppermute(t, "section", m) for t, m in zip(tiles, z_moves())]
        cr = chip(pc)
        cz = [chip(t) for t in zr]
        return xr, cr, [*zr, *xz, *cz]

    def shape(*dims):
        return jax.ShapeDtypeStruct(dims, F32)

    def call(kernel, inputs, outs, scratch, smem=1, specs=None):
        if specs is None:
            specs = [pl.BlockSpec(memory_space=pltpu.SMEM)] * (smem - 1)
            specs += [pl.BlockSpec(memory_space=pltpu.VMEM)] * (len(inputs) - smem)
        used = sum(4 * d[0] * d[1] * d[2] for d in scratch)
        return pl.pallas_call(
            functools.partial(kernel, geo),
            out_shape=outs,
            grid_spec=pltpu.PrefetchScalarGridSpec(
                num_scalar_prefetch=1,
                grid=(1,),
                in_specs=specs,
                out_specs=[pl.BlockSpec(memory_space=pltpu.VMEM)] * len(outs),
                scratch_shapes=[pltpu.VMEM(d, F32) for d in scratch],
            ),
            compiler_params=pltpu.CompilerParams(vmem_limit_bytes=used + SLACK),
        )(*inputs)

    block, wide, ext = (B, Z, Y), (B + 2, ZE, Y), (3 * B, ZE, Y)

    def tile_outs(depths, corner=2):
        return [shape(tiles_of(depths, geo)[1], TILE, Y)] * n + [shape(corner, TILE, Y)] * n

    fields = (wave_now, wave_before, courant, anisotropy, tilt)
    near_half = pl.BlockSpec((B, Z, H), lambda i, scal: (scal[0], 0, 0))
    far_half = pl.BlockSpec((B, Z, H), lambda i, scal: (1 - scal[0], 0, 0))
    whole = pl.BlockSpec(memory_space=pltpu.VMEM)
    (sent,) = call(half_kernel, [scal, *fields], [shape(5, B, Z, H)], [], specs=[far_half] * 5)
    far = chip(sent)
    *own, px, pc, r0, r1 = _split(
        call(
            join_kernel,
            [scal, *fields, far],
            [shape(*block)] * 5 + [shape(6, Z, Y)] * 2 + tile_outs([2, 1, 1, 1, 1]),
            [],
            specs=[near_half] * 5 + [whole],
        ),
        7,
        n,
    )
    xr, cr, halo = exchange(px, pc, r0, r1)
    refl_half = pl.BlockSpec((NOFF, B, Z, H), lambda i, scal: (0, 1 - scal[0], 0, 0))
    (refl_far,) = call(widen_kernel, [scal, reflectivity], [shape(NOFF, B, Z, H)], [], specs=[refl_half])
    refl_far = chip(refl_far)
    now, prior, *coefs, r0, r1 = _split(
        call(
            first_kernel, [scal, *own, xr, cr, *halo], [shape(*block)] + [shape(*wide)] * 5 + tile_outs([2]), [ext] * 8
        ),
        6,
        n,
    )
    xr, cr, halo = exchange(now, now, r0, r1)
    px, pc, prior, force, r0, r1 = _split(
        call(
            second_kernel,
            [scal, offsets, now, prior, xr, cr, own[2], reflectivity, refl_far, *coefs, *halo],
            [shape(B + 2, Z, Y)] * 2 + [shape(*wide), shape(*block)] + tile_outs([2, 2]),
            [ext] * 4,
            2,
        ),
        4,
        n,
    )
    xr, cr, halo = exchange(px, pc, r0, r1)
    px, pc, force2, scat, scat_prior, r0, r1 = _split(
        call(
            third_kernel,
            [scal, offsets, px, prior, xr, cr, own[2], reflectivity, refl_far, *coefs, force, *halo],
            [shape(B + 3, Z, Y)] * 2 + [shape(*block)] * 2 + [shape(*wide)] + tile_outs([2, 1]),
            [ext] * 5,
            2,
        ),
        5,
        n,
    )
    xr, cr, halo = exchange(px, pc, r0, r1)
    scat, scat_prior, force3, qx, qc, near_u, back, r0, r1 = _split(
        call(
            fourth_kernel,
            [scal, offsets, px, scat, scat_prior, xr, cr, own[2], reflectivity, refl_far, *coefs, force2, *halo],
            [shape(*block)] * 3 + [shape(1, Z, Y)] * 2 + [shape(B, Z, H)] * 2 + tile_outs([1], 1),
            [ext] * 5,
            2,
        ),
        7,
        n,
    )
    xr, cr, halo = exchange(qx, qc, r0, r1)
    back = chip(back)
    (background,) = call(finish_kernel, [scal, near_u, back], [shape(rows, Z, H)], [])
    near_w, far_w = call(
        fifth_kernel, [scal, scat, scat_prior, force3, xr, cr, *coefs, *halo], [shape(B, Z, H)] * 2, [ext] * 3
    )
    (scattered,) = call(finish_kernel, [scal, near_w, chip(far_w)], [shape(rows, Z, H)], [])
    return background, scattered


def _split(values, count, n):
    return [*values[:count], values[count : count + n], values[count + n :]]


def solution(mesh):
    spec = P(("shot", "gx"), "section", "gy")
    assert mesh.shape["gy"] == 2
    return jax.shard_map(
        functools.partial(shards, mesh.shape["section"], mesh.shape["gx"]),
        mesh=mesh,
        in_specs=(spec,) * 5 + (P(None, ("shot", "gx"), "section", "gy"), P()),
        out_specs=(spec, spec),
        check_vma=False,
    )
```

```python
import functools

import jax
import jax.numpy as jnp
from jax import lax
from jax.experimental import pallas as pl
from jax.experimental.pallas import tpu as pltpu
from jax.sharding import PartitionSpec as P


NOFF = 17
MARGIN = 16
TILE = 8
F32 = jnp.float32
UNROLL = 4
SLACK = 8 << 20


class Geometry:
    def __init__(self, rows, depth, half, sections):
        self.B, self.Z, self.H, self.Y = rows // 2, depth, half, 2 * half
        self.two = sections == 2
        self.sides = 1 if self.two else 2
        self.ZE = depth + TILE * self.sides
        assert self.B >= MARGIN and depth % TILE == 0 and half % 128 == 0


def near_side(side, geo):
    first = (geo.B - 2) + side * (geo.B + 2)
    return first, first + 1 - side


def tile_mask(sender, depth, turn, width):
    place = lax.broadcasted_iota(jnp.int32, (TILE, width), 0)
    place = lax.rem(place + (TILE - turn), TILE)
    start = (1 - sender) * (TILE - depth)
    return (place >= start) & (place < start + depth)


def turned(value, turn):
    turn = turn % TILE
    return value if turn == 0 else pltpu.roll(value, turn, 0)


def senders(s, geo):
    return [s] if geo.two else [0, 1]


def receivers(s, geo):
    return [(geo.Z, 1 - s)] if geo.two else [(geo.ZE - TILE, 0), (geo.Z, 1)]


def edge_tile(ref, row, sender, geo):
    start = pl.multiple_of((1 - sender) * (geo.Z - TILE), TILE)
    return ref[row, pl.ds(start, TILE), :]


def pack_corner(items, row, sender, geo):
    out = jnp.zeros((TILE, geo.Y), F32)
    for ref, depth, turn in items:
        value = turned(edge_tile(ref, row, sender, geo), turn)
        out = jnp.where(tile_mask(sender, depth, turn, geo.Y), value, out)
    return out


def tiles_of(depths, geo):
    starts, total = [], 0
    for depth in depths:
        starts.append(total)
        total += geo.B * depth // TILE
    return starts, total


def pack_tiles(items, g, s, tiles, corners, geo):
    starts, _ = tiles_of([depth for _, depth, _ in items], geo)
    for sender, tile_ref, corner_ref in zip(senders(s, geo), tiles, corners):
        for (ref, depth, _), start in zip(items, starts):
            per = TILE // depth
            masks = [tile_mask(sender, depth, k * depth, geo.Y) for k in range(1, per)]
            for q in range(geo.B // per):
                out = edge_tile(ref, q * per, sender, geo)
                for k in range(1, per):
                    value = turned(edge_tile(ref, q * per + k, sender, geo), k * depth)
                    out = jnp.where(masks[k - 1], value, out)
                tile_ref[start + q] = out
        for k in range(corner_ref.shape[0]):
            row = g * (geo.B - corner_ref.shape[0]) + k
            corner_ref[k] = pack_corner(items, row, sender, geo)


def unpack_row(ref, start, x, depth, sender, geo):
    per = TILE // depth
    value = turned(ref[start + x // per], TILE - (x % per) * depth)
    return jnp.where(tile_mask(sender, depth, 0, geo.Y), value, 0.0)


def fill(dst, own, xrow, crow, tiles, xtiles, ctiles, start, depth, turn, g, s, geo):
    ends = list(zip(receivers(s, geo), tiles, xtiles, ctiles))

    def one(row, carry):
        dst[geo.B + row, 0 : geo.Z, :] = own[row]
        return carry

    lax.fori_loop(0, geo.B, one, 0, unroll=4)
    for (offset, sender), tile, _, _ in ends:
        for row in range(geo.B):
            dst[geo.B + row, offset : offset + TILE, :] = unpack_row(tile, start, row, depth, sender, geo)
    for side, get, is_x in ((g, xrow, True), (1 - g, crow, False)):
        first, nearest = near_side(side, geo)
        for k in range(depth):
            place = first + k if depth == 2 else nearest
            if get is not None:
                dst[place, 0 : geo.Z, :] = get(k)
            for (offset, sender), _, xtile, ctile in ends:
                if is_x:
                    index = k if depth == xtile.shape[0] else 1 - side
                    value = turned(xtile[index], TILE - turn)
                    value = jnp.where(tile_mask(sender, depth, 0, geo.Y), value, 0.0)
                else:
                    low = unpack_row(ctile, start, k, depth, sender, geo)
                    high = unpack_row(ctile, start, geo.B - depth + k, depth, sender, geo)
                    value = jnp.where(side == 1, low, high)
                dst[place, offset : offset + TILE, :] = value


def fill_blocks(dst, xblock, cblock, g, geo):
    def one(row, carry):
        dst[g * 2 * geo.B + row, 0 : geo.Z, :] = xblock[row]
        dst[(1 - g) * 2 * geo.B + row, 0 : geo.Z, :] = cblock[row]
        return carry

    lax.fori_loop(0, geo.B, one, 0)


def each(first, count, body, group):
    group = max(k for k in range(1, group + 1) if count % k == 0)

    def trip(index, carry):
        for k in range(group):
            body(first + index * group + k)
        return carry

    lax.fori_loop(0, count // group, trip, 0)


def advance(src, first, count, prior, extra, store, coefs, dif, tot, geo):
    xx, zz, yy, xz = coefs

    def rolls(row):
        value = src[row]
        above = pltpu.roll(value, geo.ZE - 1, 0)
        below = pltpu.roll(value, 1, 0)
        dif[row] = above - below
        tot[row] = above + below

    each(first - 1, count + 2, rolls, 6)
    lane = lax.broadcasted_iota(jnp.int32, (geo.ZE, geo.Y), 1)

    def one(row):
        at = row - (geo.B - 1)
        value = src[row]
        right = jnp.where(lane == geo.Y - 1, 0.0, pltpu.roll(value, geo.Y - 1, 1))
        left = jnp.where(lane == 0, 0.0, pltpu.roll(value, 1, 1))
        cx, cz, cy = xx[at], zz[at], yy[at]
        out = (2.0 - 2.0 * (cx + cz + cy)) * value - prior(row)
        out = out + cx * (src[row + 1] + src[row - 1]) + cz * tot[row] + cy * (right + left)
        out = out + xz[at] * (dif[row + 1] - dif[row - 1])
        if extra is not None:
            out = out + extra(row)
        store(row, out)

    each(first, count, one, UNROLL)


def make_source(ext, refl, refl_far, offsets, courant, out, g, geo):
    near = pl.multiple_of(g * geo.H, 128)
    far = pl.multiple_of((1 - g) * geo.H, 128)

    def one(row):
        acc = jnp.zeros((geo.Z, geo.H), F32)
        acc_far = jnp.zeros((geo.Z, geo.H), F32)
        for h in range(NOFF):
            place = geo.B + row + offsets[h]
            acc = acc + refl[h, row].astype(F32) * ext[place, 0 : geo.Z, pl.ds(near, geo.H)]
            acc_far = acc_far + refl_far[h, row] * ext[place, 0 : geo.Z, pl.ds(far, geo.H)]
        out[row, :, pl.ds(near, geo.H)] = courant[row, :, pl.ds(near, geo.H)] * acc
        out[row, :, pl.ds(far, geo.H)] = courant[row, :, pl.ds(far, geo.H)] * acc_far

    each(0, geo.B, one, 2)


def edge_rows(depth, side, geo):
    return side * (geo.B - depth)


def trig_products(angle):
    turns = jnp.floor(angle * 0.6366197723675814 + 0.5)
    rest = angle - turns * 1.5703125
    rest = rest - turns * 4.837512969970703125e-4
    rest = rest - turns * 7.549789954891882e-8
    odd = (turns - 2.0 * jnp.floor(turns * 0.5)) > 0.5
    square = rest * rest
    sine = rest + rest * square * (
        -1.6666654611e-1 + square * (8.3321608736e-3 + square * -1.9515295891e-4)
    )
    cosine = 1.0 - 0.5 * square + square * square * (
        4.166664568298827e-2 + square * (-1.388731625493765e-3 + square * 2.443315711809948e-5)
    )
    sine_square = jnp.where(odd, cosine * cosine, sine * sine)
    cosine_square = jnp.where(odd, sine * sine, cosine * cosine)
    product = sine * cosine
    return sine_square, cosine_square, jnp.where(odd, -product, product)


def half_kernel(geo, scal, *refs, other):
    *fields, out, sems = refs
    half = 1 - scal[0] if other else scal[0]
    start = pl.multiple_of(half * geo.B, TILE)
    copies = [
        pltpu.make_async_copy(field.at[pl.ds(start, geo.B)], out.at[k], sems.at[k]) for k, field in enumerate(fields)
    ]
    for copy in copies:
        copy.start()
    for copy in copies:
        copy.wait()


def widen_kernel(geo, scal, refl, near, out, held, sems):
    start = pl.multiple_of(scal[0] * geo.B, TILE)
    other = pl.multiple_of((1 - scal[0]) * geo.B, TILE)
    first = pltpu.make_async_copy(refl.at[:, pl.ds(other, geo.B)], held, sems.at[0])
    second = pltpu.make_async_copy(refl.at[:, pl.ds(start, geo.B)], near, sems.at[1])
    first.start()
    second.start()
    first.wait()

    def one(h, carry):
        for row in range(geo.B):
            out[h, row] = held[h, row].astype(F32)
        return carry

    lax.fori_loop(0, NOFF, one, 0)
    second.wait()


def join_kernel(geo, scal, *refs):
    near, far = refs[:2]
    own = refs[2:7]
    px, pc = refs[7:9]
    tiles, corners = refs[9 : 9 + geo.sides], refs[9 + geo.sides :]
    g, s = scal[0], scal[1]
    near_y = pl.multiple_of(g * geo.H, 128)
    far_y = pl.multiple_of((1 - g) * geo.H, 128)

    def one(row, carry):
        for k in range(5):
            own[k][row, :, pl.ds(near_y, geo.H)] = near[k, row]
            own[k][row, :, pl.ds(far_y, geo.H)] = far[k, row]
        return carry

    lax.fori_loop(0, geo.B, one, 0, unroll=2)
    for side, out in ((g, px), (1 - g, pc)):
        for k in range(2):
            out[k] = own[0][edge_rows(2, side, geo) + k]
        for k in range(1, 5):
            out[1 + k] = own[k][edge_rows(1, side, geo)]
    items = [(own[0], 2, 0)] + [(own[k], 1, 1 + k) for k in range(1, 5)]
    pack_tiles(items, g, s, tiles, corners, geo)


def first_kernel(geo, scal, *refs):
    n = geo.sides
    now, before, courant, aniso, tilt, xr, cr = refs[:7]
    tiles, xtiles, ctiles = refs[7 : 7 + n], refs[7 + n : 7 + 2 * n], refs[7 + 2 * n : 7 + 3 * n]
    out_block, prior_ext, xx, zz, yy, xz = refs[7 + 3 * n : 13 + 3 * n]
    out_tiles, out_corners = refs[13 + 3 * n : 13 + 4 * n], refs[13 + 4 * n : 13 + 5 * n]
    ext, old, dif, tot, mid, ca, cb, cc = refs[13 + 5 * n :]
    g, s = scal[0], scal[1]
    starts, _ = tiles_of([2, 1, 1, 1, 1], geo)
    for k, (dst, own) in enumerate(((old, before), (ca, courant), (cb, aniso), (cc, tilt)), 1):
        xrow, crow = (lambda _, k=k: xr[1 + k]), (lambda _, k=k: cr[1 + k])
        fill(dst, own, xrow, crow, tiles, xtiles, ctiles, starts[k], 1, 1 + k, g, s, geo)
    fill(ext, now, lambda k: xr[k], lambda k: cr[k], tiles, xtiles, ctiles, 0, 2, 0, g, s, geo)

    def coefficients(row, carry):
        at = row - (geo.B - 1)
        speed, stretch = ca[row], 2.0 * cb[row]
        sine_square, cosine_square, product = trig_products(cc[row])
        xx[at] = speed * (1.0 + stretch * cosine_square)
        zz[at] = speed * (1.0 + stretch * sine_square)
        yy[at] = speed * (1.0 + stretch)
        xz[at] = (0.5 * speed) * (stretch * product)
        return carry

    lax.fori_loop(geo.B - 1, 2 * geo.B + 1, coefficients, 0)
    two_steps(ext, mid, lambda row: old[row], prior_ext, out_block, (xx, zz, yy, xz), dif, tot, geo)
    pack_tiles([(out_block, 2, 0)], g, s, out_tiles, out_corners, geo)


def two_steps(ext, mid, prior, prior_ext, out_block, coefs, dif, tot, geo):
    def keep(row, value):
        mid[row] = value
        prior_ext[row - (geo.B - 1)] = value

    def keep_block(row, value):
        out_block[row - geo.B] = value[0 : geo.Z]

    advance(ext, geo.B - 1, geo.B + 2, prior, None, keep, coefs, dif, tot, geo)
    advance(mid, geo.B, geo.B, lambda row: ext[row], None, keep_block, coefs, dif, tot, geo)


def second_kernel(geo, scal, offsets, *refs):
    n = geo.sides
    now, before, xr, cr, courant, refl, refl_far, *coefs = refs[:11]
    tiles, xtiles, ctiles = refs[11 : 11 + n], refs[11 + n : 11 + 2 * n], refs[11 + 2 * n : 11 + 3 * n]
    px, pc, prior_ext, force = refs[11 + 3 * n : 15 + 3 * n]
    out_tiles, out_corners = refs[15 + 3 * n : 15 + 4 * n], refs[15 + 4 * n : 15 + 5 * n]
    ext, dif, tot, mid = refs[15 + 5 * n :]
    g, s = scal[0], scal[1]
    fill(ext, now, None, None, tiles, xtiles, ctiles, 0, 2, 0, g, s, geo)
    fill_blocks(ext, xr, cr, g, geo)
    two_steps(ext, mid, lambda row: before[row - (geo.B - 1)], prior_ext, px, coefs, dif, tot, geo)
    make_source(ext, refl, refl_far, offsets, courant, force, g, geo)

    def one(row, carry):
        pc[row] = px[row]
        return carry

    lax.fori_loop(0, geo.B, one, 0)
    for side, out in ((g, px), (1 - g, pc)):
        for k in range(2):
            out[geo.B + k] = force[edge_rows(2, side, geo) + k]
    pack_tiles([(px, 2, 0), (force, 2, 4)], g, s, out_tiles, out_corners, geo)


def third_kernel(geo, scal, offsets, *refs):
    n = geo.sides
    now, before, xr, cr, courant, refl, refl_far, *coefs = refs[:11]
    force = refs[11]
    tiles, xtiles, ctiles = refs[12 : 12 + n], refs[12 + n : 12 + 2 * n], refs[12 + 2 * n : 12 + 3 * n]
    px, pc, force_out, scat, scat_prior, near, back = refs[12 + 3 * n : 19 + 3 * n]
    out_tiles, out_corners = refs[19 + 3 * n : 19 + 4 * n], refs[19 + 4 * n : 19 + 5 * n]
    ext, dif, tot, mid, wave = refs[19 + 5 * n :]
    g, s = scal[0], scal[1]
    B = geo.B
    fill(ext, now, None, None, tiles, xtiles, ctiles, 0, 2, 0, g, s, geo)
    fill_blocks(ext, xr, cr, g, geo)

    def keep_mid(row, value):
        mid[row] = value

    def keep_block(row, value):
        value = value[0 : geo.Z]
        px[row - B] = value
        pc[row - B] = value
        low, high = value[:, 0 : geo.H], value[:, geo.H : geo.Y]
        near[row - B] = jnp.where(g == 0, low, high)
        back[row - B] = jnp.where(g == 0, high, low)

    advance(ext, B - 1, B + 2, lambda row: before[row - (B - 1)], None, keep_mid, coefs, dif, tot, geo)
    advance(mid, B, B, lambda row: ext[row], None, keep_block, coefs, dif, tot, geo)
    make_source(ext, refl, refl_far, offsets, courant, force_out, g, geo)
    start = tiles_of([2, 2], geo)[0][1]
    fill(wave, force, lambda k: xr[B + k], lambda k: cr[B + k], tiles, xtiles, ctiles, start, 2, 4, g, s, geo)

    def keep_wave(row, value):
        mid[row] = value
        scat_prior[row - (B - 1)] = value

    def keep_scat(row, value):
        scat[row - B] = value[0 : geo.Z] + force_out[row - B]

    advance(wave, B - 1, B + 2, lambda row: -wave[row], None, keep_wave, coefs, dif, tot, geo)
    advance(mid, B, B, lambda row: wave[row], None, keep_scat, coefs, dif, tot, geo)
    for side, out in ((g, px), (1 - g, pc)):
        for k in range(2):
            out[B + k] = scat[edge_rows(2, side, geo) + k]
        out[B + 2] = force_out[edge_rows(1, side, geo)]
    pack_tiles([(scat, 2, 0), (force_out, 1, 2)], g, s, out_tiles, out_corners, geo)


def fourth_kernel(geo, scal, offsets, *refs):
    n = geo.sides
    now, scat, before, xr, cr, courant, refl, refl_far, *coefs = refs[:12]
    force2 = refs[12]
    tiles, xtiles, ctiles = refs[13 : 13 + n], refs[13 + n : 13 + 2 * n], refs[13 + 2 * n : 13 + 3 * n]
    scat_out, scat_prior, force_out, px, pc = refs[13 + 3 * n : 18 + 3 * n]
    out_tiles, out_corners = refs[18 + 3 * n : 18 + 4 * n], refs[18 + 4 * n : 18 + 5 * n]
    ext, dif, tot, mid, wave = refs[18 + 5 * n :]
    g, s = scal[0], scal[1]
    B = geo.B

    def own(row, carry):
        ext[B + row, 0 : geo.Z, :] = now[row]
        return carry

    lax.fori_loop(0, B, own, 0)
    fill_blocks(ext, xr, cr, g, geo)
    make_source(ext, refl, refl_far, offsets, courant, force_out, g, geo)
    fill(wave, scat, lambda k: xr[B + k], lambda k: cr[B + k], tiles, xtiles, ctiles, 0, 2, 0, g, s, geo)
    start = tiles_of([2, 1], geo)[0][1]
    fill(ext, force2, lambda _: xr[B + 2], lambda _: cr[B + 2], tiles, xtiles, ctiles, start, 1, 2, g, s, geo)

    def keep_wave(row, value):
        mid[row] = value

    def keep_scat(row, value):
        scat_out[row - B] = value[0 : geo.Z] + force_out[row - B]
        scat_prior[row - B] = mid[row, 0 : geo.Z, :]

    advance(wave, B - 1, B + 2, lambda row: before[row - (B - 1)], lambda row: ext[row], keep_wave, coefs, dif, tot, geo)
    advance(mid, B, B, lambda row: wave[row], None, keep_scat, coefs, dif, tot, geo)
    px[0] = scat_out[edge_rows(1, g, geo)]
    pc[0] = scat_out[edge_rows(1, 1 - g, geo)]
    pack_tiles([(scat_out, 1, 0)], g, s, out_tiles, out_corners, geo)


def fifth_kernel(geo, scal, *refs):
    n = geo.sides
    scat, before, force, xr, cr, *coefs = refs[:9]
    tiles, xtiles, ctiles = refs[9 : 9 + n], refs[9 + n : 9 + 2 * n], refs[9 + 2 * n : 9 + 3 * n]
    out_near, out_far = refs[9 + 3 * n : 11 + 3 * n]
    ext, dif, tot = refs[11 + 3 * n :]
    g, s = scal[0], scal[1]
    B = geo.B
    fill(ext, scat, lambda _: xr[0], lambda _: cr[0], tiles, xtiles, ctiles, 0, 1, 0, g, s, geo)
    low, high = slice(0, geo.H), slice(geo.H, geo.Y)

    def keep(row, value):
        at = row - B
        value = value[0 : geo.Z] - before[at] + force[at]
        out_near[at] = jnp.where(g == 0, value[:, low], value[:, high])
        out_far[at] = jnp.where(g == 0, value[:, high], value[:, low])

    advance(ext, B, B, lambda row: 0.0, None, keep, coefs, dif, tot, geo)


def finish_kernel(geo, scal, near, far, out):
    g = scal[0]

    def one(row, carry):
        out[g * geo.B + row] = near[row]
        out[(1 - g) * geo.B + row] = far[row]
        return carry

    lax.fori_loop(0, geo.B, one, 0, unroll=4)


def shards(sections, gx, wave_now, wave_before, courant, anisotropy, tilt, reflectivity, offsets):
    rows, depth, half = wave_now.shape
    geo = Geometry(rows, depth, half, sections)
    B, Z, H, Y, ZE, n = geo.B, geo.Z, geo.H, geo.Y, geo.ZE, geo.sides
    g = lax.axis_index("gy")
    s = lax.axis_index("section")
    scal = jnp.stack([g, s]).astype(jnp.int32)
    swap = [(0, 1), (1, 0)]
    pairs_x = [p for i in range(gx - 1) for p in ((2 * i + 1, 2 * i + 2), (2 * i + 2, 2 * i + 1))]

    def z_moves():
        if geo.two:
            return [[(0, 1), (1, 0)]]
        return [[(i, i + 1) for i in range(sections - 1)], [(i + 1, i) for i in range(sections - 1)]]

    def corner_pairs(move):
        out = []
        for a, b in pairs_x:
            for i, j in move:
                out.append((((a // 2) * sections + i) * 2 + a % 2, ((b // 2) * sections + j) * 2 + b % 2))
        return out

    def chip(value):
        return lax.ppermute(value, "gy", swap)

    def exchange(px, pc, tiles, corners):
        xr = lax.ppermute(px, ("gx", "gy"), pairs_x)
        xz = [
            lax.ppermute(t, ("gx", "section", "gy"), corner_pairs(m)) for t, m in zip(corners, z_moves())
        ]
        zr = [lax.ppermute(t, "section", m) for t, m in zip(tiles, z_moves())]
        cr = chip(pc)
        cz = [chip(t) for t in zr]
        return xr, cr, [*zr, *xz, *cz]

    def shape(*dims):
        return jax.ShapeDtypeStruct(dims, F32)

    def call(kernel, inputs, outs, scratch, smem=1, specs=None, extra=()):
        if specs is None:
            specs = [pl.BlockSpec(memory_space=pltpu.SMEM)] * (smem - 1)
            specs += [pl.BlockSpec(memory_space=pltpu.VMEM)] * (len(inputs) - smem)
        used = sum(4 * d[0] * d[1] * d[2] for d in scratch)
        return pl.pallas_call(
            functools.partial(kernel, geo),
            out_shape=outs,
            grid_spec=pltpu.PrefetchScalarGridSpec(
                num_scalar_prefetch=1,
                grid=(1,),
                in_specs=specs,
                out_specs=[pl.BlockSpec(memory_space=pltpu.VMEM)] * len(outs),
                scratch_shapes=[*(pltpu.VMEM(d, F32) for d in scratch), *extra],
            ),
            compiler_params=pltpu.CompilerParams(vmem_limit_bytes=used + SLACK),
        )(*inputs)

    block, wide, ext = (B, Z, Y), (B + 2, ZE, Y), (3 * B, ZE, Y)

    def tile_outs(depths, corner=2):
        return [shape(tiles_of(depths, geo)[1], TILE, Y)] * n + [shape(corner, TILE, Y)] * n

    in_hbm = lambda value: pltpu.with_memory_space_constraint(value, pltpu.HBM)
    fields = [in_hbm(f) for f in (wave_now, wave_before, courant, anisotropy, tilt)]
    reflectivity = in_hbm(reflectivity)
    hbm = pl.BlockSpec(memory_space=pltpu.HBM)

    def half_of(other):
        kernel = functools.partial(half_kernel, other=other)
        copies = [pltpu.SemaphoreType.DMA((5,))]
        (out,) = call(kernel, [scal, *fields], [shape(5, B, Z, H)], [], specs=[hbm] * 5, extra=copies)
        return out

    far = chip(half_of(True))
    near = half_of(False)
    *own, px, pc, r0, r1 = _split(
        call(
            join_kernel,
            [scal, near, far],
            [shape(*block)] * 5 + [shape(6, Z, Y)] * 2 + tile_outs([2, 1, 1, 1, 1]),
            [],
        ),
        7,
        n,
    )
    xr, cr, halo = exchange(px, pc, r0, r1)
    refl, refl_far = call(
        widen_kernel,
        [scal, reflectivity],
        [jax.ShapeDtypeStruct((NOFF, B, Z, H), reflectivity.dtype), shape(NOFF, B, Z, H)],
        [],
        specs=[hbm],
        extra=[pltpu.VMEM((NOFF, B, Z, H), reflectivity.dtype), pltpu.SemaphoreType.DMA((2,))],
    )
    refl_far = chip(refl_far)
    now, prior, *coefs, r0, r1 = _split(
        call(
            first_kernel, [scal, *own, xr, cr, *halo], [shape(*block)] + [shape(*wide)] * 5 + tile_outs([2]), [ext] * 8
        ),
        6,
        n,
    )
    xr, cr, halo = exchange(now, now, r0, r1)
    px, pc, prior, force, r0, r1 = _split(
        call(
            second_kernel,
            [scal, offsets, now, prior, xr, cr, own[2], refl, refl_far, *coefs, *halo],
            [shape(B + 2, Z, Y)] * 2 + [shape(*wide), shape(*block)] + tile_outs([2, 2]),
            [ext] * 4,
            2,
        ),
        4,
        n,
    )
    xr, cr, halo = exchange(px, pc, r0, r1)
    px, pc, force2, scat, scat_prior, near_u, back, r0, r1 = _split(
        call(
            third_kernel,
            [scal, offsets, px, prior, xr, cr, own[2], refl, refl_far, *coefs, force, *halo],
            [shape(B + 3, Z, Y)] * 2
            + [shape(*block)] * 2
            + [shape(*wide)]
            + [shape(B, Z, H)] * 2
            + tile_outs([2, 1]),
            [ext] * 5,
            2,
        ),
        7,
        n,
    )
    xr, cr, halo = exchange(px, pc, r0, r1)
    scat, scat_prior, force3, qx, qc, r0, r1 = _split(
        call(
            fourth_kernel,
            [scal, offsets, px, scat, scat_prior, xr, cr, own[2], refl, refl_far, *coefs, force2, *halo],
            [shape(*block)] * 3 + [shape(1, Z, Y)] * 2 + tile_outs([1], 1),
            [ext] * 5,
            2,
        ),
        5,
        n,
    )
    xr, cr, halo = exchange(qx, qc, r0, r1)
    back = chip(back)
    (background,) = call(finish_kernel, [scal, near_u, back], [shape(rows, Z, H)], [])
    near_w, far_w = call(
        fifth_kernel, [scal, scat, scat_prior, force3, xr, cr, *coefs, *halo], [shape(B, Z, H)] * 2, [ext] * 3
    )
    (scattered,) = call(finish_kernel, [scal, near_w, chip(far_w)], [shape(rows, Z, H)], [])
    return background, scattered


def _split(values, count, n):
    return [*values[:count], values[count : count + n], values[count + n :]]


def solution(mesh):
    spec = P(("shot", "gx"), "section", "gy")
    assert mesh.shape["gy"] == 2
    return jax.shard_map(
        functools.partial(shards, mesh.shape["section"], mesh.shape["gx"]),
        mesh=mesh,
        in_specs=(spec,) * 5 + (P(None, ("shot", "gx"), "section", "gy"), P()),
        out_specs=(spec, spec),
        check_vma=False,
    )
```

```python
import functools

import jax
import jax.numpy as jnp
from jax import lax
from jax.experimental import pallas as pl
from jax.experimental.pallas import tpu as pltpu
from jax.sharding import PartitionSpec as P


NOFF = 17
MARGIN = 16
TILE = 8
F32 = jnp.float32
UNROLL = 8
SLACK = 8 << 20


class Geometry:
    def __init__(self, rows, depth, half, sections):
        self.B, self.Z, self.H, self.Y = rows // 2, depth, half, 2 * half
        self.two = sections == 2
        self.sides = 1 if self.two else 2
        self.ZE = depth + TILE * self.sides
        assert self.B >= MARGIN and depth % TILE == 0 and half % 128 == 0


def near_side(side, geo):
    first = (geo.B - 2) + side * (geo.B + 2)
    return first, first + 1 - side


def tile_mask(sender, depth, turn, width):
    place = lax.broadcasted_iota(jnp.int32, (TILE, width), 0)
    place = lax.rem(place + (TILE - turn), TILE)
    start = (1 - sender) * (TILE - depth)
    return (place >= start) & (place < start + depth)


def turned(value, turn):
    turn = turn % TILE
    return value if turn == 0 else pltpu.roll(value, turn, 0)


def senders(s, geo):
    return [s] if geo.two else [0, 1]


def receivers(s, geo):
    return [(geo.Z, 1 - s)] if geo.two else [(geo.ZE - TILE, 0), (geo.Z, 1)]


def edge_tile(ref, row, sender, geo):
    start = pl.multiple_of((1 - sender) * (geo.Z - TILE), TILE)
    return ref[row, pl.ds(start, TILE), :]


def pack_corner(items, row, sender, geo):
    out = jnp.zeros((TILE, geo.Y), F32)
    for ref, depth, turn in items:
        value = turned(edge_tile(ref, row, sender, geo), turn)
        out = jnp.where(tile_mask(sender, depth, turn, geo.Y), value, out)
    return out


def tiles_of(depths, geo):
    starts, total = [], 0
    for depth in depths:
        starts.append(total)
        total += geo.B * depth // TILE
    return starts, total


def pack_tiles(items, g, s, tiles, corners, geo):
    starts, _ = tiles_of([depth for _, depth, _ in items], geo)
    for sender, tile_ref, corner_ref in zip(senders(s, geo), tiles, corners):
        for (ref, depth, _), start in zip(items, starts):
            per = TILE // depth
            masks = [tile_mask(sender, depth, k * depth, geo.Y) for k in range(1, per)]
            for q in range(geo.B // per):
                out = edge_tile(ref, q * per, sender, geo)
                for k in range(1, per):
                    value = turned(edge_tile(ref, q * per + k, sender, geo), k * depth)
                    out = jnp.where(masks[k - 1], value, out)
                tile_ref[start + q] = out
        for k in range(corner_ref.shape[0]):
            row = g * (geo.B - corner_ref.shape[0]) + k
            corner_ref[k] = pack_corner(items, row, sender, geo)


def unpack_row(ref, start, x, depth, sender, geo):
    per = TILE // depth
    value = turned(ref[start + x // per], TILE - (x % per) * depth)
    return jnp.where(tile_mask(sender, depth, 0, geo.Y), value, 0.0)


def fill(dst, own, xrow, crow, tiles, xtiles, ctiles, start, depth, turn, g, s, geo):
    ends = list(zip(receivers(s, geo), tiles, xtiles, ctiles))

    def one(row, carry):
        dst[geo.B + row, 0 : geo.Z, :] = own[row]
        return carry

    lax.fori_loop(0, geo.B, one, 0, unroll=4)
    for (offset, sender), tile, _, _ in ends:
        for row in range(geo.B):
            dst[geo.B + row, offset : offset + TILE, :] = unpack_row(tile, start, row, depth, sender, geo)
    for side, get, is_x in ((g, xrow, True), (1 - g, crow, False)):
        first, nearest = near_side(side, geo)
        for k in range(depth):
            place = first + k if depth == 2 else nearest
            if get is not None:
                dst[place, 0 : geo.Z, :] = get(k)
            for (offset, sender), _, xtile, ctile in ends:
                if is_x:
                    index = k if depth == xtile.shape[0] else 1 - side
                    value = turned(xtile[index], TILE - turn)
                    value = jnp.where(tile_mask(sender, depth, 0, geo.Y), value, 0.0)
                else:
                    low = unpack_row(ctile, start, k, depth, sender, geo)
                    high = unpack_row(ctile, start, geo.B - depth + k, depth, sender, geo)
                    value = jnp.where(side == 1, low, high)
                dst[place, offset : offset + TILE, :] = value


def fill_blocks(dst, xblock, cblock, g, geo, own=None):
    def one(row, carry):
        dst[g * 2 * geo.B + row, 0 : geo.Z, :] = xblock[row]
        dst[(1 - g) * 2 * geo.B + row, 0 : geo.Z, :] = cblock[row]
        if own is not None:
            dst[geo.B + row, 0 : geo.Z, :] = own[row]
        return carry

    lax.fori_loop(0, geo.B, one, 0, unroll=2)


def each(first, count, body, group):
    group = max(k for k in range(1, group + 1) if count % k == 0)

    def trip(index, carry):
        for k in range(group):
            body(first + index * group + k)
        return carry

    lax.fori_loop(0, count // group, trip, 0)


def advance(src, off, first, count, top, prior, extra, store, coefs, dif, tot, geo, group=None):
    xx, zz, yy, xz, mid = coefs
    lane = lax.broadcasted_iota(jnp.int32, (top, 128), 1)
    low_edge, high_edge = lane == 0, lane == 127
    spans = [slice(k, k + 128) for k in range(0, geo.Y, 128)]

    def slopes(row):
        value = src[row - off]
        above = pltpu.roll(value, geo.ZE - 1, 0)[0:top]
        below = pltpu.roll(value, 1, 0)[0:top]
        dif[row, 0:top] = above - below
        return value[0:top], above + below

    def local(row):
        at = jnp.minimum(row - (geo.B - 1), geo.B + 1)
        whole, total = slopes(row)
        value = [whole[:, span] for span in spans]
        zero = jnp.zeros_like(value[0])
        right = [pltpu.roll(v, 127, 1) for v in value] + [zero]
        left = [zero] + [pltpu.roll(v, 1, 1) for v in value]
        for k, span in enumerate(spans):
            side = jnp.where(high_edge, right[k + 1], right[k]) + jnp.where(low_edge, left[k], left[k + 1])
            new = mid[at, 0:top, span] * value[k] + zz[at, 0:top, span] * total[:, span]
            tot[row, 0:top, span] = new + yy[at, 0:top, span] * side

    slopes(first - 1)
    local(first)

    def one(row):
        local(row + 1)
        at = row - (geo.B - 1)
        new = tot[row, 0:top] + xx[at, 0:top] * (src[row + 1 - off, 0:top] + src[row - 1 - off, 0:top])
        new = new + xz[at, 0:top] * (dif[row + 1, 0:top] - dif[row - 1, 0:top])
        last = prior(row)
        if last is not None:
            new = new - last[0:top]
        if extra is not None:
            new = new + extra(row)[0:top]
        store(row, new)

    each(first, count, one, group or UNROLL)


def make_source(ext, refl, refl_far, offsets, courant, out, g, geo):
    near = pl.multiple_of(g * geo.H, 128)
    far = pl.multiple_of((1 - g) * geo.H, 128)

    def one(row):
        acc = jnp.zeros((geo.Z, geo.H), F32)
        acc_far = jnp.zeros((geo.Z, geo.H), F32)
        for h in range(NOFF):
            place = geo.B + row + offsets[h]
            acc = acc + refl[h, row].astype(F32) * ext[place, 0 : geo.Z, pl.ds(near, geo.H)]
            acc_far = acc_far + refl_far[h, row] * ext[place, 0 : geo.Z, pl.ds(far, geo.H)]
        out[row, :, pl.ds(near, geo.H)] = courant[row, :, pl.ds(near, geo.H)] * acc
        out[row, :, pl.ds(far, geo.H)] = courant[row, :, pl.ds(far, geo.H)] * acc_far

    each(0, geo.B, one, 2)


def edge_rows(depth, side, geo):
    return side * (geo.B - depth)


def trig_products(angle):
    turns = jnp.floor(angle * 0.6366197723675814 + 0.5)
    rest = angle - turns * 1.5703125
    rest = rest - turns * 4.837512969970703125e-4
    rest = rest - turns * 7.549789954891882e-8
    odd = (turns - 2.0 * jnp.floor(turns * 0.5)) > 0.5
    square = rest * rest
    sine = rest + rest * square * (
        -1.6666654611e-1 + square * (8.3321608736e-3 + square * -1.9515295891e-4)
    )
    cosine = 1.0 - 0.5 * square + square * square * (
        4.166664568298827e-2 + square * (-1.388731625493765e-3 + square * 2.443315711809948e-5)
    )
    sine_square = jnp.where(odd, cosine * cosine, sine * sine)
    cosine_square = jnp.where(odd, sine * sine, cosine * cosine)
    product = sine * cosine
    return sine_square, cosine_square, jnp.where(odd, -product, product)


def half_kernel(geo, scal, *refs, other):
    *fields, out, sems = refs
    half = 1 - scal[0] if other else scal[0]
    start = pl.multiple_of(half * geo.B, TILE)
    copies = [
        pltpu.make_async_copy(field.at[pl.ds(start, geo.B)], out.at[k], sems.at[k]) for k, field in enumerate(fields)
    ]
    for copy in copies:
        copy.start()
    for copy in copies:
        copy.wait()


def widen_kernel(geo, scal, refl, out, held, sems):
    other = pl.multiple_of((1 - scal[0]) * geo.B, TILE)
    cuts = [0, 5, 9, 13, NOFF]
    copies = [
        pltpu.make_async_copy(refl.at[pl.ds(a, b - a), pl.ds(other, geo.B)], held.at[pl.ds(a, b - a)], sems.at[k])
        for k, (a, b) in enumerate(zip(cuts, cuts[1:]))
    ]
    for copy in copies:
        copy.start()
    for copy, a, b in zip(copies, cuts, cuts[1:]):
        copy.wait()

        def one(h, carry):
            for row in range(geo.B):
                out[h, row] = held[h, row].astype(F32)
            return carry

        lax.fori_loop(a, b, one, 0)


def own_refl_kernel(geo, scal, refl, out, sem):
    start = pl.multiple_of(scal[0] * geo.B, TILE)
    copy = pltpu.make_async_copy(refl.at[:, pl.ds(start, geo.B)], out, sem)
    copy.start()
    copy.wait()


def join_kernel(geo, scal, *refs):
    near, far = refs[:2]
    own = refs[2:7]
    px, pc = refs[7:9]
    tiles, corners = refs[9 : 9 + geo.sides], refs[9 + geo.sides :]
    g, s = scal[0], scal[1]
    near_y = pl.multiple_of(g * geo.H, 128)
    far_y = pl.multiple_of((1 - g) * geo.H, 128)

    def one(row, carry):
        for k in range(5):
            own[k][row, :, pl.ds(near_y, geo.H)] = near[k, row]
            own[k][row, :, pl.ds(far_y, geo.H)] = far[k, row]
        return carry

    lax.fori_loop(0, geo.B, one, 0, unroll=2)
    for side, out in ((g, px), (1 - g, pc)):
        for k in range(2):
            out[k] = own[0][edge_rows(2, side, geo) + k]
        for k in range(1, 5):
            out[1 + k] = own[k][edge_rows(1, side, geo)]
    items = [(own[0], 2, 0)] + [(own[k], 1, 1 + k) for k in range(1, 5)]
    pack_tiles(items, g, s, tiles, corners, geo)


def coefficients(speed, aniso, angle):
    stretch = 2.0 * aniso
    sine_square, cosine_square, product = trig_products(angle)
    cx = speed * (1.0 + stretch * cosine_square)
    cz = speed * (1.0 + stretch * sine_square)
    cy = speed * (1.0 + stretch)
    return cx, cz, cy, (0.5 * speed) * (stretch * product), 2.0 - 2.0 * (cx + cz + cy)


def coef_kernel(geo, scal, courant, aniso, tilt, *coefs):
    def one(row):
        for ref, value in zip(coefs, coefficients(courant[row], aniso[row], tilt[row])):
            ref[row + 1, 0 : geo.Z, :] = value

    each(0, geo.B, one, 2)


def coef_halo(coefs, xr, cr, tiles, xtiles, ctiles, starts, g, s, geo):
    ends = list(zip(receivers(s, geo), tiles, xtiles, ctiles))
    for (offset, sender), tile, _, _ in ends:
        keep = tile_mask(sender, 1, 0, geo.Y)
        for q in range(geo.B // TILE):
            values = coefficients(*(tile[start + q] for start in starts))
            for k in range(TILE):
                for ref, value in zip(coefs, values):
                    place = (q * TILE + k + 1, slice(offset, offset + TILE))
                    ref[place] = jnp.where(keep, turned(value, TILE - k), 0.0)
    for side, line, is_x in ((g, xr, True), (1 - g, cr, False)):
        at = side * (geo.B + 1)
        for ref, value in zip(coefs, coefficients(line[3], line[4], line[5])):
            ref[at, 0 : geo.Z, :] = value
        for (offset, sender), _, xtile, ctile in ends:
            if is_x:
                fields = [turned(xtile[1 - side], TILE - turn) for turn in (3, 4, 5)]
            else:
                fields = [
                    jnp.where(
                        side == 1,
                        unpack_row(ctile, start, 0, 1, sender, geo),
                        unpack_row(ctile, start, geo.B - 1, 1, sender, geo),
                    )
                    for start in starts
                ]
            keep = tile_mask(sender, 1, 0, geo.Y)
            for ref, value in zip(coefs, coefficients(*fields)):
                ref[at, offset : offset + TILE, :] = jnp.where(keep, value, 0.0)


def first_kernel(geo, scal, *refs):
    n = geo.sides
    now, before, xr, cr = refs[:4]
    tiles, xtiles, ctiles = refs[4 : 4 + n], refs[4 + n : 4 + 2 * n], refs[4 + 2 * n : 4 + 3 * n]
    out_block, prior_ext, *coefs = refs[9 + 3 * n : 16 + 3 * n]
    out_tiles, out_corners = refs[16 + 3 * n : 16 + 4 * n], refs[16 + 4 * n : 16 + 5 * n]
    ext, old, dif, tot = refs[16 + 5 * n :]
    g, s = scal[0], scal[1]
    starts, _ = tiles_of([2, 1, 1, 1, 1], geo)
    coef_halo(coefs, xr, cr, tiles, xtiles, ctiles, starts[2:], g, s, geo)
    fill(old, before, lambda _: xr[2], lambda _: cr[2], tiles, xtiles, ctiles, starts[1], 1, 2, g, s, geo)
    fill(ext, now, lambda k: xr[k], lambda k: cr[k], tiles, xtiles, ctiles, 0, 2, 0, g, s, geo)

    def keep_block(row, value):
        out_block[row - geo.B] = value[0 : geo.Z]

    two_steps(ext, lambda row: old[row], prior_ext, keep_block, coefs, dif, tot, geo)
    pack_tiles([(out_block, 2, 0)], g, s, out_tiles, out_corners, geo)


def two_steps(ext, prior, mid, store, coefs, dif, tot, geo):
    off = geo.B - 1

    def keep(row, value):
        mid[row - off] = value

    advance(ext, 0, off, geo.B + 2, geo.ZE, prior, None, keep, coefs, dif, tot, geo)
    advance(mid, off, geo.B, geo.B, geo.Z, lambda row: ext[row], None, store, coefs, dif, tot, geo)


def second_kernel(geo, scal, offsets, *refs):
    n = geo.sides
    now, before, xr, cr, courant, refl, refl_far, *coefs = refs[:12]
    tiles, xtiles, ctiles = refs[12 : 12 + n], refs[12 + n : 12 + 2 * n], refs[12 + 2 * n : 12 + 3 * n]
    px, pc, prior_ext, force = refs[12 + 3 * n : 16 + 3 * n]
    out_tiles, out_corners = refs[16 + 3 * n : 16 + 4 * n], refs[16 + 4 * n : 16 + 5 * n]
    ext, dif, tot = refs[16 + 5 * n :]
    g, s = scal[0], scal[1]
    B = geo.B
    fill_blocks(ext, xr, cr, g, geo)
    fill(ext, now, None, None, tiles, xtiles, ctiles, 0, 2, 0, g, s, geo)

    def keep_block(row, value):
        px[row - B] = value[0 : geo.Z]
        pc[row - B] = value[0 : geo.Z]

    two_steps(ext, lambda row: before[row - (B - 1)], prior_ext, keep_block, coefs, dif, tot, geo)
    make_source(ext, refl, refl_far, offsets, courant, force, g, geo)
    for side, out in ((g, px), (1 - g, pc)):
        for k in range(2):
            out[B + k] = force[edge_rows(2, side, geo) + k]
    pack_tiles([(px, 2, 0), (force, 2, 4)], g, s, out_tiles, out_corners, geo)


def third_kernel(geo, scal, *refs):
    n = geo.sides
    now, before, xr, cr, *coefs = refs[:9]
    tiles, xtiles, ctiles = refs[9 : 9 + n], refs[9 + n : 9 + 2 * n], refs[9 + 2 * n : 9 + 3 * n]
    block, near, back = refs[9 + 3 * n : 12 + 3 * n]
    ext, dif, tot, mid = refs[12 + 3 * n :]
    g, s = scal[0], scal[1]
    B = geo.B
    fill(ext, now, lambda k: xr[near_row(g, k, geo)], lambda k: cr[near_row(1 - g, k, geo)], tiles, xtiles, ctiles, 0, 2, 0, g, s, geo)

    def keep_block(row, value):
        value = value[0 : geo.Z]
        block[row - B] = value
        low, high = value[:, 0 : geo.H], value[:, geo.H : geo.Y]
        near[row - B] = jnp.where(g == 0, low, high)
        back[row - B] = jnp.where(g == 0, high, low)

    two_steps(ext, lambda row: before[row - (B - 1)], mid, keep_block, coefs, dif, tot, geo)


def near_row(side, k, geo):
    return (1 - side) * (geo.B - 2) + k


def scatter_kernel(geo, scal, offsets, *refs):
    n = geo.sides
    now, xr, cr, courant, refl, refl_far, *coefs = refs[:11]
    force = refs[11]
    tiles, xtiles, ctiles = refs[12 : 12 + n], refs[12 + n : 12 + 2 * n], refs[12 + 2 * n : 12 + 3 * n]
    px, pc, force_out, scat, scat_prior = refs[12 + 3 * n : 17 + 3 * n]
    out_tiles, out_corners = refs[17 + 3 * n : 17 + 4 * n], refs[17 + 4 * n : 17 + 5 * n]
    ext, dif, tot, wave = refs[17 + 5 * n :]
    g, s = scal[0], scal[1]
    B = geo.B
    fill_blocks(ext, xr, cr, g, geo, now)
    make_source(ext, refl, refl_far, offsets, courant, force_out, g, geo)
    start = tiles_of([2, 2], geo)[0][1]
    fill(wave, force, lambda k: xr[B + k], lambda k: cr[B + k], tiles, xtiles, ctiles, start, 2, 4, g, s, geo)

    def keep_scat(row, value):
        scat[row - B] = value[0 : geo.Z] + force_out[row - B]

    two_steps(wave, lambda row: -wave[row], scat_prior, keep_scat, coefs, dif, tot, geo)
    for side, out in ((g, px), (1 - g, pc)):
        for k in range(2):
            out[k] = scat[edge_rows(2, side, geo) + k]
        out[2] = force_out[edge_rows(1, side, geo)]
    pack_tiles([(scat, 2, 0), (force_out, 1, 2)], g, s, out_tiles, out_corners, geo)


def source_kernel(geo, scal, offsets, now, xr, cr, courant, refl, refl_far, force, ext):
    g = scal[0]
    fill_blocks(ext, xr, cr, g, geo, now)
    make_source(ext, refl, refl_far, offsets, courant, force, g, geo)


def fourth_kernel(geo, scal, *refs):
    n = geo.sides
    scat, before, xr, cr, force2, force3, *coefs = refs[:11]
    tiles, xtiles, ctiles = refs[11 : 11 + n], refs[11 + n : 11 + 2 * n], refs[11 + 2 * n : 11 + 3 * n]
    scat_out, scat_prior, px, pc = refs[11 + 3 * n : 15 + 3 * n]
    out_tiles, out_corners = refs[15 + 3 * n : 15 + 4 * n], refs[15 + 4 * n : 15 + 5 * n]
    wave, extra, dif, tot, mid = refs[15 + 5 * n :]
    g, s = scal[0], scal[1]
    B = geo.B
    fill(wave, scat, lambda k: xr[k], lambda k: cr[k], tiles, xtiles, ctiles, 0, 2, 0, g, s, geo)
    start = tiles_of([2, 1], geo)[0][1]
    fill(extra, force2, lambda _: xr[2], lambda _: cr[2], tiles, xtiles, ctiles, start, 1, 2, g, s, geo)

    def keep_wave(row, value):
        mid[row - (B - 1)] = value

    def keep_scat(row, value):
        scat_out[row - B] = value[0 : geo.Z] + force3[row - B]
        scat_prior[row - B] = mid[row - (B - 1), 0 : geo.Z, :]

    advance(wave, 0, B - 1, B + 2, geo.ZE, lambda row: before[row - (B - 1)], lambda row: extra[row], keep_wave, coefs, dif, tot, geo)
    advance(mid, B - 1, B, B, geo.Z, lambda row: wave[row], None, keep_scat, coefs, dif, tot, geo)
    px[0] = scat_out[edge_rows(1, g, geo)]
    pc[0] = scat_out[edge_rows(1, 1 - g, geo)]
    pack_tiles([(scat_out, 1, 0)], g, s, out_tiles, out_corners, geo)


def fifth_kernel(geo, scal, *refs):
    n = geo.sides
    scat, before, force, xr, cr, *coefs = refs[:10]
    tiles, xtiles, ctiles = refs[10 : 10 + n], refs[10 + n : 10 + 2 * n], refs[10 + 2 * n : 10 + 3 * n]
    out_near, out_far = refs[10 + 3 * n : 12 + 3 * n]
    ext, dif, tot = refs[12 + 3 * n :]
    g, s = scal[0], scal[1]
    B = geo.B
    fill(ext, scat, lambda _: xr[0], lambda _: cr[0], tiles, xtiles, ctiles, 0, 1, 0, g, s, geo)
    low, high = slice(0, geo.H), slice(geo.H, geo.Y)

    def keep(row, value):
        at = row - B
        value = value[0 : geo.Z] - before[at] + force[at]
        out_near[at] = jnp.where(g == 0, value[:, low], value[:, high])
        out_far[at] = jnp.where(g == 0, value[:, high], value[:, low])

    advance(ext, 0, B, B, geo.Z, lambda row: None, None, keep, coefs, dif, tot, geo, 16)


def finish_kernel(geo, scal, near, far, out):
    g = scal[0]

    def one(row, carry):
        out[g * geo.B + row] = near[row]
        out[(1 - g) * geo.B + row] = far[row]
        return carry

    lax.fori_loop(0, geo.B, one, 0, unroll=4)


def place_kernel(geo, scal, *refs, other):
    half, out, sem = refs[0], refs[-2], refs[-1]
    start = pl.multiple_of((1 - scal[0] if other else scal[0]) * geo.B, TILE)
    copy = pltpu.make_async_copy(half, out.at[pl.ds(start, geo.B)], sem)
    copy.start()
    copy.wait()


def shards(sections, gx, wave_now, wave_before, courant, anisotropy, tilt, reflectivity, offsets):
    rows, depth, half = wave_now.shape
    geo = Geometry(rows, depth, half, sections)
    B, Z, H, Y, ZE, n = geo.B, geo.Z, geo.H, geo.Y, geo.ZE, geo.sides
    g = lax.axis_index("gy")
    s = lax.axis_index("section")
    scal = jnp.stack([g, s]).astype(jnp.int32)
    swap = [(0, 1), (1, 0)]
    pairs_x = [p for i in range(gx - 1) for p in ((2 * i + 1, 2 * i + 2), (2 * i + 2, 2 * i + 1))]

    def z_moves():
        if geo.two:
            return [[(0, 1), (1, 0)]]
        return [[(i, i + 1) for i in range(sections - 1)], [(i + 1, i) for i in range(sections - 1)]]

    def corner_pairs(move):
        out = []
        for a, b in pairs_x:
            for i, j in move:
                out.append((((a // 2) * sections + i) * 2 + a % 2, ((b // 2) * sections + j) * 2 + b % 2))
        return out

    def chip(value):
        return lax.ppermute(value, "gy", swap)

    def exchange(px, pc, tiles, corners):
        xr = lax.ppermute(px, ("gx", "gy"), pairs_x)
        xz = [
            lax.ppermute(t, ("gx", "section", "gy"), corner_pairs(m)) for t, m in zip(corners, z_moves())
        ]
        zr = [lax.ppermute(t, "section", m) for t, m in zip(tiles, z_moves())]
        cr = chip(pc)
        cz = [chip(t) for t in zr]
        return xr, cr, [*zr, *xz, *cz]

    def shape(*dims):
        return jax.ShapeDtypeStruct(dims, F32)

    def call(kernel, inputs, outs, scratch, smem=1, specs=None, extra=(), aliases=None, out_specs=None):
        if specs is None:
            specs = [pl.BlockSpec(memory_space=pltpu.SMEM)] * (smem - 1)
            specs += [pl.BlockSpec(memory_space=pltpu.VMEM)] * (len(inputs) - smem)
        used = sum(4 * d[0] * d[1] * d[2] for d in scratch)
        return pl.pallas_call(
            functools.partial(kernel, geo),
            out_shape=outs,
            grid_spec=pltpu.PrefetchScalarGridSpec(
                num_scalar_prefetch=1,
                grid=(1,),
                in_specs=specs,
                out_specs=out_specs or [pl.BlockSpec(memory_space=pltpu.VMEM)] * len(outs),
                scratch_shapes=[*(pltpu.VMEM(d, F32) for d in scratch), *extra],
            ),
            input_output_aliases=aliases or {},
            compiler_params=pltpu.CompilerParams(vmem_limit_bytes=used + SLACK),
        )(*inputs)

    block, wide, ext = (B, Z, Y), (B + 2, ZE, Y), (3 * B, ZE, Y)

    def tile_outs(depths, corner=2):
        return [shape(tiles_of(depths, geo)[1], TILE, Y)] * n + [shape(corner, TILE, Y)] * n

    in_hbm = lambda value: pltpu.with_memory_space_constraint(value, pltpu.HBM)
    fields = [in_hbm(f) for f in (wave_now, wave_before, courant, anisotropy, tilt)]
    reflectivity = in_hbm(reflectivity)
    hbm = pl.BlockSpec(memory_space=pltpu.HBM)
    whole = pl.BlockSpec(memory_space=pltpu.VMEM)

    def half_of(other):
        kernel = functools.partial(half_kernel, other=other)
        copies = [pltpu.SemaphoreType.DMA((5,))]
        (out,) = call(kernel, [scal, *fields], [shape(5, B, Z, H)], [], specs=[hbm] * 5, extra=copies)
        return out

    far = chip(half_of(True))
    near = half_of(False)
    *own, px, pc, r0, r1 = _split(
        call(
            join_kernel,
            [scal, near, far],
            [shape(*block)] * 5 + [shape(6, Z, Y)] * 2 + tile_outs([2, 1, 1, 1, 1]),
            [],
        ),
        7,
        n,
    )
    xr, cr, halo = exchange(px, pc, r0, r1)
    (refl_far,) = call(
        widen_kernel,
        [scal, reflectivity],
        [shape(NOFF, B, Z, H)],
        [],
        specs=[hbm],
        extra=[pltpu.VMEM((NOFF, B, Z, H), reflectivity.dtype), pltpu.SemaphoreType.DMA((4,))],
    )
    refl_far = chip(refl_far)
    coefs = call(coef_kernel, [scal, *own[2:]], [shape(*wide)] * 5, [])
    inputs = [scal, *own[:2], xr, cr, *halo, *coefs]
    first = len(inputs) - 5
    now, prior, *coefs, r0, r1 = _split(
        call(
            first_kernel,
            inputs,
            [shape(*block)] + [shape(*wide)] * 6 + tile_outs([2]),
            [ext] * 4,
            aliases={first + k: 2 + k for k in range(5)},
        ),
        7,
        n,
    )
    courant_own = own[2]
    xr, cr, halo = exchange(now, now, r0, r1)
    (refl,) = call(
        own_refl_kernel,
        [scal, reflectivity],
        [jax.ShapeDtypeStruct((NOFF, B, Z, H), reflectivity.dtype)],
        [],
        specs=[hbm],
        extra=[pltpu.SemaphoreType.DMA],
    )
    px, pc, prior, force, r0, r1 = _split(
        call(
            second_kernel,
            [scal, offsets, now, prior, xr, cr, courant_own, refl, refl_far, *coefs, *halo],
            [shape(B + 2, Z, Y)] * 2 + [shape(*wide), shape(*block)] + tile_outs([2, 2]),
            [ext] * 3,
            2,
        ),
        4,
        n,
    )
    xr, cr, halo = exchange(px, pc, r0, r1)
    wave, near_u, back = call(
        third_kernel, [scal, px, prior, xr, cr, *coefs, *halo], [shape(*block)] + [shape(B, Z, H)] * 2, [ext] * 3 + [wide]
    )
    wave_x = lax.ppermute(wave, ("gx", "gy"), pairs_x)
    wave_c = chip(wave)
    qx, qc, force2, scat, scat_prior, r0, r1 = _split(
        call(
            scatter_kernel,
            [scal, offsets, px, xr, cr, courant_own, refl, refl_far, *coefs, force, *halo],
            [shape(3, Z, Y)] * 2 + [shape(*block)] * 2 + [shape(*wide)] + tile_outs([2, 1]),
            [ext] * 4,
            2,
        ),
        5,
        n,
    )
    xr, cr, halo = exchange(qx, qc, r0, r1)
    back = chip(back)
    (force3,) = call(
        source_kernel,
        [scal, offsets, wave, wave_x, wave_c, courant_own, refl, refl_far],
        [shape(*block)],
        [ext],
        2,
    )
    scat, scat_prior, qx, qc, r0, r1 = _split(
        call(
            fourth_kernel,
            [scal, scat, scat_prior, xr, cr, force2, force3, *coefs, *halo],
            [shape(*block)] * 2 + [shape(1, Z, Y)] * 2 + tile_outs([1], 1),
            [ext] * 4 + [wide],
        ),
        4,
        n,
    )
    xr, cr, halo = exchange(qx, qc, r0, r1)

    def placed(half, other, into=None):
        return call(
            functools.partial(place_kernel, other=other),
            [scal, half] + ([] if into is None else [into]),
            [shape(rows, Z, H)],
            [],
            specs=[whole] + ([] if into is None else [hbm]),
            extra=[pltpu.SemaphoreType.DMA],
            aliases={} if into is None else {2: 0},
            out_specs=[hbm],
        )[0]

    (background,) = call(finish_kernel, [scal, near_u, back], [shape(rows, Z, H)], [])
    near_w, far_w = call(
        fifth_kernel, [scal, scat, scat_prior, force3, xr, cr, *coefs, *halo], [shape(B, Z, H)] * 2, [ext] * 3
    )
    far_w = chip(far_w)
    scattered = placed(near_w, False)
    scattered = placed(far_w, True, scattered)
    return background, scattered


def _split(values, count, n):
    return [*values[:count], values[count : count + n], values[count + n :]]


def solution(mesh):
    spec = P(("shot", "gx"), "section", "gy")
    assert mesh.shape["gy"] == 2
    return jax.shard_map(
        functools.partial(shards, mesh.shape["section"], mesh.shape["gx"]),
        mesh=mesh,
        in_specs=(spec,) * 5 + (P(None, ("shot", "gx"), "section", "gy"), P()),
        out_specs=(spec, spec),
        check_vma=False,
    )
```

```python
import functools

import jax
import jax.numpy as jnp
from jax import lax
from jax.experimental import pallas as pl
from jax.experimental.pallas import tpu as pltpu
from jax.sharding import PartitionSpec as P


NOFF = 17
MARGIN = 16
TILE = 8
F32 = jnp.float32
UNROLL = 8
FIRST, SECOND, THIRD, LAST = (2, 1, 2, 2, 2), (2,), (2, 3), (3, 2, 1)
SLACK = 8 << 20


class Geometry:
    def __init__(self, rows, depth, half, sections):
        self.B, self.Z, self.H, self.Y = rows // 2, depth, half, 2 * half
        self.two = sections == 2
        self.sides = 1 if self.two else 2
        self.ZE = depth + TILE * self.sides
        assert self.B >= MARGIN and depth % TILE == 0 and half % 128 == 0


def halo_place(side, depth, k, geo):
    return (1 - side) * (geo.B - depth) + side * 2 * geo.B + k


def slot_of(depth):
    return 4 if depth > 2 else depth


def tile_mask(sender, depth, turn, width):
    place = lax.broadcasted_iota(jnp.int32, (TILE, width), 0)
    place = lax.rem(place + (TILE - turn), TILE)
    start = (1 - sender) * (TILE - depth)
    return (place >= start) & (place < start + depth)


def turned(value, turn):
    turn = turn % TILE
    return value if turn == 0 else pltpu.roll(value, turn, 0)


def senders(s, geo):
    return [s] if geo.two else [0, 1]


def receivers(s, geo):
    return [(geo.Z, 1 - s)] if geo.two else [(geo.ZE - TILE, 0), (geo.Z, 1)]


def edge_tile(ref, row, sender, geo):
    start = pl.multiple_of((1 - sender) * (geo.Z - TILE), TILE)
    return ref[row, pl.ds(start, TILE), :]


def tiles_of(depths, geo):
    starts, total = [], 0
    for depth in depths:
        starts.append(total)
        total += geo.B * slot_of(depth) // TILE
    return starts, total


def corner_slot(depths):
    return 4 if max(depths) > 2 else 2


def corner_tiles(depths):
    return -(-sum(depths) * corner_slot(depths) // TILE)


def pack_tiles(items, g, s, tiles, corners, geo):
    depths = [depth for _, depth in items]
    starts, _ = tiles_of(depths, geo)
    for sender, tile_ref, corner_ref in zip(senders(s, geo), tiles, corners):
        for (ref, depth), start in zip(items, starts):
            slot = slot_of(depth)
            per = TILE // slot
            masks = [tile_mask(sender, depth, k * slot, geo.Y) for k in range(1, per)]
            for q in range(geo.B // per):
                out = edge_tile(ref, q * per, sender, geo)
                for k in range(1, per):
                    value = turned(edge_tile(ref, q * per + k, sender, geo), k * slot)
                    out = jnp.where(masks[k - 1], value, out)
                tile_ref[start + q] = out
        slot, place = corner_slot(depths), 0
        for ref, depth in items:
            for k in range(depth):
                at, turn = divmod(place * slot, TILE)
                value = turned(edge_tile(ref, g * (geo.B - depth) + k, sender, geo), turn)
                if turn:
                    value = jnp.where(tile_mask(sender, depth, turn, geo.Y), value, corner_ref[at])
                corner_ref[at] = value
                place += 1


def unpack_row(ref, depths, index, x, geo):
    depth = depths[index]
    per = TILE // slot_of(depth)
    return turned(ref[tiles_of(depths, geo)[0][index] + x // per], TILE - (x % per) * slot_of(depth))


def unpack_corner(ref, depths, index, k):
    at, turn = divmod((sum(depths[:index]) + k) * corner_slot(depths), TILE)
    return turned(ref[at], TILE - turn)


def unpack_c(ref, depths, index, side, k, geo):
    low = unpack_row(ref, depths, index, k, geo)
    high = unpack_row(ref, depths, index, geo.B - depths[index] + k, geo)
    return jnp.where(side == 1, low, high)


def fill(dst, own, xrow, crow, halo, depths, index, g, s, geo):
    n = geo.sides
    depth = depths[index]
    ends = list(zip(receivers(s, geo), halo[:n], halo[n : 2 * n], halo[2 * n :]))

    def one(row, carry):
        dst[geo.B + row, 0 : geo.Z, :] = own[row]
        return carry

    lax.fori_loop(0, geo.B, one, 0, unroll=4)
    for (offset, sender), tile, xtile, ctile in ends:
        keep = tile_mask(sender, depth, 0, geo.Y)
        span = slice(offset, offset + TILE)
        for row in range(geo.B):
            dst[geo.B + row, span, :] = jnp.where(keep, unpack_row(tile, depths, index, row, geo), 0.0)
        for k in range(depth):
            dst[halo_place(g, depth, k, geo), span, :] = jnp.where(keep, unpack_corner(xtile, depths, index, k), 0.0)
            value = unpack_c(ctile, depths, index, 1 - g, k, geo)
            dst[halo_place(1 - g, depth, k, geo), span, :] = jnp.where(keep, value, 0.0)
    for side, get in ((g, xrow), (1 - g, crow)):
        for k in range(depth if get is not None else 0):
            dst[halo_place(side, depth, k, geo), 0 : geo.Z, :] = get(k)


def fill_blocks(dst, xblock, cblock, g, geo, own=None):
    def one(row, carry):
        dst[g * 2 * geo.B + row, 0 : geo.Z, :] = xblock[row]
        dst[(1 - g) * 2 * geo.B + row, 0 : geo.Z, :] = cblock[row]
        if own is not None:
            dst[geo.B + row, 0 : geo.Z, :] = own[row]
        return carry

    lax.fori_loop(0, geo.B, one, 0, unroll=2)


def each(first, count, body, group):
    group = max(k for k in range(1, group + 1) if count % k == 0)

    def trip(index, carry):
        for k in range(group):
            body(first + index * group + k)
        return carry

    lax.fori_loop(0, count // group, trip, 0)


def advance(src, off, first, count, top, prior, extra, store, coefs, dif, tot, geo, group=None):
    xx, zz, yy, xz, mid = coefs
    lane = lax.broadcasted_iota(jnp.int32, (top, 128), 1)
    low_edge, high_edge = lane == 0, lane == 127
    spans = [slice(k, k + 128) for k in range(0, geo.Y, 128)]

    def slopes(row):
        value = src[row - off]
        above = pltpu.roll(value, geo.ZE - 1, 0)[0:top]
        below = pltpu.roll(value, 1, 0)[0:top]
        dif[row, 0:top] = above - below
        return value[0:top], above + below

    def local(row):
        at = jnp.minimum(row - (geo.B - 2), geo.B + 3)
        whole, total = slopes(row)
        value = [whole[:, span] for span in spans]
        zero = jnp.zeros_like(value[0])
        right = [pltpu.roll(v, 127, 1) for v in value] + [zero]
        left = [zero] + [pltpu.roll(v, 1, 1) for v in value]
        for k, span in enumerate(spans):
            side = jnp.where(high_edge, right[k + 1], right[k]) + jnp.where(low_edge, left[k], left[k + 1])
            new = mid[at, 0:top, span] * value[k] + zz[at, 0:top, span] * total[:, span]
            tot[row, 0:top, span] = new + yy[at, 0:top, span] * side

    slopes(first - 1)
    local(first)

    def one(row):
        local(row + 1)
        at = row - (geo.B - 2)
        new = tot[row, 0:top] + xx[at, 0:top] * (src[row + 1 - off, 0:top] + src[row - 1 - off, 0:top])
        new = new + xz[at, 0:top] * (dif[row + 1, 0:top] - dif[row - 1, 0:top])
        last = prior(row)
        if last is not None:
            new = new - last[0:top]
        if extra is not None:
            new = new + extra(row)[0:top]
        store(row, new)

    each(first, count, one, group or UNROLL)


def make_source(ext, refl, refl_far, offsets, courant, out, g, geo):
    near = pl.multiple_of(g * geo.H, 128)
    far = pl.multiple_of((1 - g) * geo.H, 128)

    def one(row):
        acc = jnp.zeros((geo.Z, geo.H), F32)
        acc_far = jnp.zeros((geo.Z, geo.H), F32)
        for h in range(NOFF):
            place = geo.B + row + offsets[h]
            acc = acc + refl[h, row].astype(F32) * ext[place, 0 : geo.Z, pl.ds(near, geo.H)]
            acc_far = acc_far + refl_far[h, row] * ext[place, 0 : geo.Z, pl.ds(far, geo.H)]
        out[row, :, pl.ds(near, geo.H)] = courant[row, :, pl.ds(near, geo.H)] * acc
        out[row, :, pl.ds(far, geo.H)] = courant[row, :, pl.ds(far, geo.H)] * acc_far

    each(0, geo.B, one, 2)


def edge_rows(depth, side, geo):
    return side * (geo.B - depth)


def trig_products(angle):
    turns = jnp.floor(angle * 0.6366197723675814 + 0.5)
    rest = angle - turns * 1.5703125
    rest = rest - turns * 4.837512969970703125e-4
    rest = rest - turns * 7.549789954891882e-8
    odd = (turns - 2.0 * jnp.floor(turns * 0.5)) > 0.5
    square = rest * rest
    sine = rest + rest * square * (
        -1.6666654611e-1 + square * (8.3321608736e-3 + square * -1.9515295891e-4)
    )
    cosine = 1.0 - 0.5 * square + square * square * (
        4.166664568298827e-2 + square * (-1.388731625493765e-3 + square * 2.443315711809948e-5)
    )
    sine_square = jnp.where(odd, cosine * cosine, sine * sine)
    cosine_square = jnp.where(odd, sine * sine, cosine * cosine)
    product = sine * cosine
    return sine_square, cosine_square, jnp.where(odd, -product, product)


def half_kernel(geo, scal, *refs, other):
    *fields, out, sems = refs
    half = 1 - scal[0] if other else scal[0]
    start = pl.multiple_of(half * geo.B, TILE)
    copies = [
        pltpu.make_async_copy(field.at[pl.ds(start, geo.B)], out.at[k], sems.at[k]) for k, field in enumerate(fields)
    ]
    for copy in copies:
        copy.start()
    for copy in copies:
        copy.wait()


def widen_kernel(geo, scal, refl, out, held, sems):
    other = pl.multiple_of((1 - scal[0]) * geo.B, TILE)
    cuts = [0, 5, 9, 13, NOFF]
    copies = [
        pltpu.make_async_copy(refl.at[pl.ds(a, b - a), pl.ds(other, geo.B)], held.at[pl.ds(a, b - a)], sems.at[k])
        for k, (a, b) in enumerate(zip(cuts, cuts[1:]))
    ]
    for copy in copies:
        copy.start()
    for copy, a, b in zip(copies, cuts, cuts[1:]):
        copy.wait()

        def one(h, carry):
            for row in range(geo.B):
                out[h, row] = held[h, row].astype(F32)
            return carry

        lax.fori_loop(a, b, one, 0)


def own_refl_kernel(geo, scal, refl, out, sem):
    start = pl.multiple_of(scal[0] * geo.B, TILE)
    copy = pltpu.make_async_copy(refl.at[:, pl.ds(start, geo.B)], out, sem)
    copy.start()
    copy.wait()


def join_kernel(geo, scal, *refs):
    near, far = refs[:2]
    own = refs[2:7]
    px, pc = refs[7:9]
    tiles, corners = refs[9 : 9 + geo.sides], refs[9 + geo.sides :]
    g, s = scal[0], scal[1]
    near_y = pl.multiple_of(g * geo.H, 128)
    far_y = pl.multiple_of((1 - g) * geo.H, 128)

    def one(row, carry):
        for k in range(5):
            own[k][row, :, pl.ds(near_y, geo.H)] = near[k, row]
            own[k][row, :, pl.ds(far_y, geo.H)] = far[k, row]
        return carry

    lax.fori_loop(0, geo.B, one, 0, unroll=2)
    put_rows(list(zip(own, FIRST)), px, pc, 0, g, geo)
    pack_tiles(list(zip(own, FIRST)), g, s, tiles, corners, geo)


def put_rows(items, px, pc, start, g, geo):
    for side, out in ((g, px), (1 - g, pc)):
        at = start
        for ref, depth in items:
            for k in range(depth):
                out[at] = ref[edge_rows(depth, side, geo) + k]
                at += 1


def coefficients(speed, aniso, angle):
    stretch = 2.0 * aniso
    sine_square, cosine_square, product = trig_products(angle)
    cx = speed * (1.0 + stretch * cosine_square)
    cz = speed * (1.0 + stretch * sine_square)
    cy = speed * (1.0 + stretch)
    return cx, cz, cy, (0.5 * speed) * (stretch * product), 2.0 - 2.0 * (cx + cz + cy)


def coef_kernel(geo, scal, courant, aniso, tilt, *coefs):
    def one(row):
        for ref, value in zip(coefs, coefficients(courant[row], aniso[row], tilt[row])):
            ref[row + 2, 0 : geo.Z, :] = value

    each(0, geo.B, one, 2)


def coef_halo(coefs, xr, cr, halo, g, s, geo):
    n, depth, depths = geo.sides, FIRST[2], FIRST
    starts, _ = tiles_of(depths, geo)
    slot = slot_of(depth)
    per = TILE // slot
    for (offset, sender), tile, xtile, ctile in zip(receivers(s, geo), halo[:n], halo[n : 2 * n], halo[2 * n :]):
        keep = tile_mask(sender, depth, 0, geo.Y)
        span = slice(offset, offset + TILE)
        for q in range(geo.B // per):
            values = coefficients(*(tile[start + q] for start in starts[2:]))
            for k in range(per):
                for ref, value in zip(coefs, values):
                    ref[q * per + k + 2, span, :] = jnp.where(keep, turned(value, TILE - k * slot), 0.0)
        for k in range(depth):
            corner = [unpack_corner(xtile, depths, i, k) for i in (2, 3, 4)]
            for ref, value in zip(coefs, coefficients(*corner)):
                ref[halo_place(g, depth, k, geo) - (geo.B - 2), span, :] = jnp.where(keep, value, 0.0)
            other = [unpack_c(ctile, depths, i, 1 - g, k, geo) for i in (2, 3, 4)]
            for ref, value in zip(coefs, coefficients(*other)):
                ref[halo_place(1 - g, depth, k, geo) - (geo.B - 2), span, :] = jnp.where(keep, value, 0.0)
    for side, line in ((g, xr), (1 - g, cr)):
        for k in range(depth):
            for ref, value in zip(coefs, coefficients(line[3 + k], line[5 + k], line[7 + k])):
                ref[halo_place(side, depth, k, geo) - (geo.B - 2), 0 : geo.Z, :] = value


def first_kernel(geo, scal, *refs):
    n = geo.sides
    now, before, xr, cr = refs[:4]
    halo = refs[4 : 4 + 3 * n]
    out_block, prior_ext, *coefs = refs[9 + 3 * n : 16 + 3 * n]
    out_tiles, out_corners = refs[16 + 3 * n : 16 + 4 * n], refs[16 + 4 * n : 16 + 5 * n]
    ext, old, dif, tot = refs[16 + 5 * n :]
    g, s = scal[0], scal[1]
    coef_halo(coefs, xr, cr, halo, g, s, geo)
    fill(old, before, lambda k: xr[2 + k], lambda k: cr[2 + k], halo, FIRST, 1, g, s, geo)
    fill(ext, now, lambda k: xr[k], lambda k: cr[k], halo, FIRST, 0, g, s, geo)

    def keep_block(row, value):
        out_block[row - geo.B] = value

    two_steps(ext, 1, lambda row: old[row], prior_ext, keep_block, coefs, dif, tot, geo)
    pack_tiles([(out_block, 2)], g, s, out_tiles, out_corners, geo)


def two_steps(ext, beyond, prior, mid, store, coefs, dif, tot, geo):
    off = geo.B - beyond

    def keep(row, value):
        mid[row - off] = value

    advance(ext, 0, off, geo.B + 2 * beyond, geo.ZE, prior, None, keep, coefs, dif, tot, geo)
    advance(mid, off, geo.B, geo.B, geo.Z, lambda row: ext[row], None, store, coefs, dif, tot, geo)


def second_kernel(geo, scal, offsets, *refs):
    n = geo.sides
    now, before, xr, cr, courant, refl, refl_far, *coefs = refs[:12]
    halo = refs[12 : 12 + 3 * n]
    px, pc, prior_ext, force = refs[12 + 3 * n : 16 + 3 * n]
    out_tiles, out_corners = refs[16 + 3 * n : 16 + 4 * n], refs[16 + 4 * n : 16 + 5 * n]
    ext, dif, tot = refs[16 + 5 * n :]
    g, s = scal[0], scal[1]
    B = geo.B
    fill_blocks(ext, xr, cr, g, geo)
    fill(ext, now, None, None, halo, SECOND, 0, g, s, geo)

    def keep_block(row, value):
        px[row - B] = value
        pc[row - B] = value

    two_steps(ext, 1, lambda row: before[row - (B - 1)], prior_ext, keep_block, coefs, dif, tot, geo)
    make_source(ext, refl, refl_far, offsets, courant, force, g, geo)
    put_rows([(force, THIRD[1])], px, pc, B, g, geo)
    pack_tiles([(px, THIRD[0]), (force, THIRD[1])], g, s, out_tiles, out_corners, geo)


def third_kernel(geo, scal, *refs):
    n = geo.sides
    now, before, xr, cr, *coefs = refs[:9]
    halo = refs[9 : 9 + 3 * n]
    block, near, back = refs[9 + 3 * n : 12 + 3 * n]
    ext, dif, tot, mid = refs[12 + 3 * n :]
    g, s = scal[0], scal[1]
    B = geo.B

    def row_of(side, k):
        return (1 - side) * (B - 2) + k

    fill(ext, now, lambda k: xr[row_of(g, k)], lambda k: cr[row_of(1 - g, k)], halo, THIRD, 0, g, s, geo)

    def keep_block(row, value):
        block[row - B] = value
        low, high = value[:, 0 : geo.H], value[:, geo.H : geo.Y]
        near[row - B] = jnp.where(g == 0, low, high)
        back[row - B] = jnp.where(g == 0, high, low)

    two_steps(ext, 1, lambda row: before[row - (B - 1)], mid, keep_block, coefs, dif, tot, geo)


def scatter_kernel(geo, scal, offsets, *refs):
    n = geo.sides
    now, xr, cr, courant, refl, refl_far, *coefs = refs[:11]
    force = refs[11]
    halo = refs[12 : 12 + 3 * n]
    force_out, scat, scat_prior = refs[12 + 3 * n : 15 + 3 * n]
    ext, dif, tot, wave = refs[15 + 3 * n :]
    g, s = scal[0], scal[1]
    B = geo.B
    fill_blocks(ext, xr, cr, g, geo, now)
    make_source(ext, refl, refl_far, offsets, courant, force_out, g, geo)
    fill(wave, force, lambda k: xr[B + k], lambda k: cr[B + k], halo, THIRD, 1, g, s, geo)

    def keep_scat(row, value):
        scat[row - B] = value + force_out[row - B]

    two_steps(wave, 2, lambda row: -wave[row], scat_prior, keep_scat, coefs, dif, tot, geo)


def source_kernel(geo, scal, offsets, *refs):
    n = geo.sides
    now, xr, cr, courant, refl, refl_far, scat, force2 = refs[:8]
    force3, px, pc = refs[8:11]
    tiles, corners, ext = refs[11 : 11 + n], refs[11 + n : 11 + 2 * n], refs[11 + 2 * n]
    g, s = scal[0], scal[1]
    fill_blocks(ext, xr, cr, g, geo, now)
    make_source(ext, refl, refl_far, offsets, courant, force3, g, geo)
    items = list(zip((scat, force2, force3), LAST))
    put_rows(items, px, pc, 0, g, geo)
    pack_tiles(items, g, s, tiles, corners, geo)


def last_kernel(geo, scal, *refs):
    n = geo.sides
    scat, before, force2, force3, xr, cr, *coefs = refs[:11]
    halo = refs[11 : 11 + 3 * n]
    out_near, out_far = refs[11 + 3 * n : 13 + 3 * n]
    wave, second, third, dif, tot, mid4, mid5 = refs[13 + 3 * n :]
    g, s = scal[0], scal[1]
    B = geo.B
    fill(wave, scat, lambda k: xr[k], lambda k: cr[k], halo, LAST, 0, g, s, geo)
    fill(second, force2, lambda k: xr[3 + k], lambda k: cr[3 + k], halo, LAST, 1, g, s, geo)
    fill(third, force3, lambda k: xr[5 + k], lambda k: cr[5 + k], halo, LAST, 2, g, s, geo)

    def keep4(row, value):
        mid4[row - (B - 2)] = value

    def keep5(row, value):
        mid5[row - (B - 1)] = value

    def keep6(row, value):
        low, high = value[:, 0 : geo.H], value[:, geo.H : geo.Y]
        out_near[row - B] = jnp.where(g == 0, low, high)
        out_far[row - B] = jnp.where(g == 0, high, low)

    prior2 = lambda row: before[row - (B - 2)]
    prior4 = lambda row: mid4[row - (B - 2)]
    advance(wave, 0, B - 2, B + 4, geo.ZE, prior2, lambda row: second[row], keep4, coefs, dif, tot, geo)
    advance(mid4, B - 2, B - 1, B + 2, geo.ZE, lambda row: wave[row], lambda row: third[row], keep5, coefs, dif, tot, geo)
    advance(mid5, B - 1, B, B, geo.Z, prior4, lambda row: force3[row - B], keep6, coefs, dif, tot, geo)


def finish_kernel(geo, scal, near, far, out):
    g = scal[0]

    def one(row, carry):
        out[g * geo.B + row] = near[row]
        out[(1 - g) * geo.B + row] = far[row]
        return carry

    lax.fori_loop(0, geo.B, one, 0, unroll=4)


def place_kernel(geo, scal, *refs, other):
    half, out, sem = refs[0], refs[-2], refs[-1]
    start = pl.multiple_of((1 - scal[0] if other else scal[0]) * geo.B, TILE)
    copy = pltpu.make_async_copy(half, out.at[pl.ds(start, geo.B)], sem)
    copy.start()
    copy.wait()


def shards(sections, gx, wave_now, wave_before, courant, anisotropy, tilt, reflectivity, offsets):
    rows, depth, half = wave_now.shape
    geo = Geometry(rows, depth, half, sections)
    B, Z, H, Y, ZE, n = geo.B, geo.Z, geo.H, geo.Y, geo.ZE, geo.sides
    g = lax.axis_index("gy")
    s = lax.axis_index("section")
    scal = jnp.stack([g, s]).astype(jnp.int32)
    swap = [(0, 1), (1, 0)]
    pairs_x = [p for i in range(gx - 1) for p in ((2 * i + 1, 2 * i + 2), (2 * i + 2, 2 * i + 1))]

    def z_moves():
        if geo.two:
            return [[(0, 1), (1, 0)]]
        return [[(i, i + 1) for i in range(sections - 1)], [(i + 1, i) for i in range(sections - 1)]]

    def corner_pairs(move):
        out = []
        for a, b in pairs_x:
            for i, j in move:
                out.append((((a // 2) * sections + i) * 2 + a % 2, ((b // 2) * sections + j) * 2 + b % 2))
        return out

    def chip(value):
        return lax.ppermute(value, "gy", swap)

    def exchange(px, pc, tiles, corners):
        xr = lax.ppermute(px, ("gx", "gy"), pairs_x)
        xz = [
            lax.ppermute(t, ("gx", "section", "gy"), corner_pairs(m)) for t, m in zip(corners, z_moves())
        ]
        zr = [lax.ppermute(t, "section", m) for t, m in zip(tiles, z_moves())]
        cr = chip(pc)
        cz = [chip(t) for t in zr]
        return xr, cr, [*zr, *xz, *cz]

    def shape(*dims):
        return jax.ShapeDtypeStruct(dims, F32)

    def call(kernel, inputs, outs, scratch, smem=1, specs=None, extra=(), aliases=None, out_specs=None):
        if specs is None:
            specs = [pl.BlockSpec(memory_space=pltpu.SMEM)] * (smem - 1)
            specs += [pl.BlockSpec(memory_space=pltpu.VMEM)] * (len(inputs) - smem)
        used = sum(4 * d[0] * d[1] * d[2] for d in scratch)
        return pl.pallas_call(
            functools.partial(kernel, geo),
            out_shape=outs,
            grid_spec=pltpu.PrefetchScalarGridSpec(
                num_scalar_prefetch=1,
                grid=(1,),
                in_specs=specs,
                out_specs=out_specs or [pl.BlockSpec(memory_space=pltpu.VMEM)] * len(outs),
                scratch_shapes=[*(pltpu.VMEM(d, F32) for d in scratch), *extra],
            ),
            input_output_aliases=aliases or {},
            compiler_params=pltpu.CompilerParams(vmem_limit_bytes=used + SLACK),
        )(*inputs)

    block, wide, wider, ext = (B, Z, Y), (B + 2, ZE, Y), (B + 4, ZE, Y), (3 * B, ZE, Y)

    def tile_outs(depths):
        return [shape(tiles_of(depths, geo)[1], TILE, Y)] * n + [shape(corner_tiles(depths), TILE, Y)] * n

    in_hbm = lambda value: pltpu.with_memory_space_constraint(value, pltpu.HBM)
    fields = [in_hbm(f) for f in (wave_now, wave_before, courant, anisotropy, tilt)]
    reflectivity = in_hbm(reflectivity)
    hbm = pl.BlockSpec(memory_space=pltpu.HBM)
    whole = pl.BlockSpec(memory_space=pltpu.VMEM)

    def half_of(other):
        kernel = functools.partial(half_kernel, other=other)
        copies = [pltpu.SemaphoreType.DMA((5,))]
        (out,) = call(kernel, [scal, *fields], [shape(5, B, Z, H)], [], specs=[hbm] * 5, extra=copies)
        return out

    far = chip(half_of(True))
    near = half_of(False)
    *own, px, pc, r0, r1 = _split(
        call(
            join_kernel,
            [scal, near, far],
            [shape(*block)] * 5 + [shape(sum(FIRST), Z, Y)] * 2 + tile_outs(FIRST),
            [],
        ),
        7,
        n,
    )
    xr, cr, halo = exchange(px, pc, r0, r1)
    (refl_far,) = call(
        widen_kernel,
        [scal, reflectivity],
        [shape(NOFF, B, Z, H)],
        [],
        specs=[hbm],
        extra=[pltpu.VMEM((NOFF, B, Z, H), reflectivity.dtype), pltpu.SemaphoreType.DMA((4,))],
    )
    refl_far = chip(refl_far)
    coefs = call(coef_kernel, [scal, *own[2:]], [shape(*wider)] * 5, [])
    inputs = [scal, *own[:2], xr, cr, *halo, *coefs]
    first = len(inputs) - 5
    now, prior, *coefs, r0, r1 = _split(
        call(
            first_kernel,
            inputs,
            [shape(*block), shape(*wide)] + [shape(*wider)] * 5 + tile_outs(SECOND),
            [ext] * 4,
            aliases={first + k: 2 + k for k in range(5)},
        ),
        7,
        n,
    )
    courant_own = own[2]
    xr, cr, halo = exchange(now, now, r0, r1)
    (refl,) = call(
        own_refl_kernel,
        [scal, reflectivity],
        [jax.ShapeDtypeStruct((NOFF, B, Z, H), reflectivity.dtype)],
        [],
        specs=[hbm],
        extra=[pltpu.SemaphoreType.DMA],
    )
    px, pc, prior, force, r0, r1 = _split(
        call(
            second_kernel,
            [scal, offsets, now, prior, xr, cr, courant_own, refl, refl_far, *coefs, *halo],
            [shape(B + THIRD[1], Z, Y)] * 2 + [shape(*wide), shape(*block)] + tile_outs(THIRD),
            [ext] * 3,
            2,
        ),
        4,
        n,
    )
    xr, cr, halo = exchange(px, pc, r0, r1)
    wave, near_u, back = call(
        third_kernel, [scal, px, prior, xr, cr, *coefs, *halo], [shape(*block)] + [shape(B, Z, H)] * 2, [ext] * 3 + [wide]
    )
    wave_x = lax.ppermute(wave, ("gx", "gy"), pairs_x)
    wave_c = chip(wave)
    force2, scat, scat_prior = call(
        scatter_kernel,
        [scal, offsets, px, xr, cr, courant_own, refl, refl_far, *coefs, force, *halo],
        [shape(*block)] * 2 + [shape(*wider)],
        [ext] * 4,
        2,
    )
    force3, qx, qc, r0, r1 = _split(
        call(
            source_kernel,
            [scal, offsets, wave, wave_x, wave_c, courant_own, refl, refl_far, scat, force2],
            [shape(*block)] + [shape(sum(LAST), Z, Y)] * 2 + tile_outs(LAST),
            [ext],
            2,
        ),
        3,
        n,
    )
    xr, cr, halo = exchange(qx, qc, r0, r1)

    def placed(half, other, into=None):
        return call(
            functools.partial(place_kernel, other=other),
            [scal, half] + ([] if into is None else [into]),
            [shape(rows, Z, H)],
            [],
            specs=[whole] + ([] if into is None else [hbm]),
            extra=[pltpu.SemaphoreType.DMA],
            aliases={} if into is None else {2: 0},
            out_specs=[hbm],
        )[0]

    back = chip(back)
    (background,) = call(finish_kernel, [scal, near_u, back], [shape(rows, Z, H)], [])
    near_w, far_w = call(
        last_kernel,
        [scal, scat, scat_prior, force2, force3, xr, cr, *coefs, *halo],
        [shape(B, Z, H)] * 2,
        [ext] * 5 + [wider, wide],
    )
    far_w = chip(far_w)
    scattered = placed(near_w, False)
    scattered = placed(far_w, True, scattered)
    return background, scattered


def _split(values, count, n):
    return [*values[:count], values[count : count + n], values[count + n :]]


def solution(mesh):
    spec = P(("shot", "gx"), "section", "gy")
    assert mesh.shape["gy"] == 2
    return jax.shard_map(
        functools.partial(shards, mesh.shape["section"], mesh.shape["gx"]),
        mesh=mesh,
        in_specs=(spec,) * 5 + (P(None, ("shot", "gx"), "section", "gy"), P()),
        out_specs=(spec, spec),
        check_vma=False,
    )
```

```python
import functools

import jax
import jax.numpy as jnp
from jax import lax
from jax.experimental import pallas as pl
from jax.experimental.pallas import tpu as pltpu
from jax.sharding import PartitionSpec as P


NOFF = 17
MARGIN = 16
TILE = 8
F32 = jnp.float32
UNROLL = 8
FIRST, SECOND, THIRD, LAST = (2, 1, 2, 2, 2), (2,), (2, 3), (3, 2, 1)
SLACK = 8 << 20


class Geometry:
    def __init__(self, rows, depth, half, sections):
        self.B, self.Z, self.H, self.Y = rows // 2, depth, half, 2 * half
        self.two = sections == 2
        self.sides = 1 if self.two else 2
        self.ZE = depth + TILE * self.sides
        assert self.B >= MARGIN and depth % TILE == 0 and half % 128 == 0


def halo_place(side, depth, k, geo):
    return (1 - side) * (geo.B - depth) + side * 2 * geo.B + k


def slot_of(depth):
    return 4 if depth > 2 else depth


def tile_mask(sender, depth, turn, width):
    place = lax.broadcasted_iota(jnp.int32, (TILE, width), 0)
    place = lax.rem(place + (TILE - turn), TILE)
    start = (1 - sender) * (TILE - depth)
    return (place >= start) & (place < start + depth)


def turned(value, turn):
    turn = turn % TILE
    return value if turn == 0 else pltpu.roll(value, turn, 0)


def senders(s, geo):
    return [s] if geo.two else [0, 1]


def receivers(s, geo):
    return [(geo.Z, 1 - s)] if geo.two else [(geo.ZE - TILE, 0), (geo.Z, 1)]


def edge_tile(ref, row, sender, geo):
    start = pl.multiple_of((1 - sender) * (geo.Z - TILE), TILE)
    return ref[row, pl.ds(start, TILE), :]


def tiles_of(depths, geo):
    starts, total = [], 0
    for depth in depths:
        starts.append(total)
        total += geo.B * slot_of(depth) // TILE
    return starts, total


def corner_slot(depths):
    return 4 if max(depths) > 2 else 2


def corner_tiles(depths):
    return -(-sum(depths) * corner_slot(depths) // TILE)


def pack_tiles(items, g, s, tiles, corners, geo):
    depths = [depth for _, depth in items]
    starts, _ = tiles_of(depths, geo)
    for sender, tile_ref, corner_ref in zip(senders(s, geo), tiles, corners):
        for (ref, depth), start in zip(items, starts):
            slot = slot_of(depth)
            per = TILE // slot
            masks = [tile_mask(sender, depth, k * slot, geo.Y) for k in range(1, per)]
            for q in range(geo.B // per):
                out = edge_tile(ref, q * per, sender, geo)
                for k in range(1, per):
                    value = turned(edge_tile(ref, q * per + k, sender, geo), k * slot)
                    out = jnp.where(masks[k - 1], value, out)
                tile_ref[start + q] = out
        slot, place = corner_slot(depths), 0
        for ref, depth in items:
            for k in range(depth):
                at, turn = divmod(place * slot, TILE)
                value = turned(edge_tile(ref, g * (geo.B - depth) + k, sender, geo), turn)
                if turn:
                    value = jnp.where(tile_mask(sender, depth, turn, geo.Y), value, corner_ref[at])
                corner_ref[at] = value
                place += 1


def unpack_row(ref, depths, index, x, geo):
    depth = depths[index]
    per = TILE // slot_of(depth)
    return turned(ref[tiles_of(depths, geo)[0][index] + x // per], TILE - (x % per) * slot_of(depth))


def unpack_corner(ref, depths, index, k):
    at, turn = divmod((sum(depths[:index]) + k) * corner_slot(depths), TILE)
    return turned(ref[at], TILE - turn)


def unpack_c(ref, depths, index, side, k, geo):
    low = unpack_row(ref, depths, index, k, geo)
    high = unpack_row(ref, depths, index, geo.B - depths[index] + k, geo)
    return jnp.where(side == 1, low, high)


def fill(dst, own, xrow, crow, halo, depths, index, g, s, geo):
    n = geo.sides
    depth = depths[index]
    ends = list(zip(receivers(s, geo), halo[:n], halo[n : 2 * n], halo[2 * n :]))

    def one(row, carry):
        dst[geo.B + row, 0 : geo.Z, :] = own[row]
        return carry

    lax.fori_loop(0, geo.B, one, 0, unroll=4)
    for (offset, sender), tile, xtile, ctile in ends:
        keep = tile_mask(sender, depth, 0, geo.Y)
        span = slice(offset, offset + TILE)
        for row in range(geo.B):
            dst[geo.B + row, span, :] = jnp.where(keep, unpack_row(tile, depths, index, row, geo), 0.0)
        for k in range(depth):
            dst[halo_place(g, depth, k, geo), span, :] = jnp.where(keep, unpack_corner(xtile, depths, index, k), 0.0)
            value = unpack_c(ctile, depths, index, 1 - g, k, geo)
            dst[halo_place(1 - g, depth, k, geo), span, :] = jnp.where(keep, value, 0.0)
    for side, get in ((g, xrow), (1 - g, crow)):
        for k in range(depth if get is not None else 0):
            dst[halo_place(side, depth, k, geo), 0 : geo.Z, :] = get(k)


def fill_blocks(dst, xblock, cblock, g, geo, own=None):
    def one(row, carry):
        dst[g * 2 * geo.B + row, 0 : geo.Z, :] = xblock[row]
        dst[(1 - g) * 2 * geo.B + row, 0 : geo.Z, :] = cblock[row]
        if own is not None:
            dst[geo.B + row, 0 : geo.Z, :] = own[row]
        return carry

    lax.fori_loop(0, geo.B, one, 0, unroll=2)


def each(first, count, body, group):
    group = max(k for k in range(1, group + 1) if count % k == 0)

    def trip(index, carry):
        for k in range(group):
            body(first + index * group + k)
        return carry

    lax.fori_loop(0, count // group, trip, 0)


def advance(src, off, first, count, top, prior, extra, store, coefs, dif, tot, geo, group=None):
    xx, zz, yy, xz, mid = coefs
    lane = lax.broadcasted_iota(jnp.int32, (top, 128), 1)
    low_edge, high_edge = lane == 0, lane == 127
    spans = [slice(k, k + 128) for k in range(0, geo.Y, 128)]

    def slopes(row):
        value = src[row - off]
        above = pltpu.roll(value, geo.ZE - 1, 0)[0:top]
        below = pltpu.roll(value, 1, 0)[0:top]
        dif[row, 0:top] = above - below
        return value[0:top], above + below

    def local(row):
        at = jnp.minimum(row - (geo.B - 2), geo.B + 3)
        whole, total = slopes(row)
        value = [whole[:, span] for span in spans]
        zero = jnp.zeros_like(value[0])
        right = [pltpu.roll(v, 127, 1) for v in value] + [zero]
        left = [zero] + [pltpu.roll(v, 1, 1) for v in value]
        for k, span in enumerate(spans):
            side = jnp.where(high_edge, right[k + 1], right[k]) + jnp.where(low_edge, left[k], left[k + 1])
            new = mid[at, 0:top, span] * value[k] + zz[at, 0:top, span] * total[:, span]
            tot[row, 0:top, span] = new + yy[at, 0:top, span] * side

    slopes(first - 1)
    local(first)

    def one(row):
        local(row + 1)
        at = row - (geo.B - 2)
        new = tot[row, 0:top] + xx[at, 0:top] * (src[row + 1 - off, 0:top] + src[row - 1 - off, 0:top])
        new = new + xz[at, 0:top] * (dif[row + 1, 0:top] - dif[row - 1, 0:top])
        last = prior(row)
        if last is not None:
            new = new - last[0:top]
        if extra is not None:
            new = new + extra(row)[0:top]
        store(row, new)

    each(first, count, one, group or UNROLL)


def make_source(ext, refl, refl_far, offsets, courant, out, g, geo):
    near = pl.multiple_of(g * geo.H, 128)
    far = pl.multiple_of((1 - g) * geo.H, 128)

    def one(row):
        acc = jnp.zeros((geo.Z, geo.H), F32)
        acc_far = jnp.zeros((geo.Z, geo.H), F32)
        for h in range(NOFF):
            place = geo.B + row + offsets[h]
            acc = acc + refl[h, row].astype(F32) * ext[place, 0 : geo.Z, pl.ds(near, geo.H)]
            acc_far = acc_far + refl_far[h, row] * ext[place, 0 : geo.Z, pl.ds(far, geo.H)]
        out[row, :, pl.ds(near, geo.H)] = courant[row, :, pl.ds(near, geo.H)] * acc
        out[row, :, pl.ds(far, geo.H)] = courant[row, :, pl.ds(far, geo.H)] * acc_far

    each(0, geo.B, one, 2)


def edge_rows(depth, side, geo):
    return side * (geo.B - depth)


def trig_products(angle):
    turns = jnp.floor(angle * 0.6366197723675814 + 0.5)
    rest = angle - turns * 1.5703125
    rest = rest - turns * 4.837512969970703125e-4
    rest = rest - turns * 7.549789954891882e-8
    odd = (turns - 2.0 * jnp.floor(turns * 0.5)) > 0.5
    square = rest * rest
    sine = rest + rest * square * (
        -1.6666654611e-1 + square * (8.3321608736e-3 + square * -1.9515295891e-4)
    )
    cosine = 1.0 - 0.5 * square + square * square * (
        4.166664568298827e-2 + square * (-1.388731625493765e-3 + square * 2.443315711809948e-5)
    )
    sine_square = jnp.where(odd, cosine * cosine, sine * sine)
    cosine_square = jnp.where(odd, sine * sine, cosine * cosine)
    product = sine * cosine
    return sine_square, cosine_square, jnp.where(odd, -product, product)


def half_kernel(geo, scal, *refs, other):
    *fields, out, sems = refs
    half = 1 - scal[0] if other else scal[0]
    start = pl.multiple_of(half * geo.B, TILE)
    copies = [
        pltpu.make_async_copy(field.at[pl.ds(start, geo.B)], out.at[k], sems.at[k]) for k, field in enumerate(fields)
    ]
    for copy in copies:
        copy.start()
    for copy in copies:
        copy.wait()


def join_kernel(geo, scal, *refs):
    near, far = refs[:2]
    own = refs[2:7]
    px, pc = refs[7:9]
    tiles, corners = refs[9 : 9 + geo.sides], refs[9 + geo.sides :]
    g, s = scal[0], scal[1]
    near_y = pl.multiple_of(g * geo.H, 128)
    far_y = pl.multiple_of((1 - g) * geo.H, 128)

    def one(row, carry):
        for k in range(5):
            own[k][row, :, pl.ds(near_y, geo.H)] = near[k, row]
            own[k][row, :, pl.ds(far_y, geo.H)] = far[k, row]
        return carry

    lax.fori_loop(0, geo.B, one, 0, unroll=2)
    put_rows(list(zip(own, FIRST)), px, pc, 0, g, geo)
    pack_tiles(list(zip(own, FIRST)), g, s, tiles, corners, geo)


def put_rows(items, px, pc, start, g, geo):
    for side, out in ((g, px), (1 - g, pc)):
        at = start
        for ref, depth in items:
            for k in range(depth):
                out[at] = ref[edge_rows(depth, side, geo) + k]
                at += 1


def coefficients(speed, aniso, angle):
    stretch = 2.0 * aniso
    sine_square, cosine_square, product = trig_products(angle)
    cx = speed * (1.0 + stretch * cosine_square)
    cz = speed * (1.0 + stretch * sine_square)
    cy = speed * (1.0 + stretch)
    return cx, cz, cy, (0.5 * speed) * (stretch * product), 2.0 - 2.0 * (cx + cz + cy)


def prepare_kernel(geo, scal, courant, aniso, tilt, refl, *refs):
    *coefs, out, held, sems = refs
    other = pl.multiple_of((1 - scal[0]) * geo.B, TILE)
    cuts = [0, 5, 9, 13, NOFF]
    copies = [
        pltpu.make_async_copy(refl.at[pl.ds(a, b - a), pl.ds(other, geo.B)], held.at[pl.ds(a, b - a)], sems.at[k])
        for k, (a, b) in enumerate(zip(cuts, cuts[1:]))
    ]
    for copy in copies:
        copy.start()

    def one(row):
        for ref, value in zip(coefs, coefficients(courant[row], aniso[row], tilt[row])):
            ref[row + 2, 0 : geo.Z, :] = value

    each(0, geo.B, one, 2)
    for copy, a, b in zip(copies, cuts, cuts[1:]):
        copy.wait()

        def widen(h, carry):
            for row in range(geo.B):
                out[h, row] = held[h, row].astype(F32)
            return carry

        lax.fori_loop(a, b, widen, 0)


def coef_halo(coefs, xr, cr, halo, g, s, geo):
    n, depth, depths = geo.sides, FIRST[2], FIRST
    starts, _ = tiles_of(depths, geo)
    slot = slot_of(depth)
    per = TILE // slot
    for (offset, sender), tile, xtile, ctile in zip(receivers(s, geo), halo[:n], halo[n : 2 * n], halo[2 * n :]):
        keep = tile_mask(sender, depth, 0, geo.Y)
        span = slice(offset, offset + TILE)
        for q in range(geo.B // per):
            values = coefficients(*(tile[start + q] for start in starts[2:]))
            for k in range(per):
                for ref, value in zip(coefs, values):
                    ref[q * per + k + 2, span, :] = jnp.where(keep, turned(value, TILE - k * slot), 0.0)
        for k in range(depth):
            corner = [unpack_corner(xtile, depths, i, k) for i in (2, 3, 4)]
            for ref, value in zip(coefs, coefficients(*corner)):
                ref[halo_place(g, depth, k, geo) - (geo.B - 2), span, :] = jnp.where(keep, value, 0.0)
            other = [unpack_c(ctile, depths, i, 1 - g, k, geo) for i in (2, 3, 4)]
            for ref, value in zip(coefs, coefficients(*other)):
                ref[halo_place(1 - g, depth, k, geo) - (geo.B - 2), span, :] = jnp.where(keep, value, 0.0)
    for side, line in ((g, xr), (1 - g, cr)):
        for k in range(depth):
            for ref, value in zip(coefs, coefficients(line[3 + k], line[5 + k], line[7 + k])):
                ref[halo_place(side, depth, k, geo) - (geo.B - 2), 0 : geo.Z, :] = value


def first_kernel(geo, scal, *refs):
    n = geo.sides
    now, before, xr, cr = refs[:4]
    halo = refs[4 : 4 + 3 * n]
    refl = refs[9 + 3 * n]
    out_block, prior_ext, *coefs = refs[10 + 3 * n : 17 + 3 * n]
    out_tiles, out_corners = refs[17 + 3 * n : 17 + 4 * n], refs[17 + 4 * n : 17 + 5 * n]
    near_refl, ext, old, dif, tot, sem = refs[17 + 5 * n :]
    g, s = scal[0], scal[1]
    copy = pltpu.make_async_copy(refl.at[:, pl.ds(pl.multiple_of(g * geo.B, TILE), geo.B)], near_refl, sem)
    copy.start()
    coef_halo(coefs, xr, cr, halo, g, s, geo)
    fill(old, before, lambda k: xr[2 + k], lambda k: cr[2 + k], halo, FIRST, 1, g, s, geo)
    fill(ext, now, lambda k: xr[k], lambda k: cr[k], halo, FIRST, 0, g, s, geo)

    def keep_block(row, value):
        out_block[row - geo.B] = value

    two_steps(ext, 1, lambda row: old[row], prior_ext, keep_block, coefs, dif, tot, geo)
    pack_tiles([(out_block, 2)], g, s, out_tiles, out_corners, geo)
    copy.wait()


def two_steps(ext, beyond, prior, mid, store, coefs, dif, tot, geo):
    off = geo.B - beyond

    def keep(row, value):
        mid[row - off] = value

    advance(ext, 0, off, geo.B + 2 * beyond, geo.ZE, prior, None, keep, coefs, dif, tot, geo)
    advance(mid, off, geo.B, geo.B, geo.Z, lambda row: ext[row], None, store, coefs, dif, tot, geo)


def second_kernel(geo, scal, *refs):
    n = geo.sides
    now, before, xr, cr, force, *coefs = refs[:10]
    halo = refs[10 : 10 + 3 * n]
    px, pc, prior_ext = refs[10 + 3 * n : 13 + 3 * n]
    out_tiles, out_corners = refs[13 + 3 * n : 13 + 4 * n], refs[13 + 4 * n : 13 + 5 * n]
    ext, dif, tot = refs[13 + 5 * n :]
    g, s = scal[0], scal[1]
    B = geo.B
    fill(ext, now, lambda k: xr[row_of(g, k, geo)], lambda k: cr[row_of(1 - g, k, geo)], halo, SECOND, 0, g, s, geo)

    def keep_block(row, value):
        px[row - B] = value
        pc[row - B] = value

    two_steps(ext, 1, lambda row: before[row - (B - 1)], prior_ext, keep_block, coefs, dif, tot, geo)
    put_rows([(force, THIRD[1])], px, pc, B, g, geo)
    pack_tiles([(px, THIRD[0]), (force, THIRD[1])], g, s, out_tiles, out_corners, geo)


def row_of(side, k, geo):
    return (1 - side) * (geo.B - 2) + k


def source_only_kernel(geo, scal, offsets, now, xr, cr, courant, refl, refl_far, force, ext):
    fill_blocks(ext, xr, cr, scal[0], geo, now)
    make_source(ext, refl, refl_far, offsets, courant, force, scal[0], geo)


def third_kernel(geo, scal, *refs):
    n = geo.sides
    now, before, xr, cr, *coefs = refs[:9]
    halo = refs[9 : 9 + 3 * n]
    block, near, back = refs[9 + 3 * n : 12 + 3 * n]
    ext, dif, tot, mid = refs[12 + 3 * n :]
    g, s = scal[0], scal[1]
    B = geo.B

    fill(ext, now, lambda k: xr[row_of(g, k, geo)], lambda k: cr[row_of(1 - g, k, geo)], halo, THIRD, 0, g, s, geo)

    def keep_block(row, value):
        block[row - B] = value
        low, high = value[:, 0 : geo.H], value[:, geo.H : geo.Y]
        near[row - B] = jnp.where(g == 0, low, high)
        back[row - B] = jnp.where(g == 0, high, low)

    two_steps(ext, 1, lambda row: before[row - (B - 1)], mid, keep_block, coefs, dif, tot, geo)


def scatter_kernel(geo, scal, offsets, *refs):
    n = geo.sides
    now, xr, cr, courant, refl, refl_far, *coefs = refs[:11]
    force = refs[11]
    halo = refs[12 : 12 + 3 * n]
    force_out, scat, scat_prior = refs[12 + 3 * n : 15 + 3 * n]
    ext, dif, tot, wave = refs[15 + 3 * n :]
    g, s = scal[0], scal[1]
    B = geo.B
    fill_blocks(ext, xr, cr, g, geo, now)
    make_source(ext, refl, refl_far, offsets, courant, force_out, g, geo)
    fill(wave, force, lambda k: xr[B + k], lambda k: cr[B + k], halo, THIRD, 1, g, s, geo)

    def keep_scat(row, value):
        scat[row - B] = value + force_out[row - B]

    two_steps(wave, 2, lambda row: -wave[row], scat_prior, keep_scat, coefs, dif, tot, geo)


def source_kernel(geo, scal, offsets, *refs):
    n = geo.sides
    now, xr, cr, courant, refl, refl_far, scat, force2 = refs[:8]
    force3, px, pc = refs[8:11]
    tiles, corners, ext = refs[11 : 11 + n], refs[11 + n : 11 + 2 * n], refs[11 + 2 * n]
    g, s = scal[0], scal[1]
    fill_blocks(ext, xr, cr, g, geo, now)
    make_source(ext, refl, refl_far, offsets, courant, force3, g, geo)
    items = list(zip((scat, force2, force3), LAST))
    put_rows(items, px, pc, 0, g, geo)
    pack_tiles(items, g, s, tiles, corners, geo)


def last_kernel(geo, scal, *refs):
    n = geo.sides
    scat, before, force2, force3, xr, cr, *coefs = refs[:11]
    halo = refs[11 : 11 + 3 * n]
    out_near, out_far = refs[11 + 3 * n : 13 + 3 * n]
    wave, second, third, dif, tot, mid4, mid5 = refs[13 + 3 * n :]
    g, s = scal[0], scal[1]
    B = geo.B
    fill(wave, scat, lambda k: xr[k], lambda k: cr[k], halo, LAST, 0, g, s, geo)
    fill(second, force2, lambda k: xr[3 + k], lambda k: cr[3 + k], halo, LAST, 1, g, s, geo)
    fill(third, force3, lambda k: xr[5 + k], lambda k: cr[5 + k], halo, LAST, 2, g, s, geo)

    def keep4(row, value):
        mid4[row - (B - 2)] = value

    def keep5(row, value):
        mid5[row - (B - 1)] = value

    def keep6(row, value):
        low, high = value[:, 0 : geo.H], value[:, geo.H : geo.Y]
        out_near[row - B] = jnp.where(g == 0, low, high)
        out_far[row - B] = jnp.where(g == 0, high, low)

    prior2 = lambda row: before[row - (B - 2)]
    prior4 = lambda row: mid4[row - (B - 2)]
    advance(wave, 0, B - 2, B + 4, geo.ZE, prior2, lambda row: second[row], keep4, coefs, dif, tot, geo)
    advance(mid4, B - 2, B - 1, B + 2, geo.ZE, lambda row: wave[row], lambda row: third[row], keep5, coefs, dif, tot, geo)
    advance(mid5, B - 1, B, B, geo.Z, prior4, lambda row: force3[row - B], keep6, coefs, dif, tot, geo)


def finish_kernel(geo, scal, near, far, out):
    g = scal[0]

    def one(row, carry):
        out[g * geo.B + row] = near[row]
        out[(1 - g) * geo.B + row] = far[row]
        return carry

    lax.fori_loop(0, geo.B, one, 0, unroll=4)


def place_kernel(geo, scal, *refs, other):
    half, out, sem = refs[0], refs[-2], refs[-1]
    start = pl.multiple_of((1 - scal[0] if other else scal[0]) * geo.B, TILE)
    copy = pltpu.make_async_copy(half, out.at[pl.ds(start, geo.B)], sem)
    copy.start()
    copy.wait()


def shards(sections, gx, wave_now, wave_before, courant, anisotropy, tilt, reflectivity, offsets):
    rows, depth, half = wave_now.shape
    geo = Geometry(rows, depth, half, sections)
    B, Z, H, Y, ZE, n = geo.B, geo.Z, geo.H, geo.Y, geo.ZE, geo.sides
    g = lax.axis_index("gy")
    s = lax.axis_index("section")
    scal = jnp.stack([g, s]).astype(jnp.int32)
    swap = [(0, 1), (1, 0)]
    pairs_x = [p for i in range(gx - 1) for p in ((2 * i + 1, 2 * i + 2), (2 * i + 2, 2 * i + 1))]

    def z_moves():
        if geo.two:
            return [[(0, 1), (1, 0)]]
        return [[(i, i + 1) for i in range(sections - 1)], [(i + 1, i) for i in range(sections - 1)]]

    def corner_pairs(move):
        out = []
        for a, b in pairs_x:
            for i, j in move:
                out.append((((a // 2) * sections + i) * 2 + a % 2, ((b // 2) * sections + j) * 2 + b % 2))
        return out

    def chip(value):
        return lax.ppermute(value, "gy", swap)

    def exchange(px, pc, tiles, corners):
        xr = lax.ppermute(px, ("gx", "gy"), pairs_x)
        xz = [
            lax.ppermute(t, ("gx", "section", "gy"), corner_pairs(m)) for t, m in zip(corners, z_moves())
        ]
        zr = [lax.ppermute(t, "section", m) for t, m in zip(tiles, z_moves())]
        cr = chip(pc)
        cz = [chip(t) for t in zr]
        return xr, cr, [*zr, *xz, *cz]

    def shape(*dims):
        return jax.ShapeDtypeStruct(dims, F32)

    def call(kernel, inputs, outs, scratch, smem=1, specs=None, extra=(), aliases=None, out_specs=None):
        if specs is None:
            specs = [pl.BlockSpec(memory_space=pltpu.SMEM)] * (smem - 1)
            specs += [pl.BlockSpec(memory_space=pltpu.VMEM)] * (len(inputs) - smem)
        used = sum(4 * d[0] * d[1] * d[2] for d in scratch)
        return pl.pallas_call(
            functools.partial(kernel, geo),
            out_shape=outs,
            grid_spec=pltpu.PrefetchScalarGridSpec(
                num_scalar_prefetch=1,
                grid=(1,),
                in_specs=specs,
                out_specs=out_specs or [pl.BlockSpec(memory_space=pltpu.VMEM)] * len(outs),
                scratch_shapes=[*(pltpu.VMEM(d, F32) for d in scratch), *extra],
            ),
            input_output_aliases=aliases or {},
            compiler_params=pltpu.CompilerParams(vmem_limit_bytes=used + SLACK),
        )(*inputs)

    block, wide, wider, ext = (B, Z, Y), (B + 2, ZE, Y), (B + 4, ZE, Y), (3 * B, ZE, Y)

    def tile_outs(depths):
        return [shape(tiles_of(depths, geo)[1], TILE, Y)] * n + [shape(corner_tiles(depths), TILE, Y)] * n

    in_hbm = lambda value: pltpu.with_memory_space_constraint(value, pltpu.HBM)
    fields = [in_hbm(f) for f in (wave_now, wave_before, courant, anisotropy, tilt)]
    reflectivity = in_hbm(reflectivity)
    hbm = pl.BlockSpec(memory_space=pltpu.HBM)
    whole = pl.BlockSpec(memory_space=pltpu.VMEM)

    def half_of(other):
        kernel = functools.partial(half_kernel, other=other)
        copies = [pltpu.SemaphoreType.DMA((5,))]
        (out,) = call(kernel, [scal, *fields], [shape(5, B, Z, H)], [], specs=[hbm] * 5, extra=copies)
        return out

    far = chip(half_of(True))
    near = half_of(False)
    *own, px, pc, r0, r1 = _split(
        call(
            join_kernel,
            [scal, near, far],
            [shape(*block)] * 5 + [shape(sum(FIRST), Z, Y)] * 2 + tile_outs(FIRST),
            [],
        ),
        7,
        n,
    )
    xr, cr, halo = exchange(px, pc, r0, r1)
    *coefs, refl_far = call(
        prepare_kernel,
        [scal, *own[2:], reflectivity],
        [shape(*wider)] * 5 + [shape(NOFF, B, Z, H)],
        [],
        specs=[whole] * 3 + [hbm],
        extra=[pltpu.VMEM((NOFF, B, Z, H), reflectivity.dtype), pltpu.SemaphoreType.DMA((4,))],
    )
    refl_far = chip(refl_far)
    inputs = [scal, *own[:2], xr, cr, *halo, *coefs, reflectivity]
    first = len(inputs) - 6
    now, prior, *coefs, r0, r1 = _split(
        call(
            first_kernel,
            inputs,
            [shape(*block), shape(*wide)]
            + [shape(*wider)] * 5
            + tile_outs(SECOND)
            + [jax.ShapeDtypeStruct((NOFF, B, Z, H), reflectivity.dtype)],
            [ext] * 4,
            specs=[whole] * (len(inputs) - 2) + [hbm],
            extra=[pltpu.SemaphoreType.DMA],
            aliases={first + k: 2 + k for k in range(5)},
        ),
        7,
        n,
    )
    *r1, refl = r1
    courant_own = own[2]
    xr, cr, halo = exchange(now, now, r0, r1)
    (force,) = call(
        source_only_kernel,
        [scal, offsets, now, xr, cr, courant_own, refl, refl_far],
        [shape(*block)],
        [ext],
        2,
    )
    px, pc, prior, r0, r1 = _split(
        call(
            second_kernel,
            [scal, now, prior, xr, cr, force, *coefs, *halo],
            [shape(B + THIRD[1], Z, Y)] * 2 + [shape(*wide)] + tile_outs(THIRD),
            [ext] * 3,
        ),
        3,
        n,
    )
    xr, cr, halo = exchange(px, pc, r0, r1)
    wave, near_u, back = call(
        third_kernel, [scal, px, prior, xr, cr, *coefs, *halo], [shape(*block)] + [shape(B, Z, H)] * 2, [ext] * 3 + [wide]
    )
    wave_x = lax.ppermute(wave, ("gx", "gy"), pairs_x)
    wave_c = chip(wave)
    force2, scat, scat_prior = call(
        scatter_kernel,
        [scal, offsets, px, xr, cr, courant_own, refl, refl_far, *coefs, force, *halo],
        [shape(*block)] * 2 + [shape(*wider)],
        [ext] * 4,
        2,
    )
    force3, qx, qc, r0, r1 = _split(
        call(
            source_kernel,
            [scal, offsets, wave, wave_x, wave_c, courant_own, refl, refl_far, scat, force2],
            [shape(*block)] + [shape(sum(LAST), Z, Y)] * 2 + tile_outs(LAST),
            [ext],
            2,
        ),
        3,
        n,
    )
    xr, cr, halo = exchange(qx, qc, r0, r1)

    def placed(half, other, into=None):
        return call(
            functools.partial(place_kernel, other=other),
            [scal, half] + ([] if into is None else [into]),
            [shape(rows, Z, H)],
            [],
            specs=[whole] + ([] if into is None else [hbm]),
            extra=[pltpu.SemaphoreType.DMA],
            aliases={} if into is None else {2: 0},
            out_specs=[hbm],
        )[0]

    back = chip(back)
    (background,) = call(finish_kernel, [scal, near_u, back], [shape(rows, Z, H)], [])
    near_w, far_w = call(
        last_kernel,
        [scal, scat, scat_prior, force2, force3, xr, cr, *coefs, *halo],
        [shape(B, Z, H)] * 2,
        [ext] * 5 + [wider, wide],
    )
    far_w = chip(far_w)
    scattered = placed(near_w, False)
    scattered = placed(far_w, True, scattered)
    return background, scattered


def _split(values, count, n):
    return [*values[:count], values[count : count + n], values[count + n :]]


def solution(mesh):
    spec = P(("shot", "gx"), "section", "gy")
    assert mesh.shape["gy"] == 2
    return jax.shard_map(
        functools.partial(shards, mesh.shape["section"], mesh.shape["gx"]),
        mesh=mesh,
        in_specs=(spec,) * 5 + (P(None, ("shot", "gx"), "section", "gy"), P()),
        out_specs=(spec, spec),
        check_vma=False,
    )
```

```python
import functools

import jax
import jax.numpy as jnp
from jax import lax
from jax.experimental import pallas as pl
from jax.experimental.pallas import tpu as pltpu
from jax.sharding import PartitionSpec as P


NOFF = 17
MARGIN = 16
TILE = 8
F32 = jnp.float32
UNROLL = 8
FIRST, SECOND, THIRD, LAST = (2, 1, 2, 2, 2), (2,), (2, 3), (3, 2, 1)
SLACK = 8 << 20


class Geometry:
    def __init__(self, rows, depth, half, sections):
        self.B, self.Z, self.H, self.Y = rows // 2, depth, half, 2 * half
        self.two = sections == 2
        self.sides = 1 if self.two else 2
        self.ZE = depth + TILE * self.sides
        assert self.B >= MARGIN and depth % TILE == 0 and half % 128 == 0


def halo_place(side, depth, k, geo):
    return (1 - side) * (geo.B - depth) + side * 2 * geo.B + k


def slot_of(depth):
    return 4 if depth > 2 else depth


def tile_mask(sender, depth, turn, width):
    place = lax.broadcasted_iota(jnp.int32, (TILE, width), 0)
    place = lax.rem(place + (TILE - turn), TILE)
    start = (1 - sender) * (TILE - depth)
    return (place >= start) & (place < start + depth)


def turned(value, turn):
    turn = turn % TILE
    return value if turn == 0 else pltpu.roll(value, turn, 0)


def senders(s, geo):
    return [s] if geo.two else [0, 1]


def receivers(s, geo):
    return [(geo.Z, 1 - s)] if geo.two else [(geo.ZE - TILE, 0), (geo.Z, 1)]


def edge_tile(ref, row, sender, geo):
    start = pl.multiple_of((1 - sender) * (geo.Z - TILE), TILE)
    return ref[row, pl.ds(start, TILE), :]


def tiles_of(depths, geo):
    starts, total = [], 0
    for depth in depths:
        starts.append(total)
        total += geo.B * slot_of(depth) // TILE
    return starts, total


def corner_slot(depths):
    return 4 if max(depths) > 2 else 2


def corner_tiles(depths):
    return -(-sum(depths) * corner_slot(depths) // TILE)


def pack_tiles(items, g, s, tiles, corners, geo):
    depths = [depth for _, depth in items]
    starts, _ = tiles_of(depths, geo)
    for sender, tile_ref, corner_ref in zip(senders(s, geo), tiles, corners):
        for (ref, depth), start in zip(items, starts):
            slot = slot_of(depth)
            per = TILE // slot
            masks = [tile_mask(sender, depth, k * slot, geo.Y) for k in range(1, per)]
            for q in range(geo.B // per):
                out = edge_tile(ref, q * per, sender, geo)
                for k in range(1, per):
                    value = turned(edge_tile(ref, q * per + k, sender, geo), k * slot)
                    out = jnp.where(masks[k - 1], value, out)
                tile_ref[start + q] = out
        slot, place = corner_slot(depths), 0
        for ref, depth in items:
            for k in range(depth):
                at, turn = divmod(place * slot, TILE)
                value = turned(edge_tile(ref, g * (geo.B - depth) + k, sender, geo), turn)
                if turn:
                    value = jnp.where(tile_mask(sender, depth, turn, geo.Y), value, corner_ref[at])
                corner_ref[at] = value
                place += 1


def unpack_row(ref, depths, index, x, geo):
    depth = depths[index]
    per = TILE // slot_of(depth)
    return turned(ref[tiles_of(depths, geo)[0][index] + x // per], TILE - (x % per) * slot_of(depth))


def unpack_corner(ref, depths, index, k):
    at, turn = divmod((sum(depths[:index]) + k) * corner_slot(depths), TILE)
    return turned(ref[at], TILE - turn)


def unpack_c(ref, depths, index, side, k, geo):
    low = unpack_row(ref, depths, index, k, geo)
    high = unpack_row(ref, depths, index, geo.B - depths[index] + k, geo)
    return jnp.where(side == 1, low, high)


def fill(dst, own, xrow, crow, halo, depths, index, g, s, geo):
    n = geo.sides
    depth = depths[index]
    ends = list(zip(receivers(s, geo), halo[:n], halo[n : 2 * n], halo[2 * n :]))

    def one(row, carry):
        dst[geo.B + row, 0 : geo.Z, :] = own[row]
        return carry

    lax.fori_loop(0, geo.B, one, 0, unroll=4)
    for (offset, sender), tile, xtile, ctile in ends:
        keep = tile_mask(sender, depth, 0, geo.Y)
        span = slice(offset, offset + TILE)
        for row in range(geo.B):
            dst[geo.B + row, span, :] = jnp.where(keep, unpack_row(tile, depths, index, row, geo), 0.0)
        for k in range(depth):
            dst[halo_place(g, depth, k, geo), span, :] = jnp.where(keep, unpack_corner(xtile, depths, index, k), 0.0)
            value = unpack_c(ctile, depths, index, 1 - g, k, geo)
            dst[halo_place(1 - g, depth, k, geo), span, :] = jnp.where(keep, value, 0.0)
    for side, get in ((g, xrow), (1 - g, crow)):
        for k in range(depth if get is not None else 0):
            dst[halo_place(side, depth, k, geo), 0 : geo.Z, :] = get(k)


def fill_blocks(dst, xblock, cblock, g, geo, own=None):
    def one(row, carry):
        dst[g * 2 * geo.B + row, 0 : geo.Z, :] = xblock[row]
        dst[(1 - g) * 2 * geo.B + row, 0 : geo.Z, :] = cblock[row]
        if own is not None:
            dst[geo.B + row, 0 : geo.Z, :] = own[row]
        return carry

    lax.fori_loop(0, geo.B, one, 0, unroll=2)


def each(first, count, body, group):
    group = max(k for k in range(1, group + 1) if count % k == 0)

    def trip(index, carry):
        for k in range(group):
            body(first + index * group + k)
        return carry

    lax.fori_loop(0, count // group, trip, 0)


def advance(src, off, first, count, top, prior, extra, store, coefs, dif, tot, geo, group=None):
    xx, zz, yy, xz, mid = coefs
    lane = lax.broadcasted_iota(jnp.int32, (top, 128), 1)
    low_edge, high_edge = lane == 0, lane == 127
    spans = [slice(k, k + 128) for k in range(0, geo.Y, 128)]

    def slopes(row):
        value = src[row - off]
        above = pltpu.roll(value, geo.ZE - 1, 0)[0:top]
        below = pltpu.roll(value, 1, 0)[0:top]
        dif[row, 0:top] = above - below
        return value[0:top], above + below

    def local(row):
        at = jnp.minimum(row - (geo.B - 2), geo.B + 3)
        whole, total = slopes(row)
        value = [whole[:, span] for span in spans]
        zero = jnp.zeros_like(value[0])
        right = [pltpu.roll(v, 127, 1) for v in value] + [zero]
        left = [zero] + [pltpu.roll(v, 1, 1) for v in value]
        for k, span in enumerate(spans):
            side = jnp.where(high_edge, right[k + 1], right[k]) + jnp.where(low_edge, left[k], left[k + 1])
            new = mid[at, 0:top, span] * value[k] + zz[at, 0:top, span] * total[:, span]
            tot[row, 0:top, span] = new + yy[at, 0:top, span] * side

    slopes(first - 1)
    local(first)

    def one(row):
        local(row + 1)
        at = row - (geo.B - 2)
        new = tot[row, 0:top] + xx[at, 0:top] * (src[row + 1 - off, 0:top] + src[row - 1 - off, 0:top])
        new = new + xz[at, 0:top] * (dif[row + 1, 0:top] - dif[row - 1, 0:top])
        last = prior(row)
        if last is not None:
            new = new - last[0:top]
        if extra is not None:
            new = new + extra(row)[0:top]
        store(row, new)

    each(first, count, one, group or UNROLL)


def make_source(ext, refl, refl_far, offsets, courant, out, g, geo):
    near = pl.multiple_of(g * geo.H, 128)
    far = pl.multiple_of((1 - g) * geo.H, 128)

    def one(row):
        acc = jnp.zeros((geo.Z, geo.H), F32)
        acc_far = jnp.zeros((geo.Z, geo.H), F32)
        for h in range(NOFF):
            place = geo.B + row + offsets[h]
            acc = acc + refl[h, row].astype(F32) * ext[place, 0 : geo.Z, pl.ds(near, geo.H)]
            acc_far = acc_far + refl_far[h, row] * ext[place, 0 : geo.Z, pl.ds(far, geo.H)]
        out[row, :, pl.ds(near, geo.H)] = courant[row, :, pl.ds(near, geo.H)] * acc
        out[row, :, pl.ds(far, geo.H)] = courant[row, :, pl.ds(far, geo.H)] * acc_far

    each(0, geo.B, one, 2)


def edge_rows(depth, side, geo):
    return side * (geo.B - depth)


def trig_products(angle):
    turns = jnp.floor(angle * 0.6366197723675814 + 0.5)
    rest = angle - turns * 1.5703125
    rest = rest - turns * 4.837512969970703125e-4
    rest = rest - turns * 7.549789954891882e-8
    odd = (turns - 2.0 * jnp.floor(turns * 0.5)) > 0.5
    square = rest * rest
    sine = rest + rest * square * (
        -1.6666654611e-1 + square * (8.3321608736e-3 + square * -1.9515295891e-4)
    )
    cosine = 1.0 - 0.5 * square + square * square * (
        4.166664568298827e-2 + square * (-1.388731625493765e-3 + square * 2.443315711809948e-5)
    )
    sine_square = jnp.where(odd, cosine * cosine, sine * sine)
    cosine_square = jnp.where(odd, sine * sine, cosine * cosine)
    product = sine * cosine
    return sine_square, cosine_square, jnp.where(odd, -product, product)


def half_kernel(geo, scal, *refs, other):
    *fields, out, sems = refs
    half = 1 - scal[0] if other else scal[0]
    start = pl.multiple_of(half * geo.B, TILE)
    copies = [
        pltpu.make_async_copy(field.at[pl.ds(start, geo.B)], out.at[k], sems.at[k]) for k, field in enumerate(fields)
    ]
    for copy in copies:
        copy.start()
    for copy in copies:
        copy.wait()


def join_kernel(geo, scal, *refs):
    near, far = refs[:2]
    own = refs[2:7]
    px, pc = refs[7:9]
    tiles, corners = refs[9 : 9 + geo.sides], refs[9 + geo.sides :]
    g, s = scal[0], scal[1]
    near_y = pl.multiple_of(g * geo.H, 128)
    far_y = pl.multiple_of((1 - g) * geo.H, 128)

    def one(row, carry):
        for k in range(5):
            own[k][row, :, pl.ds(near_y, geo.H)] = near[k, row]
            own[k][row, :, pl.ds(far_y, geo.H)] = far[k, row]
        return carry

    lax.fori_loop(0, geo.B, one, 0, unroll=2)
    put_rows(list(zip(own, FIRST)), px, pc, 0, g, geo)
    pack_tiles(list(zip(own, FIRST)), g, s, tiles, corners, geo)


def put_rows(items, px, pc, start, g, geo):
    for side, out in ((g, px), (1 - g, pc)):
        at = start
        for ref, depth in items:
            for k in range(depth):
                out[at] = ref[edge_rows(depth, side, geo) + k]
                at += 1


def coefficients(speed, aniso, angle):
    stretch = 2.0 * aniso
    sine_square, cosine_square, product = trig_products(angle)
    cx = speed * (1.0 + stretch * cosine_square)
    cz = speed * (1.0 + stretch * sine_square)
    cy = speed * (1.0 + stretch)
    return cx, cz, cy, (0.5 * speed) * (stretch * product), 2.0 - 2.0 * (cx + cz + cy)


def prepare_kernel(geo, scal, courant, aniso, tilt, refl, *refs):
    *coefs, out, held, sems = refs
    other = pl.multiple_of((1 - scal[0]) * geo.B, TILE)
    cuts = [0, 5, 9, 13, NOFF]
    copies = [
        pltpu.make_async_copy(refl.at[pl.ds(a, b - a), pl.ds(other, geo.B)], held.at[pl.ds(a, b - a)], sems.at[k])
        for k, (a, b) in enumerate(zip(cuts, cuts[1:]))
    ]
    for copy in copies:
        copy.start()

    def one(row):
        for ref, value in zip(coefs, coefficients(courant[row], aniso[row], tilt[row])):
            ref[row + 2, 0 : geo.Z, :] = value

    each(0, geo.B, one, 2)
    for copy, a, b in zip(copies, cuts, cuts[1:]):
        copy.wait()

        def widen(h, carry):
            for row in range(geo.B):
                out[h, row] = held[h, row].astype(F32)
            return carry

        lax.fori_loop(a, b, widen, 0)


def coef_halo(coefs, xr, cr, halo, g, s, geo):
    n, depth, depths = geo.sides, FIRST[2], FIRST
    starts, _ = tiles_of(depths, geo)
    slot = slot_of(depth)
    per = TILE // slot
    for (offset, sender), tile, xtile, ctile in zip(receivers(s, geo), halo[:n], halo[n : 2 * n], halo[2 * n :]):
        keep = tile_mask(sender, depth, 0, geo.Y)
        span = slice(offset, offset + TILE)
        for q in range(geo.B // per):
            values = coefficients(*(tile[start + q] for start in starts[2:]))
            for k in range(per):
                for ref, value in zip(coefs, values):
                    ref[q * per + k + 2, span, :] = jnp.where(keep, turned(value, TILE - k * slot), 0.0)
        for k in range(depth):
            corner = [unpack_corner(xtile, depths, i, k) for i in (2, 3, 4)]
            for ref, value in zip(coefs, coefficients(*corner)):
                ref[halo_place(g, depth, k, geo) - (geo.B - 2), span, :] = jnp.where(keep, value, 0.0)
            other = [unpack_c(ctile, depths, i, 1 - g, k, geo) for i in (2, 3, 4)]
            for ref, value in zip(coefs, coefficients(*other)):
                ref[halo_place(1 - g, depth, k, geo) - (geo.B - 2), span, :] = jnp.where(keep, value, 0.0)
    for side, line in ((g, xr), (1 - g, cr)):
        for k in range(depth):
            for ref, value in zip(coefs, coefficients(line[3 + k], line[5 + k], line[7 + k])):
                ref[halo_place(side, depth, k, geo) - (geo.B - 2), 0 : geo.Z, :] = value


def first_kernel(geo, scal, *refs):
    n = geo.sides
    now, before, xr, cr = refs[:4]
    halo = refs[4 : 4 + 3 * n]
    refl = refs[9 + 3 * n]
    out_block, prior_ext, *coefs = refs[10 + 3 * n : 17 + 3 * n]
    out_tiles, out_corners = refs[17 + 3 * n : 17 + 4 * n], refs[17 + 4 * n : 17 + 5 * n]
    near_refl, ext, old, dif, tot, sem = refs[17 + 5 * n :]
    g, s = scal[0], scal[1]
    copy = pltpu.make_async_copy(refl.at[:, pl.ds(pl.multiple_of(g * geo.B, TILE), geo.B)], near_refl, sem)
    copy.start()
    coef_halo(coefs, xr, cr, halo, g, s, geo)
    fill(old, before, lambda k: xr[2 + k], lambda k: cr[2 + k], halo, FIRST, 1, g, s, geo)
    fill(ext, now, lambda k: xr[k], lambda k: cr[k], halo, FIRST, 0, g, s, geo)

    def keep_block(row, value):
        out_block[row - geo.B] = value

    two_steps(ext, 1, lambda row: old[row], prior_ext, keep_block, coefs, dif, tot, geo)
    pack_tiles([(out_block, 2)], g, s, out_tiles, out_corners, geo)
    copy.wait()


def two_steps(ext, beyond, prior, mid, store, coefs, dif, tot, geo):
    off = geo.B - beyond

    def keep(row, value):
        mid[row - off] = value

    advance(ext, 0, off, geo.B + 2 * beyond, geo.ZE, prior, None, keep, coefs, dif, tot, geo)
    advance(mid, off, geo.B, geo.B, geo.Z, lambda row: ext[row], None, store, coefs, dif, tot, geo)


def second_kernel(geo, scal, *refs):
    n = geo.sides
    now, before, xr, cr, force, *coefs = refs[:10]
    halo = refs[10 : 10 + 3 * n]
    block, px, pc, prior_ext = refs[10 + 3 * n : 14 + 3 * n]
    out_tiles, out_corners = refs[14 + 3 * n : 14 + 4 * n], refs[14 + 4 * n : 14 + 5 * n]
    ext, dif, tot = refs[14 + 5 * n :]
    g, s = scal[0], scal[1]
    B = geo.B
    fill(ext, now, lambda k: xr[row_of(g, k, geo)], lambda k: cr[row_of(1 - g, k, geo)], halo, SECOND, 0, g, s, geo)

    def keep_block(row, value):
        block[row - B] = value

    two_steps(ext, 1, lambda row: before[row - (B - 1)], prior_ext, keep_block, coefs, dif, tot, geo)
    items = list(zip((block, force), THIRD))
    put_rows(items, px, pc, 0, g, geo)
    pack_tiles(items, g, s, out_tiles, out_corners, geo)


def row_of(side, k, geo):
    return (1 - side) * (geo.B - 2) + k


def source_only_kernel(geo, scal, offsets, now, xr, cr, courant, refl, refl_far, force, ext):
    fill_blocks(ext, xr, cr, scal[0], geo, now)
    make_source(ext, refl, refl_far, offsets, courant, force, scal[0], geo)


def third_kernel(geo, scal, *refs):
    n = geo.sides
    now, before, xr, cr, *coefs = refs[:9]
    halo = refs[9 : 9 + 3 * n]
    block, near, back = refs[9 + 3 * n : 12 + 3 * n]
    ext, dif, tot, mid = refs[12 + 3 * n :]
    g, s = scal[0], scal[1]
    B = geo.B

    fill(ext, now, lambda k: xr[k], lambda k: cr[k], halo, THIRD, 0, g, s, geo)

    def keep_block(row, value):
        block[row - B] = value
        low, high = value[:, 0 : geo.H], value[:, geo.H : geo.Y]
        near[row - B] = jnp.where(g == 0, low, high)
        back[row - B] = jnp.where(g == 0, high, low)

    two_steps(ext, 1, lambda row: before[row - (B - 1)], mid, keep_block, coefs, dif, tot, geo)


def scatter_kernel(geo, scal, offsets, *refs):
    n = geo.sides
    now, xblock, cblock, xr, cr, courant, refl, refl_far, *coefs = refs[:13]
    force = refs[13]
    halo = refs[14 : 14 + 3 * n]
    force_out, scat, scat_prior = refs[14 + 3 * n : 17 + 3 * n]
    ext, dif, tot, wave = refs[17 + 3 * n :]
    g, s = scal[0], scal[1]
    B = geo.B
    fill_blocks(ext, xblock, cblock, g, geo, now)
    make_source(ext, refl, refl_far, offsets, courant, force_out, g, geo)
    fill(wave, force, lambda k: xr[THIRD[0] + k], lambda k: cr[THIRD[0] + k], halo, THIRD, 1, g, s, geo)

    def keep_scat(row, value):
        scat[row - B] = value + force_out[row - B]

    two_steps(wave, 2, lambda row: -wave[row], scat_prior, keep_scat, coefs, dif, tot, geo)


def source_kernel(geo, scal, offsets, *refs):
    n = geo.sides
    now, xr, cr, courant, refl, refl_far, scat, force2 = refs[:8]
    force3, px, pc = refs[8:11]
    tiles, corners, ext = refs[11 : 11 + n], refs[11 + n : 11 + 2 * n], refs[11 + 2 * n]
    g, s = scal[0], scal[1]
    fill_blocks(ext, xr, cr, g, geo, now)
    make_source(ext, refl, refl_far, offsets, courant, force3, g, geo)
    items = list(zip((scat, force2, force3), LAST))
    put_rows(items, px, pc, 0, g, geo)
    pack_tiles(items, g, s, tiles, corners, geo)


def last_kernel(geo, scal, *refs):
    n = geo.sides
    scat, before, force2, force3, xr, cr, *coefs = refs[:11]
    halo = refs[11 : 11 + 3 * n]
    out_near, out_far = refs[11 + 3 * n : 13 + 3 * n]
    wave, second, third, dif, tot, mid4, mid5 = refs[13 + 3 * n :]
    g, s = scal[0], scal[1]
    B = geo.B
    fill(wave, scat, lambda k: xr[k], lambda k: cr[k], halo, LAST, 0, g, s, geo)
    fill(second, force2, lambda k: xr[3 + k], lambda k: cr[3 + k], halo, LAST, 1, g, s, geo)
    fill(third, force3, lambda k: xr[5 + k], lambda k: cr[5 + k], halo, LAST, 2, g, s, geo)

    def keep4(row, value):
        mid4[row - (B - 2)] = value

    def keep5(row, value):
        mid5[row - (B - 1)] = value

    def keep6(row, value):
        low, high = value[:, 0 : geo.H], value[:, geo.H : geo.Y]
        out_near[row - B] = jnp.where(g == 0, low, high)
        out_far[row - B] = jnp.where(g == 0, high, low)

    prior2 = lambda row: before[row - (B - 2)]
    prior4 = lambda row: mid4[row - (B - 2)]
    advance(wave, 0, B - 2, B + 4, geo.ZE, prior2, lambda row: second[row], keep4, coefs, dif, tot, geo)
    advance(mid4, B - 2, B - 1, B + 2, geo.ZE, lambda row: wave[row], lambda row: third[row], keep5, coefs, dif, tot, geo)
    advance(mid5, B - 1, B, B, geo.Z, prior4, lambda row: force3[row - B], keep6, coefs, dif, tot, geo)


def finish_kernel(geo, scal, near, far, out):
    g = scal[0]

    def one(row, carry):
        out[g * geo.B + row] = near[row]
        out[(1 - g) * geo.B + row] = far[row]
        return carry

    lax.fori_loop(0, geo.B, one, 0, unroll=4)


def shards(sections, gx, wave_now, wave_before, courant, anisotropy, tilt, reflectivity, offsets):
    rows, depth, half = wave_now.shape
    geo = Geometry(rows, depth, half, sections)
    B, Z, H, Y, ZE, n = geo.B, geo.Z, geo.H, geo.Y, geo.ZE, geo.sides
    g = lax.axis_index("gy")
    s = lax.axis_index("section")
    scal = jnp.stack([g, s]).astype(jnp.int32)
    swap = [(0, 1), (1, 0)]
    pairs_x = [p for i in range(gx - 1) for p in ((2 * i + 1, 2 * i + 2), (2 * i + 2, 2 * i + 1))]

    def z_moves():
        if geo.two:
            return [[(0, 1), (1, 0)]]
        return [[(i, i + 1) for i in range(sections - 1)], [(i + 1, i) for i in range(sections - 1)]]

    def corner_pairs(move):
        out = []
        for a, b in pairs_x:
            for i, j in move:
                out.append((((a // 2) * sections + i) * 2 + a % 2, ((b // 2) * sections + j) * 2 + b % 2))
        return out

    def chip(value):
        return lax.ppermute(value, "gy", swap)

    def exchange(px, pc, tiles, corners):
        xr = lax.ppermute(px, ("gx", "gy"), pairs_x)
        xz = [
            lax.ppermute(t, ("gx", "section", "gy"), corner_pairs(m)) for t, m in zip(corners, z_moves())
        ]
        zr = [lax.ppermute(t, "section", m) for t, m in zip(tiles, z_moves())]
        cr = chip(pc)
        cz = [chip(t) for t in zr]
        return xr, cr, [*zr, *xz, *cz]

    def shape(*dims):
        return jax.ShapeDtypeStruct(dims, F32)

    def call(kernel, inputs, outs, scratch, smem=1, specs=None, extra=(), aliases=None, out_specs=None):
        if specs is None:
            specs = [pl.BlockSpec(memory_space=pltpu.SMEM)] * (smem - 1)
            specs += [pl.BlockSpec(memory_space=pltpu.VMEM)] * (len(inputs) - smem)
        used = sum(4 * d[0] * d[1] * d[2] for d in scratch)
        return pl.pallas_call(
            functools.partial(kernel, geo),
            out_shape=outs,
            grid_spec=pltpu.PrefetchScalarGridSpec(
                num_scalar_prefetch=1,
                grid=(1,),
                in_specs=specs,
                out_specs=out_specs or [pl.BlockSpec(memory_space=pltpu.VMEM)] * len(outs),
                scratch_shapes=[*(pltpu.VMEM(d, F32) for d in scratch), *extra],
            ),
            input_output_aliases=aliases or {},
            compiler_params=pltpu.CompilerParams(vmem_limit_bytes=used + SLACK),
        )(*inputs)

    block, wide, wider, ext = (B, Z, Y), (B + 2, ZE, Y), (B + 4, ZE, Y), (3 * B, ZE, Y)

    def tile_outs(depths):
        return [shape(tiles_of(depths, geo)[1], TILE, Y)] * n + [shape(corner_tiles(depths), TILE, Y)] * n

    in_hbm = lambda value: pltpu.with_memory_space_constraint(value, pltpu.HBM)
    fields = [in_hbm(f) for f in (wave_now, wave_before, courant, anisotropy, tilt)]
    reflectivity = in_hbm(reflectivity)
    hbm = pl.BlockSpec(memory_space=pltpu.HBM)
    whole = pl.BlockSpec(memory_space=pltpu.VMEM)

    def half_of(other):
        kernel = functools.partial(half_kernel, other=other)
        copies = [pltpu.SemaphoreType.DMA((5,))]
        (out,) = call(kernel, [scal, *fields], [shape(5, B, Z, H)], [], specs=[hbm] * 5, extra=copies)
        return out

    far = chip(half_of(True))
    near = half_of(False)
    *own, px, pc, r0, r1 = _split(
        call(
            join_kernel,
            [scal, near, far],
            [shape(*block)] * 5 + [shape(sum(FIRST), Z, Y)] * 2 + tile_outs(FIRST),
            [],
        ),
        7,
        n,
    )
    xr, cr, halo = exchange(px, pc, r0, r1)
    *coefs, refl_far = call(
        prepare_kernel,
        [scal, *own[2:], reflectivity],
        [shape(*wider)] * 5 + [shape(NOFF, B, Z, H)],
        [],
        specs=[whole] * 3 + [hbm],
        extra=[pltpu.VMEM((NOFF, B, Z, H), reflectivity.dtype), pltpu.SemaphoreType.DMA((4,))],
    )
    refl_far = chip(refl_far)
    inputs = [scal, *own[:2], xr, cr, *halo, *coefs, reflectivity]
    first = len(inputs) - 6
    now, prior, *coefs, r0, r1 = _split(
        call(
            first_kernel,
            inputs,
            [shape(*block), shape(*wide)]
            + [shape(*wider)] * 5
            + tile_outs(SECOND)
            + [jax.ShapeDtypeStruct((NOFF, B, Z, H), reflectivity.dtype)],
            [ext] * 4,
            specs=[whole] * (len(inputs) - 2) + [hbm],
            extra=[pltpu.SemaphoreType.DMA],
            aliases={first + k: 2 + k for k in range(5)},
        ),
        7,
        n,
    )
    *r1, refl = r1
    courant_own = own[2]
    xr, cr, halo = exchange(now, now, r0, r1)
    (force,) = call(
        source_only_kernel,
        [scal, offsets, now, xr, cr, courant_own, refl, refl_far],
        [shape(*block)],
        [ext],
        2,
    )
    now, px, pc, prior, r0, r1 = _split(
        call(
            second_kernel,
            [scal, now, prior, xr, cr, force, *coefs, *halo],
            [shape(*block)] + [shape(sum(THIRD), Z, Y)] * 2 + [shape(*wide)] + tile_outs(THIRD),
            [ext] * 3,
        ),
        4,
        n,
    )
    xr, cr, halo = exchange(px, pc, r0, r1)
    now_x = lax.ppermute(now, ("gx", "gy"), pairs_x)
    now_c = chip(now)
    wave, near_u, back = call(
        third_kernel, [scal, now, prior, xr, cr, *coefs, *halo], [shape(*block)] + [shape(B, Z, H)] * 2, [ext] * 3 + [wide]
    )
    wave_x = lax.ppermute(wave, ("gx", "gy"), pairs_x)
    wave_c = chip(wave)
    force2, scat, scat_prior = call(
        scatter_kernel,
        [scal, offsets, now, now_x, now_c, xr, cr, courant_own, refl, refl_far, *coefs, force, *halo],
        [shape(*block)] * 2 + [shape(*wider)],
        [ext] * 4,
        2,
    )
    force3, qx, qc, r0, r1 = _split(
        call(
            source_kernel,
            [scal, offsets, wave, wave_x, wave_c, courant_own, refl, refl_far, scat, force2],
            [shape(*block)] + [shape(sum(LAST), Z, Y)] * 2 + tile_outs(LAST),
            [ext],
            2,
        ),
        3,
        n,
    )
    xr, cr, halo = exchange(qx, qc, r0, r1)

    back = chip(back)
    (background,) = call(finish_kernel, [scal, near_u, back], [shape(rows, Z, H)], [])
    near_w, far_w = call(
        last_kernel,
        [scal, scat, scat_prior, force2, force3, xr, cr, *coefs, *halo],
        [shape(B, Z, H)] * 2,
        [ext] * 5 + [wider, wide],
    )
    far_w = chip(far_w)
    low_half = jnp.where(g == 0, near_w, far_w)
    high_half = jnp.where(g == 0, far_w, near_w)
    scattered = jnp.concatenate([low_half, high_half], 0)
    return background, scattered


def _split(values, count, n):
    return [*values[:count], values[count : count + n], values[count + n :]]


def solution(mesh):
    spec = P(("shot", "gx"), "section", "gy")
    assert mesh.shape["gy"] == 2
    return jax.shard_map(
        functools.partial(shards, mesh.shape["section"], mesh.shape["gx"]),
        mesh=mesh,
        in_specs=(spec,) * 5 + (P(None, ("shot", "gx"), "section", "gy"), P()),
        out_specs=(spec, spec),
        check_vma=False,
    )
```

```python
import functools

import jax
import jax.numpy as jnp
from jax import lax
from jax.experimental import pallas as pl
from jax.experimental.pallas import tpu as pltpu
from jax.sharding import PartitionSpec as P


NOFF = 17
MARGIN = 16
TILE = 8
F32 = jnp.float32
UNROLL = 8
FIRST, SECOND, THIRD, LAST = (2, 1, 2, 2, 2), (2,), (2, 3), (3, 2, 1)
SLACK = 8 << 20


class Geometry:
    def __init__(self, rows, depth, half, sections):
        self.B, self.Z, self.H, self.Y = rows // 2, depth, half, 2 * half
        self.two = sections == 2
        self.sides = 1 if self.two else 2
        self.ZE = depth + TILE * self.sides
        assert self.B >= MARGIN and depth % TILE == 0 and half % 128 == 0


def halo_place(side, depth, k, geo):
    return (1 - side) * (geo.B - depth) + side * 2 * geo.B + k


def slot_of(depth):
    return 4 if depth > 2 else depth


def tile_mask(sender, depth, turn, width):
    place = lax.broadcasted_iota(jnp.int32, (TILE, width), 0)
    place = lax.rem(place + (TILE - turn), TILE)
    start = (1 - sender) * (TILE - depth)
    return (place >= start) & (place < start + depth)


def turned(value, turn):
    turn = turn % TILE
    return value if turn == 0 else pltpu.roll(value, turn, 0)


def senders(s, geo):
    return [s] if geo.two else [0, 1]


def receivers(s, geo):
    return [(geo.Z, 1 - s)] if geo.two else [(geo.ZE - TILE, 0), (geo.Z, 1)]


def edge_tile(ref, row, sender, geo):
    start = pl.multiple_of((1 - sender) * (geo.Z - TILE), TILE)
    return ref[row, pl.ds(start, TILE), :]


def tiles_of(depths, geo):
    starts, total = [], 0
    for depth in depths:
        starts.append(total)
        total += geo.B * slot_of(depth) // TILE
    return starts, total


def corner_slot(depths):
    return 4 if max(depths) > 2 else 2


def corner_tiles(depths):
    return -(-sum(depths) * corner_slot(depths) // TILE)


def pack_tiles(items, g, s, tiles, corners, geo):
    depths = [depth for _, depth in items]
    starts, _ = tiles_of(depths, geo)
    for sender, tile_ref, corner_ref in zip(senders(s, geo), tiles, corners):
        for (ref, depth), start in zip(items, starts):
            if ref is None:
                continue
            slot = slot_of(depth)
            per = TILE // slot
            masks = [tile_mask(sender, depth, k * slot, geo.Y) for k in range(1, per)]
            for q in range(geo.B // per):
                out = edge_tile(ref, q * per, sender, geo)
                for k in range(1, per):
                    value = turned(edge_tile(ref, q * per + k, sender, geo), k * slot)
                    out = jnp.where(masks[k - 1], value, out)
                tile_ref[start + q] = out
        slot, place = corner_slot(depths), 0
        for ref, depth in items:
            for k in range(depth):
                at, turn = divmod(place * slot, TILE)
                place += 1
                if ref is None:
                    continue
                value = turned(edge_tile(ref, g * (geo.B - depth) + k, sender, geo), turn)
                if turn:
                    value = jnp.where(tile_mask(sender, depth, turn, geo.Y), value, corner_ref[at])
                corner_ref[at] = value


def unpack_row(ref, depths, index, x, geo):
    depth = depths[index]
    per = TILE // slot_of(depth)
    return turned(ref[tiles_of(depths, geo)[0][index] + x // per], TILE - (x % per) * slot_of(depth))


def unpack_corner(ref, depths, index, k):
    at, turn = divmod((sum(depths[:index]) + k) * corner_slot(depths), TILE)
    return turned(ref[at], TILE - turn)


def unpack_c(ref, depths, index, side, k, geo):
    low = unpack_row(ref, depths, index, k, geo)
    high = unpack_row(ref, depths, index, geo.B - depths[index] + k, geo)
    return jnp.where(side == 1, low, high)


def fill(dst, own, xrow, crow, halo, depths, index, g, s, geo):
    n = geo.sides
    depth = depths[index]
    ends = list(zip(receivers(s, geo), halo[:n], halo[n : 2 * n], halo[2 * n :]))

    def one(row, carry):
        dst[geo.B + row, 0 : geo.Z, :] = own[row]
        return carry

    lax.fori_loop(0, geo.B, one, 0, unroll=4)
    for (offset, sender), tile, xtile, ctile in ends:
        keep = tile_mask(sender, depth, 0, geo.Y)
        span = slice(offset, offset + TILE)
        for row in range(geo.B):
            dst[geo.B + row, span, :] = jnp.where(keep, unpack_row(tile, depths, index, row, geo), 0.0)
        for k in range(depth):
            dst[halo_place(g, depth, k, geo), span, :] = jnp.where(keep, unpack_corner(xtile, depths, index, k), 0.0)
            value = unpack_c(ctile, depths, index, 1 - g, k, geo)
            dst[halo_place(1 - g, depth, k, geo), span, :] = jnp.where(keep, value, 0.0)
    for side, get in ((g, xrow), (1 - g, crow)):
        for k in range(depth if get is not None else 0):
            dst[halo_place(side, depth, k, geo), 0 : geo.Z, :] = get(k)


def fill_blocks(dst, xblock, cblock, g, geo, own=None):
    def one(row, carry):
        dst[g * 2 * geo.B + row, 0 : geo.Z, :] = xblock[row]
        dst[(1 - g) * 2 * geo.B + row, 0 : geo.Z, :] = cblock[row]
        if own is not None:
            dst[geo.B + row, 0 : geo.Z, :] = own[row]
        return carry

    lax.fori_loop(0, geo.B, one, 0, unroll=2)


def each(first, count, body, group):
    group = max(k for k in range(1, group + 1) if count % k == 0)

    def trip(index, carry):
        for k in range(group):
            body(first + index * group + k)
        return carry

    lax.fori_loop(0, count // group, trip, 0)


def advance(src, off, first, count, top, prior, extra, store, coefs, dif, tot, geo, group=None):
    xx, zz, yy, xz, mid = coefs
    lane = lax.broadcasted_iota(jnp.int32, (top, 128), 1)
    low_edge, high_edge = lane == 0, lane == 127
    spans = [slice(k, k + 128) for k in range(0, geo.Y, 128)]

    def slopes(row):
        value = src[row - off]
        above = pltpu.roll(value, geo.ZE - 1, 0)[0:top]
        below = pltpu.roll(value, 1, 0)[0:top]
        dif[row, 0:top] = above - below
        return value[0:top], above + below

    def local(row):
        at = jnp.minimum(row - (geo.B - 2), geo.B + 3)
        whole, total = slopes(row)
        value = [whole[:, span] for span in spans]
        zero = jnp.zeros_like(value[0])
        right = [pltpu.roll(v, 127, 1) for v in value] + [zero]
        left = [zero] + [pltpu.roll(v, 1, 1) for v in value]
        for k, span in enumerate(spans):
            side = jnp.where(high_edge, right[k + 1], right[k]) + jnp.where(low_edge, left[k], left[k + 1])
            new = mid[at, 0:top, span] * value[k] + zz[at, 0:top, span] * total[:, span]
            tot[row, 0:top, span] = new + yy[at, 0:top, span] * side

    slopes(first - 1)
    local(first)

    def one(row):
        local(row + 1)
        at = row - (geo.B - 2)
        new = tot[row, 0:top] + xx[at, 0:top] * (src[row + 1 - off, 0:top] + src[row - 1 - off, 0:top])
        new = new + xz[at, 0:top] * (dif[row + 1, 0:top] - dif[row - 1, 0:top])
        last = prior(row)
        if last is not None:
            new = new - last[0:top]
        if extra is not None:
            new = new + extra(row)[0:top]
        store(row, new)

    each(first, count, one, group or UNROLL)


def make_source(ext, refl, refl_far, offsets, courant, out, g, geo):
    near = pl.multiple_of(g * geo.H, 128)
    far = pl.multiple_of((1 - g) * geo.H, 128)

    def one(row):
        acc = jnp.zeros((geo.Z, geo.H), F32)
        acc_far = jnp.zeros((geo.Z, geo.H), F32)
        for h in range(NOFF):
            place = geo.B + row + offsets[h]
            acc = acc + refl[h, row].astype(F32) * ext[place, 0 : geo.Z, pl.ds(near, geo.H)]
            acc_far = acc_far + refl_far[h, row] * ext[place, 0 : geo.Z, pl.ds(far, geo.H)]
        out[row, :, pl.ds(near, geo.H)] = courant[row, :, pl.ds(near, geo.H)] * acc
        out[row, :, pl.ds(far, geo.H)] = courant[row, :, pl.ds(far, geo.H)] * acc_far

    each(0, geo.B, one, 2)


def edge_rows(depth, side, geo):
    return side * (geo.B - depth)


def trig_products(angle):
    turns = jnp.floor(angle * 0.6366197723675814 + 0.5)
    rest = angle - turns * 1.5703125
    rest = rest - turns * 4.837512969970703125e-4
    rest = rest - turns * 7.549789954891882e-8
    odd = (turns - 2.0 * jnp.floor(turns * 0.5)) > 0.5
    square = rest * rest
    sine = rest + rest * square * (
        -1.6666654611e-1 + square * (8.3321608736e-3 + square * -1.9515295891e-4)
    )
    cosine = 1.0 - 0.5 * square + square * square * (
        4.166664568298827e-2 + square * (-1.388731625493765e-3 + square * 2.443315711809948e-5)
    )
    sine_square = jnp.where(odd, cosine * cosine, sine * sine)
    cosine_square = jnp.where(odd, sine * sine, cosine * cosine)
    product = sine * cosine
    return sine_square, cosine_square, jnp.where(odd, -product, product)


def half_kernel(geo, scal, *refs, other):
    *fields, out, sems = refs
    half = 1 - scal[0] if other else scal[0]
    start = pl.multiple_of(half * geo.B, TILE)
    copies = [
        pltpu.make_async_copy(field.at[pl.ds(start, geo.B)], out.at[k], sems.at[k]) for k, field in enumerate(fields)
    ]
    for copy in copies:
        copy.start()
    for copy in copies:
        copy.wait()


def join_kernel(geo, scal, *refs):
    near, far = refs[:2]
    own = refs[2:7]
    px, pc = refs[7:9]
    tiles, corners = refs[9 : 9 + geo.sides], refs[9 + geo.sides :]
    g, s = scal[0], scal[1]
    near_y = pl.multiple_of(g * geo.H, 128)
    far_y = pl.multiple_of((1 - g) * geo.H, 128)

    def one(row, carry):
        for k in range(5):
            own[k][row, :, pl.ds(near_y, geo.H)] = near[k, row]
            own[k][row, :, pl.ds(far_y, geo.H)] = far[k, row]
        return carry

    lax.fori_loop(0, geo.B, one, 0, unroll=2)
    put_rows(list(zip(own, FIRST)), px, pc, 0, g, geo)
    pack_tiles(list(zip(own, FIRST)), g, s, tiles, corners, geo)


def put_rows(items, px, pc, start, g, geo):
    for side, out in ((g, px), (1 - g, pc)):
        at = start
        for ref, depth in items:
            for k in range(depth):
                out[at] = ref[edge_rows(depth, side, geo) + k]
                at += 1


def coefficients(speed, aniso, angle):
    stretch = 2.0 * aniso
    sine_square, cosine_square, product = trig_products(angle)
    cx = speed * (1.0 + stretch * cosine_square)
    cz = speed * (1.0 + stretch * sine_square)
    cy = speed * (1.0 + stretch)
    return cx, cz, cy, (0.5 * speed) * (stretch * product), 2.0 - 2.0 * (cx + cz + cy)


def prepare_kernel(geo, scal, courant, aniso, tilt, refl, *refs):
    *coefs, out, held, sems = refs
    other = pl.multiple_of((1 - scal[0]) * geo.B, TILE)
    cuts = [0, 5, 9, 13, NOFF]
    copies = [
        pltpu.make_async_copy(refl.at[pl.ds(a, b - a), pl.ds(other, geo.B)], held.at[pl.ds(a, b - a)], sems.at[k])
        for k, (a, b) in enumerate(zip(cuts, cuts[1:]))
    ]
    for copy in copies:
        copy.start()

    def one(row):
        for ref, value in zip(coefs, coefficients(courant[row], aniso[row], tilt[row])):
            ref[row + 2, 0 : geo.Z, :] = value

    each(0, geo.B, one, 2)
    for copy, a, b in zip(copies, cuts, cuts[1:]):
        copy.wait()

        def widen(h, carry):
            for row in range(geo.B):
                out[h, row] = held[h, row].astype(F32)
            return carry

        lax.fori_loop(a, b, widen, 0)


def coef_halo(coefs, xr, cr, halo, g, s, geo):
    n, depth, depths = geo.sides, FIRST[2], FIRST
    starts, _ = tiles_of(depths, geo)
    slot = slot_of(depth)
    per = TILE // slot
    for (offset, sender), tile, xtile, ctile in zip(receivers(s, geo), halo[:n], halo[n : 2 * n], halo[2 * n :]):
        keep = tile_mask(sender, depth, 0, geo.Y)
        span = slice(offset, offset + TILE)
        for q in range(geo.B // per):
            values = coefficients(*(tile[start + q] for start in starts[2:]))
            for k in range(per):
                for ref, value in zip(coefs, values):
                    ref[q * per + k + 2, span, :] = jnp.where(keep, turned(value, TILE - k * slot), 0.0)
        for k in range(depth):
            corner = [unpack_corner(xtile, depths, i, k) for i in (2, 3, 4)]
            for ref, value in zip(coefs, coefficients(*corner)):
                ref[halo_place(g, depth, k, geo) - (geo.B - 2), span, :] = jnp.where(keep, value, 0.0)
            other = [unpack_c(ctile, depths, i, 1 - g, k, geo) for i in (2, 3, 4)]
            for ref, value in zip(coefs, coefficients(*other)):
                ref[halo_place(1 - g, depth, k, geo) - (geo.B - 2), span, :] = jnp.where(keep, value, 0.0)
    for side, line in ((g, xr), (1 - g, cr)):
        for k in range(depth):
            for ref, value in zip(coefs, coefficients(line[3 + k], line[5 + k], line[7 + k])):
                ref[halo_place(side, depth, k, geo) - (geo.B - 2), 0 : geo.Z, :] = value


def first_kernel(geo, scal, *refs):
    n = geo.sides
    now, before, xr, cr = refs[:4]
    halo = refs[4 : 4 + 3 * n]
    refl = refs[9 + 3 * n]
    out_block, prior_ext, *coefs = refs[10 + 3 * n : 17 + 3 * n]
    out_tiles, out_corners = refs[17 + 3 * n : 17 + 4 * n], refs[17 + 4 * n : 17 + 5 * n]
    near_refl, ext, old, dif, tot, sem = refs[17 + 5 * n :]
    g, s = scal[0], scal[1]
    copy = pltpu.make_async_copy(refl.at[:, pl.ds(pl.multiple_of(g * geo.B, TILE), geo.B)], near_refl, sem)
    copy.start()
    coef_halo(coefs, xr, cr, halo, g, s, geo)
    fill(old, before, lambda k: xr[2 + k], lambda k: cr[2 + k], halo, FIRST, 1, g, s, geo)
    fill(ext, now, lambda k: xr[k], lambda k: cr[k], halo, FIRST, 0, g, s, geo)

    def keep_block(row, value):
        out_block[row - geo.B] = value

    two_steps(ext, 1, lambda row: old[row], prior_ext, keep_block, coefs, dif, tot, geo)
    pack_tiles([(out_block, 2)], g, s, out_tiles, out_corners, geo)
    copy.wait()


def two_steps(ext, beyond, prior, mid, store, coefs, dif, tot, geo):
    off = geo.B - beyond

    def keep(row, value):
        mid[row - off] = value

    advance(ext, 0, off, geo.B + 2 * beyond, geo.ZE, prior, None, keep, coefs, dif, tot, geo)
    advance(mid, off, geo.B, geo.B, geo.Z, lambda row: ext[row], None, store, coefs, dif, tot, geo)


def second_kernel(geo, scal, *refs):
    n = geo.sides
    now, before, xr, cr, force, *coefs = refs[:10]
    halo = refs[10 : 10 + 3 * n]
    block, px, pc, prior_ext = refs[10 + 3 * n : 14 + 3 * n]
    out_tiles, out_corners = refs[14 + 3 * n : 14 + 4 * n], refs[14 + 4 * n : 14 + 5 * n]
    ext, dif, tot = refs[14 + 5 * n :]
    g, s = scal[0], scal[1]
    B = geo.B
    fill(ext, now, lambda k: xr[row_of(g, k, geo)], lambda k: cr[row_of(1 - g, k, geo)], halo, SECOND, 0, g, s, geo)

    def keep_block(row, value):
        block[row - B] = value

    two_steps(ext, 1, lambda row: before[row - (B - 1)], prior_ext, keep_block, coefs, dif, tot, geo)
    items = list(zip((block, force), THIRD))
    put_rows(items, px, pc, 0, g, geo)
    pack_tiles(items, g, s, out_tiles, out_corners, geo)


def row_of(side, k, geo):
    return (1 - side) * (geo.B - 2) + k


def source_only_kernel(geo, scal, offsets, now, xr, cr, courant, refl, refl_far, force, ext):
    fill_blocks(ext, xr, cr, scal[0], geo, now)
    make_source(ext, refl, refl_far, offsets, courant, force, scal[0], geo)


def third_kernel(geo, scal, *refs):
    n = geo.sides
    now, before, xr, cr, *coefs = refs[:9]
    halo = refs[9 : 9 + 3 * n]
    block, near, back = refs[9 + 3 * n : 12 + 3 * n]
    ext, dif, tot, mid = refs[12 + 3 * n :]
    g, s = scal[0], scal[1]
    B = geo.B

    fill(ext, now, lambda k: xr[k], lambda k: cr[k], halo, THIRD, 0, g, s, geo)

    def keep_block(row, value):
        block[row - B] = value
        low, high = value[:, 0 : geo.H], value[:, geo.H : geo.Y]
        near[row - B] = jnp.where(g == 0, low, high)
        back[row - B] = jnp.where(g == 0, high, low)

    two_steps(ext, 1, lambda row: before[row - (B - 1)], mid, keep_block, coefs, dif, tot, geo)


def scatter_kernel(geo, scal, offsets, *refs):
    n = geo.sides
    now, xblock, cblock, xr, cr, courant, refl, refl_far, *coefs = refs[:13]
    force = refs[13]
    halo = refs[14 : 14 + 3 * n]
    force_out, scat, scat_prior, px, pc = refs[14 + 3 * n : 19 + 3 * n]
    out_tiles, out_corners = refs[19 + 3 * n : 19 + 4 * n], refs[19 + 4 * n : 19 + 5 * n]
    ext, dif, tot, wave = refs[19 + 5 * n :]
    g, s = scal[0], scal[1]
    B = geo.B
    fill_blocks(ext, xblock, cblock, g, geo, now)
    make_source(ext, refl, refl_far, offsets, courant, force_out, g, geo)
    fill(wave, force, lambda k: xr[THIRD[0] + k], lambda k: cr[THIRD[0] + k], halo, THIRD, 1, g, s, geo)

    def keep_scat(row, value):
        scat[row - B] = value + force_out[row - B]

    two_steps(wave, 2, lambda row: -wave[row], scat_prior, keep_scat, coefs, dif, tot, geo)
    put_rows([(scat, LAST[0]), (force_out, LAST[1])], px, pc, 0, g, geo)
    pack_tiles(list(zip((scat, force_out, None), LAST)), g, s, out_tiles, out_corners, geo)


def source_kernel(geo, scal, offsets, *refs):
    n = geo.sides
    now, xr, cr, courant, refl, refl_far = refs[:6]
    force3, px, pc = refs[8 + 2 * n : 11 + 2 * n]
    tiles, corners, ext = refs[11 + 2 * n : 11 + 3 * n], refs[11 + 3 * n : 11 + 4 * n], refs[11 + 4 * n]
    g, s = scal[0], scal[1]
    fill_blocks(ext, xr, cr, g, geo, now)
    make_source(ext, refl, refl_far, offsets, courant, force3, g, geo)
    put_rows([(force3, LAST[2])], px, pc, LAST[0] + LAST[1], g, geo)
    pack_tiles(list(zip((None, None, force3), LAST)), g, s, tiles, corners, geo)


def last_kernel(geo, scal, *refs):
    n = geo.sides
    scat, before, force2, force3, xr, cr, *coefs = refs[:11]
    halo = refs[11 : 11 + 3 * n]
    out_near, out_far = refs[11 + 3 * n : 13 + 3 * n]
    wave, second, third, dif, tot, mid4, mid5 = refs[13 + 3 * n :]
    g, s = scal[0], scal[1]
    B = geo.B
    fill(wave, scat, lambda k: xr[k], lambda k: cr[k], halo, LAST, 0, g, s, geo)
    fill(second, force2, lambda k: xr[3 + k], lambda k: cr[3 + k], halo, LAST, 1, g, s, geo)
    fill(third, force3, lambda k: xr[5 + k], lambda k: cr[5 + k], halo, LAST, 2, g, s, geo)

    def keep4(row, value):
        mid4[row - (B - 2)] = value

    def keep5(row, value):
        mid5[row - (B - 1)] = value

    def keep6(row, value):
        low, high = value[:, 0 : geo.H], value[:, geo.H : geo.Y]
        out_near[row - B] = jnp.where(g == 0, low, high)
        out_far[row - B] = jnp.where(g == 0, high, low)

    prior2 = lambda row: before[row - (B - 2)]
    prior4 = lambda row: mid4[row - (B - 2)]
    advance(wave, 0, B - 2, B + 4, geo.ZE, prior2, lambda row: second[row], keep4, coefs, dif, tot, geo)
    advance(mid4, B - 2, B - 1, B + 2, geo.ZE, lambda row: wave[row], lambda row: third[row], keep5, coefs, dif, tot, geo)
    advance(mid5, B - 1, B, B, geo.Z, prior4, lambda row: force3[row - B], keep6, coefs, dif, tot, geo)


def finish_kernel(geo, scal, near, far, out):
    g = scal[0]

    def one(row, carry):
        out[g * geo.B + row] = near[row]
        out[(1 - g) * geo.B + row] = far[row]
        return carry

    lax.fori_loop(0, geo.B, one, 0, unroll=4)


def shards(sections, gx, wave_now, wave_before, courant, anisotropy, tilt, reflectivity, offsets):
    rows, depth, half = wave_now.shape
    geo = Geometry(rows, depth, half, sections)
    B, Z, H, Y, ZE, n = geo.B, geo.Z, geo.H, geo.Y, geo.ZE, geo.sides
    g = lax.axis_index("gy")
    scal = None
    swap = [(0, 1), (1, 0)]
    pairs_x = [p for i in range(gx - 1) for p in ((2 * i + 1, 2 * i + 2), (2 * i + 2, 2 * i + 1))]

    def z_moves():
        if geo.two:
            return [[(0, 1), (1, 0)]]
        return [[(i, i + 1) for i in range(sections - 1)], [(i + 1, i) for i in range(sections - 1)]]

    def corner_pairs(move):
        out = []
        for a, b in pairs_x:
            for i, j in move:
                out.append((((a // 2) * sections + i) * 2 + a % 2, ((b // 2) * sections + j) * 2 + b % 2))
        return out

    def chip(value):
        return lax.ppermute(value, "gy", swap)

    def exchange(px, pc, tiles, corners):
        xr = lax.ppermute(px, ("gx", "gy"), pairs_x)
        xz = [
            lax.ppermute(t, ("gx", "section", "gy"), corner_pairs(m)) for t, m in zip(corners, z_moves())
        ]
        zr = [lax.ppermute(t, "section", m) for t, m in zip(tiles, z_moves())]
        cr = chip(pc)
        cz = [chip(t) for t in zr]
        return xr, cr, [*zr, *xz, *cz]

    def shape(*dims):
        return jax.ShapeDtypeStruct(dims, F32)

    def call(kernel, inputs, outs, scratch, smem=1, specs=None, extra=(), aliases=None, out_specs=None):
        if specs is None:
            specs = [pl.BlockSpec(memory_space=pltpu.SMEM)] * (smem - 1)
            specs += [pl.BlockSpec(memory_space=pltpu.VMEM)] * (len(inputs) - smem)
        used = sum(4 * d[0] * d[1] * d[2] for d in scratch)

        def body(*refs):
            kernel(geo, (lax.axis_index("gy"), lax.axis_index("section")), *refs)

        return pl.pallas_call(
            body,
            out_shape=outs,
            grid_spec=pltpu.PrefetchScalarGridSpec(
                num_scalar_prefetch=0,
                grid=(1,),
                in_specs=specs,
                out_specs=out_specs or [pl.BlockSpec(memory_space=pltpu.VMEM)] * len(outs),
                scratch_shapes=[*(pltpu.VMEM(d, F32) for d in scratch), *extra],
            ),
            input_output_aliases={k - 1: v for k, v in (aliases or {}).items()},
            compiler_params=pltpu.CompilerParams(vmem_limit_bytes=used + SLACK),
        )(*inputs[1:])

    block, wide, wider, ext = (B, Z, Y), (B + 2, ZE, Y), (B + 4, ZE, Y), (3 * B, ZE, Y)

    def tile_outs(depths):
        return [shape(tiles_of(depths, geo)[1], TILE, Y)] * n + [shape(corner_tiles(depths), TILE, Y)] * n

    in_hbm = lambda value: pltpu.with_memory_space_constraint(value, pltpu.HBM)
    fields = [in_hbm(f) for f in (wave_now, wave_before, courant, anisotropy, tilt)]
    reflectivity = in_hbm(reflectivity)
    hbm = pl.BlockSpec(memory_space=pltpu.HBM)
    whole = pl.BlockSpec(memory_space=pltpu.VMEM)

    def half_of(other):
        kernel = functools.partial(half_kernel, other=other)
        copies = [pltpu.SemaphoreType.DMA((5,))]
        (out,) = call(kernel, [scal, *fields], [shape(5, B, Z, H)], [], specs=[hbm] * 5, extra=copies)
        return out

    far = chip(half_of(True))
    near = half_of(False)
    *own, px, pc, r0, r1 = _split(
        call(
            join_kernel,
            [scal, near, far],
            [shape(*block)] * 5 + [shape(sum(FIRST), Z, Y)] * 2 + tile_outs(FIRST),
            [],
        ),
        7,
        n,
    )
    xr, cr, halo = exchange(px, pc, r0, r1)
    *coefs, refl_far = call(
        prepare_kernel,
        [scal, *own[2:], reflectivity],
        [shape(*wider)] * 5 + [shape(NOFF, B, Z, H)],
        [],
        specs=[whole] * 3 + [hbm],
        extra=[pltpu.VMEM((NOFF, B, Z, H), reflectivity.dtype), pltpu.SemaphoreType.DMA((4,))],
    )
    refl_far = chip(refl_far)
    inputs = [scal, *own[:2], xr, cr, *halo, *coefs, reflectivity]
    first = len(inputs) - 6
    now, prior, *coefs, r0, r1 = _split(
        call(
            first_kernel,
            inputs,
            [shape(*block), shape(*wide)]
            + [shape(*wider)] * 5
            + tile_outs(SECOND)
            + [jax.ShapeDtypeStruct((NOFF, B, Z, H), reflectivity.dtype)],
            [ext] * 4,
            specs=[whole] * (len(inputs) - 2) + [hbm],
            extra=[pltpu.SemaphoreType.DMA],
            aliases={first + k: 2 + k for k in range(5)},
        ),
        7,
        n,
    )
    *r1, refl = r1
    courant_own = own[2]
    xr, cr, halo = exchange(now, now, r0, r1)
    (force,) = call(
        source_only_kernel,
        [scal, offsets, now, xr, cr, courant_own, refl, refl_far],
        [shape(*block)],
        [ext],
        2,
    )
    now, px, pc, prior, r0, r1 = _split(
        call(
            second_kernel,
            [scal, now, prior, xr, cr, force, *coefs, *halo],
            [shape(*block)] + [shape(sum(THIRD), Z, Y)] * 2 + [shape(*wide)] + tile_outs(THIRD),
            [ext] * 3,
        ),
        4,
        n,
    )
    xr, cr, halo = exchange(px, pc, r0, r1)
    now_x = lax.ppermute(now, ("gx", "gy"), pairs_x)
    now_c = chip(now)
    wave, near_u, back = call(
        third_kernel, [scal, now, prior, xr, cr, *coefs, *halo], [shape(*block)] + [shape(B, Z, H)] * 2, [ext] * 3 + [wide]
    )
    wave_x = lax.ppermute(wave, ("gx", "gy"), pairs_x)
    wave_c = chip(wave)
    force2, scat, scat_prior, *payload = call(
        scatter_kernel,
        [scal, offsets, now, now_x, now_c, xr, cr, courant_own, refl, refl_far, *coefs, force, *halo],
        [shape(*block)] * 2 + [shape(*wider)] + [shape(sum(LAST), Z, Y)] * 2 + tile_outs(LAST),
        [ext] * 4,
        2,
    )
    force3, qx, qc, r0, r1 = _split(
        call(
            source_kernel,
            [scal, offsets, wave, wave_x, wave_c, courant_own, refl, refl_far, *payload],
            [shape(*block)] + [shape(sum(LAST), Z, Y)] * 2 + tile_outs(LAST),
            [ext],
            2,
            aliases={8 + k: 1 + k for k in range(len(payload))},
        ),
        3,
        n,
    )
    xr, cr, halo = exchange(qx, qc, r0, r1)
    back = chip(back)
    (background,) = call(finish_kernel, [scal, near_u, back], [shape(rows, Z, H)], [])
    near_w, far_w = call(
        last_kernel,
        [scal, scat, scat_prior, force2, force3, xr, cr, *coefs, *halo],
        [shape(B, Z, H)] * 2,
        [ext] * 5 + [wider, wide],
    )
    far_w = chip(far_w)
    low_half = jnp.where(g == 0, near_w, far_w)
    high_half = jnp.where(g == 0, far_w, near_w)
    scattered = jnp.concatenate([low_half, high_half], 0)
    return background, scattered


def _split(values, count, n):
    return [*values[:count], values[count : count + n], values[count + n :]]


def solution(mesh):
    spec = P(("shot", "gx"), "section", "gy")
    assert mesh.shape["gy"] == 2
    return jax.shard_map(
        functools.partial(shards, mesh.shape["section"], mesh.shape["gx"]),
        mesh=mesh,
        in_specs=(spec,) * 5 + (P(None, ("shot", "gx"), "section", "gy"), P()),
        out_specs=(spec, spec),
        check_vma=False,
    )
```

```python
import functools

import jax
import jax.numpy as jnp
from jax import lax
from jax.experimental import pallas as pl
from jax.experimental.pallas import tpu as pltpu
from jax.sharding import PartitionSpec as P


NOFF = 17
MARGIN = 16
TILE = 8
F32 = jnp.float32
UNROLL = 8
FIRST, SECOND, THIRD, LAST = (2, 1, 2, 2, 2), (2,), (2, 3), (3, 2, 1)
SLACK = 8 << 20


class Geometry:
    def __init__(self, rows, depth, half, sections):
        self.B, self.Z, self.H, self.Y = rows // 2, depth, half, 2 * half
        self.two = sections == 2
        self.sides = 1 if self.two else 2
        self.ZE = depth + TILE * self.sides
        assert self.B >= MARGIN and depth % TILE == 0 and half % 128 == 0


def halo_place(side, depth, k, geo):
    return (1 - side) * (geo.B - depth) + side * 2 * geo.B + k


def slot_of(depth):
    return 4 if depth > 2 else depth


def tile_mask(sender, depth, turn, width):
    place = lax.broadcasted_iota(jnp.int32, (TILE, width), 0)
    place = lax.rem(place + (TILE - turn), TILE)
    start = (1 - sender) * (TILE - depth)
    return (place >= start) & (place < start + depth)


def turned(value, turn):
    turn = turn % TILE
    return value if turn == 0 else pltpu.roll(value, turn, 0)


def senders(s, geo):
    return [s] if geo.two else [0, 1]


def receivers(s, geo):
    return [(geo.Z, 1 - s)] if geo.two else [(geo.ZE - TILE, 0), (geo.Z, 1)]


def edge_tile(ref, row, sender, geo):
    start = pl.multiple_of((1 - sender) * (geo.Z - TILE), TILE)
    return ref[row, pl.ds(start, TILE), :]


def tiles_of(depths, geo):
    starts, total = [], 0
    for depth in depths:
        starts.append(total)
        total += geo.B * slot_of(depth) // TILE
    return starts, total


def corner_slot(depths):
    return 4 if max(depths) > 2 else 2


def corner_tiles(depths):
    return -(-sum(depths) * corner_slot(depths) // TILE)


def pack_tiles(items, g, s, tiles, corners, geo):
    depths = [depth for _, depth in items]
    starts, _ = tiles_of(depths, geo)
    for sender, tile_ref, corner_ref in zip(senders(s, geo), tiles, corners):
        for (ref, depth), start in zip(items, starts):
            if ref is None:
                continue
            slot = slot_of(depth)
            per = TILE // slot
            masks = [tile_mask(sender, depth, k * slot, geo.Y) for k in range(1, per)]
            for q in range(geo.B // per):
                out = edge_tile(ref, q * per, sender, geo)
                for k in range(1, per):
                    value = turned(edge_tile(ref, q * per + k, sender, geo), k * slot)
                    out = jnp.where(masks[k - 1], value, out)
                tile_ref[start + q] = out
        slot, place = corner_slot(depths), 0
        for ref, depth in items:
            for k in range(depth):
                at, turn = divmod(place * slot, TILE)
                place += 1
                if ref is None:
                    continue
                value = turned(edge_tile(ref, g * (geo.B - depth) + k, sender, geo), turn)
                if turn:
                    value = jnp.where(tile_mask(sender, depth, turn, geo.Y), value, corner_ref[at])
                corner_ref[at] = value


def unpack_row(ref, depths, index, x, geo):
    depth = depths[index]
    per = TILE // slot_of(depth)
    return turned(ref[tiles_of(depths, geo)[0][index] + x // per], TILE - (x % per) * slot_of(depth))


def unpack_corner(ref, depths, index, k):
    at, turn = divmod((sum(depths[:index]) + k) * corner_slot(depths), TILE)
    return turned(ref[at], TILE - turn)


def unpack_c(ref, depths, index, side, k, geo):
    low = unpack_row(ref, depths, index, k, geo)
    high = unpack_row(ref, depths, index, geo.B - depths[index] + k, geo)
    return jnp.where(side == 1, low, high)


def fill(dst, own, xrow, crow, halo, depths, index, g, s, geo):
    n = geo.sides
    depth = depths[index]
    ends = list(zip(receivers(s, geo), halo[:n], halo[n : 2 * n], halo[2 * n :]))

    def one(row, carry):
        dst[geo.B + row, 0 : geo.Z, :] = own[row]
        return carry

    lax.fori_loop(0, geo.B, one, 0, unroll=4)
    for (offset, sender), tile, xtile, ctile in ends:
        keep = tile_mask(sender, depth, 0, geo.Y)
        span = slice(offset, offset + TILE)
        for row in range(geo.B):
            dst[geo.B + row, span, :] = jnp.where(keep, unpack_row(tile, depths, index, row, geo), 0.0)
        for k in range(depth):
            dst[halo_place(g, depth, k, geo), span, :] = jnp.where(keep, unpack_corner(xtile, depths, index, k), 0.0)
            value = unpack_c(ctile, depths, index, 1 - g, k, geo)
            dst[halo_place(1 - g, depth, k, geo), span, :] = jnp.where(keep, value, 0.0)
    for side, get in ((g, xrow), (1 - g, crow)):
        for k in range(depth if get is not None else 0):
            dst[halo_place(side, depth, k, geo), 0 : geo.Z, :] = get(k)


def fill_blocks(dst, xblock, cblock, g, geo, own=None):
    def one(row, carry):
        dst[g * 2 * geo.B + row, 0 : geo.Z, :] = xblock[row]
        dst[(1 - g) * 2 * geo.B + row, 0 : geo.Z, :] = cblock[row]
        if own is not None:
            dst[geo.B + row, 0 : geo.Z, :] = own[row]
        return carry

    lax.fori_loop(0, geo.B, one, 0, unroll=2)


def each(first, count, body, group):
    group = max(k for k in range(1, group + 1) if count % k == 0)

    def trip(index, carry):
        for k in range(group):
            body(first + index * group + k)
        return carry

    lax.fori_loop(0, count // group, trip, 0)


def advance(src, off, first, count, top, prior, extra, store, coefs, dif, tot, geo, group=None):
    xx, zz, yy, xz, mid = coefs
    lane = lax.broadcasted_iota(jnp.int32, (top, 128), 1)
    low_edge, high_edge = lane == 0, lane == 127
    spans = [slice(k, k + 128) for k in range(0, geo.Y, 128)]

    def slopes(row):
        value = src[row - off]
        above = pltpu.roll(value, geo.ZE - 1, 0)[0:top]
        below = pltpu.roll(value, 1, 0)[0:top]
        dif[row, 0:top] = above - below
        return value[0:top], above + below

    def local(row):
        at = jnp.minimum(row - (geo.B - 2), geo.B + 3)
        whole, total = slopes(row)
        value = [whole[:, span] for span in spans]
        zero = jnp.zeros_like(value[0])
        right = [pltpu.roll(v, 127, 1) for v in value] + [zero]
        left = [zero] + [pltpu.roll(v, 1, 1) for v in value]
        for k, span in enumerate(spans):
            side = jnp.where(high_edge, right[k + 1], right[k]) + jnp.where(low_edge, left[k], left[k + 1])
            new = mid[at, 0:top, span] * value[k] + zz[at, 0:top, span] * total[:, span]
            tot[row, 0:top, span] = new + yy[at, 0:top, span] * side

    slopes(first - 1)
    local(first)

    def one(row):
        local(row + 1)
        at = row - (geo.B - 2)
        new = tot[row, 0:top] + xx[at, 0:top] * (src[row + 1 - off, 0:top] + src[row - 1 - off, 0:top])
        new = new + xz[at, 0:top] * (dif[row + 1, 0:top] - dif[row - 1, 0:top])
        last = prior(row)
        if last is not None:
            new = new - last[0:top]
        if extra is not None:
            new = new + extra(row)[0:top]
        store(row, new)

    each(first, count, one, group or UNROLL)


def make_source(ext, refl, refl_far, offsets, courant, out, g, geo):
    copy, offsets = offsets
    copy.wait()
    near = pl.multiple_of(g * geo.H, 128)
    far = pl.multiple_of((1 - g) * geo.H, 128)

    def one(row):
        acc = jnp.zeros((geo.Z, geo.H), F32)
        acc_far = jnp.zeros((geo.Z, geo.H), F32)
        for h in range(NOFF):
            place = geo.B + row + offsets[h]
            acc = acc + refl[h, row].astype(F32) * ext[place, 0 : geo.Z, pl.ds(near, geo.H)]
            acc_far = acc_far + refl_far[h, row] * ext[place, 0 : geo.Z, pl.ds(far, geo.H)]
        out[row, :, pl.ds(near, geo.H)] = courant[row, :, pl.ds(near, geo.H)] * acc
        out[row, :, pl.ds(far, geo.H)] = courant[row, :, pl.ds(far, geo.H)] * acc_far

    each(0, geo.B, one, 2)


def edge_rows(depth, side, geo):
    return side * (geo.B - depth)


def trig_products(angle):
    turns = jnp.floor(angle * 0.6366197723675814 + 0.5)
    rest = angle - turns * 1.5703125
    rest = rest - turns * 4.837512969970703125e-4
    rest = rest - turns * 7.549789954891882e-8
    odd = (turns - 2.0 * jnp.floor(turns * 0.5)) > 0.5
    square = rest * rest
    sine = rest + rest * square * (
        -1.6666654611e-1 + square * (8.3321608736e-3 + square * -1.9515295891e-4)
    )
    cosine = 1.0 - 0.5 * square + square * square * (
        4.166664568298827e-2 + square * (-1.388731625493765e-3 + square * 2.443315711809948e-5)
    )
    sine_square = jnp.where(odd, cosine * cosine, sine * sine)
    cosine_square = jnp.where(odd, sine * sine, cosine * cosine)
    product = sine * cosine
    return sine_square, cosine_square, jnp.where(odd, -product, product)


def half_kernel(geo, scal, *refs, other):
    *fields, out, sems = refs
    half = 1 - scal[0] if other else scal[0]
    start = pl.multiple_of(half * geo.B, TILE)
    copies = [
        pltpu.make_async_copy(field.at[pl.ds(start, geo.B)], out.at[k], sems.at[k]) for k, field in enumerate(fields)
    ]
    for copy in copies:
        copy.start()
    for copy in copies:
        copy.wait()


def join_kernel(geo, scal, *refs):
    near, far = refs[:2]
    own = refs[2:7]
    px, pc = refs[7:9]
    tiles, corners = refs[9 : 9 + geo.sides], refs[9 + geo.sides :]
    g, s = scal[0], scal[1]
    near_y = pl.multiple_of(g * geo.H, 128)
    far_y = pl.multiple_of((1 - g) * geo.H, 128)

    def one(row, carry):
        for k in range(5):
            own[k][row, :, pl.ds(near_y, geo.H)] = near[k, row]
            own[k][row, :, pl.ds(far_y, geo.H)] = far[k, row]
        return carry

    lax.fori_loop(0, geo.B, one, 0, unroll=2)
    put_rows(list(zip(own, FIRST)), px, pc, 0, g, geo)
    pack_tiles(list(zip(own, FIRST)), g, s, tiles, corners, geo)


def put_rows(items, px, pc, start, g, geo):
    for side, out in ((g, px), (1 - g, pc)):
        at = start
        for ref, depth in items:
            for k in range(depth):
                out[at] = ref[edge_rows(depth, side, geo) + k]
                at += 1


def coefficients(speed, aniso, angle):
    stretch = 2.0 * aniso
    sine_square, cosine_square, product = trig_products(angle)
    cx = speed * (1.0 + stretch * cosine_square)
    cz = speed * (1.0 + stretch * sine_square)
    cy = speed * (1.0 + stretch)
    return cx, cz, cy, (0.5 * speed) * (stretch * product), 2.0 - 2.0 * (cx + cz + cy)


def prepare_kernel(geo, scal, courant, aniso, tilt, refl, *refs):
    *coefs, out, held, sems = refs
    other = pl.multiple_of((1 - scal[0]) * geo.B, TILE)
    cuts = [0, 5, 9, 13, NOFF]
    copies = [
        pltpu.make_async_copy(refl.at[pl.ds(a, b - a), pl.ds(other, geo.B)], held.at[pl.ds(a, b - a)], sems.at[k])
        for k, (a, b) in enumerate(zip(cuts, cuts[1:]))
    ]
    for copy in copies:
        copy.start()

    def one(row):
        for ref, value in zip(coefs, coefficients(courant[row], aniso[row], tilt[row])):
            ref[row + 2, 0 : geo.Z, :] = value

    each(0, geo.B, one, 2)
    for copy, a, b in zip(copies, cuts, cuts[1:]):
        copy.wait()

        def widen(h, carry):
            for row in range(geo.B):
                out[h, row] = held[h, row].astype(F32)
            return carry

        lax.fori_loop(a, b, widen, 0)


def coef_halo(coefs, xr, cr, halo, g, s, geo):
    n, depth, depths = geo.sides, FIRST[2], FIRST
    starts, _ = tiles_of(depths, geo)
    slot = slot_of(depth)
    per = TILE // slot
    for (offset, sender), tile, xtile, ctile in zip(receivers(s, geo), halo[:n], halo[n : 2 * n], halo[2 * n :]):
        keep = tile_mask(sender, depth, 0, geo.Y)
        span = slice(offset, offset + TILE)
        for q in range(geo.B // per):
            values = coefficients(*(tile[start + q] for start in starts[2:]))
            for k in range(per):
                for ref, value in zip(coefs, values):
                    ref[q * per + k + 2, span, :] = jnp.where(keep, turned(value, TILE - k * slot), 0.0)
        for k in range(depth):
            corner = [unpack_corner(xtile, depths, i, k) for i in (2, 3, 4)]
            for ref, value in zip(coefs, coefficients(*corner)):
                ref[halo_place(g, depth, k, geo) - (geo.B - 2), span, :] = jnp.where(keep, value, 0.0)
            other = [unpack_c(ctile, depths, i, 1 - g, k, geo) for i in (2, 3, 4)]
            for ref, value in zip(coefs, coefficients(*other)):
                ref[halo_place(1 - g, depth, k, geo) - (geo.B - 2), span, :] = jnp.where(keep, value, 0.0)
    for side, line in ((g, xr), (1 - g, cr)):
        for k in range(depth):
            for ref, value in zip(coefs, coefficients(line[3 + k], line[5 + k], line[7 + k])):
                ref[halo_place(side, depth, k, geo) - (geo.B - 2), 0 : geo.Z, :] = value


def first_kernel(geo, scal, *refs):
    n = geo.sides
    now, before, xr, cr = refs[:4]
    halo = refs[4 : 4 + 3 * n]
    refl = refs[9 + 3 * n]
    out_block, prior_ext, *coefs = refs[10 + 3 * n : 17 + 3 * n]
    out_tiles, out_corners = refs[17 + 3 * n : 17 + 4 * n], refs[17 + 4 * n : 17 + 5 * n]
    near_refl, ext, old, dif, tot, sem = refs[17 + 5 * n :]
    g, s = scal[0], scal[1]
    copy = pltpu.make_async_copy(refl.at[:, pl.ds(pl.multiple_of(g * geo.B, TILE), geo.B)], near_refl, sem)
    copy.start()
    coef_halo(coefs, xr, cr, halo, g, s, geo)
    fill(old, before, lambda k: xr[2 + k], lambda k: cr[2 + k], halo, FIRST, 1, g, s, geo)
    fill(ext, now, lambda k: xr[k], lambda k: cr[k], halo, FIRST, 0, g, s, geo)

    def keep_block(row, value):
        out_block[row - geo.B] = value

    two_steps(ext, 1, lambda row: old[row], prior_ext, keep_block, coefs, dif, tot, geo)
    pack_tiles([(out_block, 2)], g, s, out_tiles, out_corners, geo)
    copy.wait()


def two_steps(ext, beyond, prior, mid, store, coefs, dif, tot, geo):
    off = geo.B - beyond

    def keep(row, value):
        mid[row - off] = value

    advance(ext, 0, off, geo.B + 2 * beyond, geo.ZE, prior, None, keep, coefs, dif, tot, geo)
    advance(mid, off, geo.B, geo.B, geo.Z, lambda row: ext[row], None, store, coefs, dif, tot, geo)


def second_kernel(geo, scal, *refs):
    n = geo.sides
    now, before, xr, cr, force, *coefs = refs[:10]
    halo = refs[10 : 10 + 3 * n]
    block, px, pc, prior_ext = refs[10 + 3 * n : 14 + 3 * n]
    out_tiles, out_corners = refs[14 + 3 * n : 14 + 4 * n], refs[14 + 4 * n : 14 + 5 * n]
    ext, dif, tot = refs[14 + 5 * n :]
    g, s = scal[0], scal[1]
    B = geo.B
    fill(ext, now, lambda k: xr[row_of(g, k, geo)], lambda k: cr[row_of(1 - g, k, geo)], halo, SECOND, 0, g, s, geo)

    def keep_block(row, value):
        block[row - B] = value

    two_steps(ext, 1, lambda row: before[row - (B - 1)], prior_ext, keep_block, coefs, dif, tot, geo)
    items = list(zip((block, force), THIRD))
    put_rows(items, px, pc, 0, g, geo)
    pack_tiles(items, g, s, out_tiles, out_corners, geo)


def row_of(side, k, geo):
    return (1 - side) * (geo.B - 2) + k


def source_only_kernel(geo, scal, offsets, now, xr, cr, courant, refl, refl_far, force, ext):
    fill_blocks(ext, xr, cr, scal[0], geo, now)
    make_source(ext, refl, refl_far, offsets, courant, force, scal[0], geo)


def third_kernel(geo, scal, *refs):
    n = geo.sides
    now, before, xr, cr, *coefs = refs[:9]
    halo = refs[9 : 9 + 3 * n]
    block, near, back = refs[9 + 3 * n : 12 + 3 * n]
    ext, dif, tot, mid = refs[12 + 3 * n :]
    g, s = scal[0], scal[1]
    B = geo.B

    fill(ext, now, lambda k: xr[k], lambda k: cr[k], halo, THIRD, 0, g, s, geo)

    def keep_block(row, value):
        block[row - B] = value
        low, high = value[:, 0 : geo.H], value[:, geo.H : geo.Y]
        near[row - B] = jnp.where(g == 0, low, high)
        back[row - B] = jnp.where(g == 0, high, low)

    two_steps(ext, 1, lambda row: before[row - (B - 1)], mid, keep_block, coefs, dif, tot, geo)


def scatter_kernel(geo, scal, offsets, *refs):
    n = geo.sides
    now, xblock, cblock, xr, cr, courant, refl, refl_far, *coefs = refs[:13]
    force = refs[13]
    halo = refs[14 : 14 + 3 * n]
    force_out, scat, scat_prior, px, pc = refs[14 + 3 * n : 19 + 3 * n]
    out_tiles, out_corners = refs[19 + 3 * n : 19 + 4 * n], refs[19 + 4 * n : 19 + 5 * n]
    ext, dif, tot, wave = refs[19 + 5 * n :]
    g, s = scal[0], scal[1]
    B = geo.B
    fill_blocks(ext, xblock, cblock, g, geo, now)
    make_source(ext, refl, refl_far, offsets, courant, force_out, g, geo)
    fill(wave, force, lambda k: xr[THIRD[0] + k], lambda k: cr[THIRD[0] + k], halo, THIRD, 1, g, s, geo)

    def keep_scat(row, value):
        scat[row - B] = value + force_out[row - B]

    two_steps(wave, 2, lambda row: -wave[row], scat_prior, keep_scat, coefs, dif, tot, geo)
    put_rows([(scat, LAST[0]), (force_out, LAST[1])], px, pc, 0, g, geo)
    pack_tiles(list(zip((scat, force_out, None), LAST)), g, s, out_tiles, out_corners, geo)


def source_kernel(geo, scal, offsets, *refs):
    n = geo.sides
    now, xr, cr, courant, refl, refl_far = refs[:6]
    force3, px, pc = refs[8 + 2 * n : 11 + 2 * n]
    tiles, corners, ext = refs[11 + 2 * n : 11 + 3 * n], refs[11 + 3 * n : 11 + 4 * n], refs[11 + 4 * n]
    g, s = scal[0], scal[1]
    fill_blocks(ext, xr, cr, g, geo, now)
    make_source(ext, refl, refl_far, offsets, courant, force3, g, geo)
    put_rows([(force3, LAST[2])], px, pc, LAST[0] + LAST[1], g, geo)
    pack_tiles(list(zip((None, None, force3), LAST)), g, s, tiles, corners, geo)


def last_kernel(geo, scal, *refs):
    n = geo.sides
    scat, before, force2, force3, xr, cr, *coefs = refs[:11]
    halo = refs[11 : 11 + 3 * n]
    out_near, out_far = refs[11 + 3 * n : 13 + 3 * n]
    wave, second, third, dif, tot, mid4, mid5 = refs[13 + 3 * n :]
    g, s = scal[0], scal[1]
    B = geo.B
    fill(wave, scat, lambda k: xr[k], lambda k: cr[k], halo, LAST, 0, g, s, geo)
    fill(second, force2, lambda k: xr[3 + k], lambda k: cr[3 + k], halo, LAST, 1, g, s, geo)
    fill(third, force3, lambda k: xr[5 + k], lambda k: cr[5 + k], halo, LAST, 2, g, s, geo)

    def keep4(row, value):
        mid4[row - (B - 2)] = value

    def keep5(row, value):
        mid5[row - (B - 1)] = value

    def keep6(row, value):
        low, high = value[:, 0 : geo.H], value[:, geo.H : geo.Y]
        out_near[row - B] = jnp.where(g == 0, low, high)
        out_far[row - B] = jnp.where(g == 0, high, low)

    prior2 = lambda row: before[row - (B - 2)]
    prior4 = lambda row: mid4[row - (B - 2)]
    advance(wave, 0, B - 2, B + 4, geo.ZE, prior2, lambda row: second[row], keep4, coefs, dif, tot, geo)
    advance(mid4, B - 2, B - 1, B + 2, geo.ZE, lambda row: wave[row], lambda row: third[row], keep5, coefs, dif, tot, geo)
    advance(mid5, B - 1, B, B, geo.Z, prior4, lambda row: force3[row - B], keep6, coefs, dif, tot, geo)


def finish_kernel(geo, scal, near, far, out):
    g = scal[0]

    def one(row, carry):
        out[g * geo.B + row] = near[row]
        out[(1 - g) * geo.B + row] = far[row]
        return carry

    lax.fori_loop(0, geo.B, one, 0, unroll=4)


def shards(sections, gx, wave_now, wave_before, courant, anisotropy, tilt, reflectivity, offsets):
    rows, depth, half = wave_now.shape
    geo = Geometry(rows, depth, half, sections)
    B, Z, H, Y, ZE, n = geo.B, geo.Z, geo.H, geo.Y, geo.ZE, geo.sides
    g = lax.axis_index("gy")
    scal = None
    swap = [(0, 1), (1, 0)]
    pairs_x = [p for i in range(gx - 1) for p in ((2 * i + 1, 2 * i + 2), (2 * i + 2, 2 * i + 1))]

    def z_moves():
        if geo.two:
            return [[(0, 1), (1, 0)]]
        return [[(i, i + 1) for i in range(sections - 1)], [(i + 1, i) for i in range(sections - 1)]]

    def corner_pairs(move):
        out = []
        for a, b in pairs_x:
            for i, j in move:
                out.append((((a // 2) * sections + i) * 2 + a % 2, ((b // 2) * sections + j) * 2 + b % 2))
        return out

    def chip(value):
        return lax.ppermute(value, "gy", swap)

    def exchange(px, pc, tiles, corners):
        xr = lax.ppermute(px, ("gx", "gy"), pairs_x)
        xz = [
            lax.ppermute(t, ("gx", "section", "gy"), corner_pairs(m)) for t, m in zip(corners, z_moves())
        ]
        zr = [lax.ppermute(t, "section", m) for t, m in zip(tiles, z_moves())]
        cr = chip(pc)
        cz = [chip(t) for t in zr]
        return xr, cr, [*zr, *xz, *cz]

    def shape(*dims):
        return jax.ShapeDtypeStruct(dims, F32)

    def call(kernel, inputs, outs, scratch, smem=1, specs=None, extra=(), aliases=None, out_specs=None):
        if specs is None:
            specs = [pl.BlockSpec(memory_space=pltpu.HBM)] * (smem - 1)
            specs += [pl.BlockSpec(memory_space=pltpu.VMEM)] * (len(inputs) - smem)
        if smem == 2:
            extra = (*extra, pltpu.SMEM((NOFF,), jnp.int32), pltpu.SemaphoreType.DMA)
        used = sum(4 * d[0] * d[1] * d[2] for d in scratch)

        def body(*refs):
            place = (lax.axis_index("gy"), lax.axis_index("section"))
            if smem == 1:
                return kernel(geo, place, *refs)
            *refs, held, sem = refs
            copy = pltpu.make_async_copy(refs[0], held, sem)
            copy.start()
            kernel(geo, place, (copy, held), *refs[1:])

        return pl.pallas_call(
            body,
            out_shape=outs,
            grid_spec=pltpu.PrefetchScalarGridSpec(
                num_scalar_prefetch=0,
                grid=(1,),
                in_specs=specs,
                out_specs=out_specs or [pl.BlockSpec(memory_space=pltpu.VMEM)] * len(outs),
                scratch_shapes=[*(pltpu.VMEM(d, F32) for d in scratch), *extra],
            ),
            input_output_aliases={k - 1: v for k, v in (aliases or {}).items()},
            compiler_params=pltpu.CompilerParams(vmem_limit_bytes=used + SLACK),
        )(*inputs[1:])

    block, wide, wider, ext = (B, Z, Y), (B + 2, ZE, Y), (B + 4, ZE, Y), (3 * B, ZE, Y)

    def tile_outs(depths):
        return [shape(tiles_of(depths, geo)[1], TILE, Y)] * n + [shape(corner_tiles(depths), TILE, Y)] * n

    in_hbm = lambda value: pltpu.with_memory_space_constraint(value, pltpu.HBM)
    fields = [in_hbm(f) for f in (wave_now, wave_before, courant, anisotropy, tilt)]
    reflectivity = in_hbm(reflectivity)
    offsets = in_hbm(offsets)
    hbm = pl.BlockSpec(memory_space=pltpu.HBM)
    whole = pl.BlockSpec(memory_space=pltpu.VMEM)

    def half_of(other):
        kernel = functools.partial(half_kernel, other=other)
        copies = [pltpu.SemaphoreType.DMA((5,))]
        (out,) = call(kernel, [scal, *fields], [shape(5, B, Z, H)], [], specs=[hbm] * 5, extra=copies)
        return out

    far = chip(half_of(True))
    near = half_of(False)
    *own, px, pc, r0, r1 = _split(
        call(
            join_kernel,
            [scal, near, far],
            [shape(*block)] * 5 + [shape(sum(FIRST), Z, Y)] * 2 + tile_outs(FIRST),
            [],
        ),
        7,
        n,
    )
    xr, cr, halo = exchange(px, pc, r0, r1)
    *coefs, refl_far = call(
        prepare_kernel,
        [scal, *own[2:], reflectivity],
        [shape(*wider)] * 5 + [shape(NOFF, B, Z, H)],
        [],
        specs=[whole] * 3 + [hbm],
        extra=[pltpu.VMEM((NOFF, B, Z, H), reflectivity.dtype), pltpu.SemaphoreType.DMA((4,))],
    )
    refl_far = chip(refl_far)
    inputs = [scal, *own[:2], xr, cr, *halo, *coefs, reflectivity]
    first = len(inputs) - 6
    now, prior, *coefs, r0, r1 = _split(
        call(
            first_kernel,
            inputs,
            [shape(*block), shape(*wide)]
            + [shape(*wider)] * 5
            + tile_outs(SECOND)
            + [jax.ShapeDtypeStruct((NOFF, B, Z, H), reflectivity.dtype)],
            [ext] * 4,
            specs=[whole] * (len(inputs) - 2) + [hbm],
            extra=[pltpu.SemaphoreType.DMA],
            aliases={first + k: 2 + k for k in range(5)},
        ),
        7,
        n,
    )
    *r1, refl = r1
    courant_own = own[2]
    xr, cr, halo = exchange(now, now, r0, r1)
    (force,) = call(
        source_only_kernel,
        [scal, offsets, now, xr, cr, courant_own, refl, refl_far],
        [shape(*block)],
        [ext],
        2,
    )
    now, px, pc, prior, r0, r1 = _split(
        call(
            second_kernel,
            [scal, now, prior, xr, cr, force, *coefs, *halo],
            [shape(*block)] + [shape(sum(THIRD), Z, Y)] * 2 + [shape(*wide)] + tile_outs(THIRD),
            [ext] * 3,
        ),
        4,
        n,
    )
    xr, cr, halo = exchange(px, pc, r0, r1)
    now_x = lax.ppermute(now, ("gx", "gy"), pairs_x)
    now_c = chip(now)
    wave, near_u, back = call(
        third_kernel, [scal, now, prior, xr, cr, *coefs, *halo], [shape(*block)] + [shape(B, Z, H)] * 2, [ext] * 3 + [wide]
    )
    wave_x = lax.ppermute(wave, ("gx", "gy"), pairs_x)
    wave_c = chip(wave)
    force2, scat, scat_prior, *payload = call(
        scatter_kernel,
        [scal, offsets, now, now_x, now_c, xr, cr, courant_own, refl, refl_far, *coefs, force, *halo],
        [shape(*block)] * 2 + [shape(*wider)] + [shape(sum(LAST), Z, Y)] * 2 + tile_outs(LAST),
        [ext] * 4,
        2,
    )
    force3, qx, qc, r0, r1 = _split(
        call(
            source_kernel,
            [scal, offsets, wave, wave_x, wave_c, courant_own, refl, refl_far, *payload],
            [shape(*block)] + [shape(sum(LAST), Z, Y)] * 2 + tile_outs(LAST),
            [ext],
            2,
            aliases={8 + k: 1 + k for k in range(len(payload))},
        ),
        3,
        n,
    )
    xr, cr, halo = exchange(qx, qc, r0, r1)
    back = chip(back)
    (background,) = call(finish_kernel, [scal, near_u, back], [shape(rows, Z, H)], [])
    near_w, far_w = call(
        last_kernel,
        [scal, scat, scat_prior, force2, force3, xr, cr, *coefs, *halo],
        [shape(B, Z, H)] * 2,
        [ext] * 5 + [wider, wide],
    )
    far_w = chip(far_w)
    low_half = jnp.where(g == 0, near_w, far_w)
    high_half = jnp.where(g == 0, far_w, near_w)
    scattered = jnp.concatenate([low_half, high_half], 0)
    return background, scattered


def _split(values, count, n):
    return [*values[:count], values[count : count + n], values[count + n :]]


def solution(mesh):
    spec = P(("shot", "gx"), "section", "gy")
    assert mesh.shape["gy"] == 2
    return jax.shard_map(
        functools.partial(shards, mesh.shape["section"], mesh.shape["gx"]),
        mesh=mesh,
        in_specs=(spec,) * 5 + (P(None, ("shot", "gx"), "section", "gy"), P()),
        out_specs=(spec, spec),
        check_vma=False,
    )
```
